32 devices in a mesh: grp: 2 (over x), beam: 16 (over z, y, core).
Axes of the slice: x: 2, y: 2, z: 4, core: 2. Of those that a mesh axis runs over, the one named last changes fastest.
Arguments:
- hidden: bfloat16 [3, 64, 8192], P(None, ('grp', 'beam')), parts along dimension 1, may hold values from -6 to 6
- norm_gain: float32 [8192], replicated, may hold values from 0.5 to 1.5
- q_weight: bfloat16 [8192, 8192], P(None, 'beam'), may hold values from -0.0625 to 0.0625
- q_bias: float32 [8192], P('beam'), may hold values from -3 to 3
- kv_weight: bfloat16 [8192, 2, 1024], P(None, None, 'beam'), may hold values from -0.0625 to 0.0625
- kv_bias: float32 [2, 1024], P(None, 'beam'), may hold values from -5 to 5
- o_weight: bfloat16 [8192, 8192], P(None, 'beam'), may hold values from -0.0625 to 0.0625
- prefix_key_cache: bfloat16 [8, 2048, 1024], P('grp', 'beam'), parts along dimension 0, may hold values from -100 to 100
- prefix_value_cache: bfloat16 [8, 2048, 1024], P('grp', 'beam'), parts along dimension 0, may hold values from -12 to 12
- prefix_index: int32 [4], P('grp'), parts along dimension 0, may hold values from 0 to 3
- prefix_lens: int32 [4], P('grp'), parts along dimension 0, may hold values from 8 to 2048, as said below
- tail_key_cache: bfloat16 [64, 256, 1024], P(('grp', 'beam')), parts along dimension 0, may hold values from -12 to 12
- tail_value_cache: bfloat16 [64, 256, 1024], P(('grp', 'beam')), parts along dimension 0, may hold values from -12 to 12
- tail_lens: int32 [64], P('grp'), parts along dimension 0, may hold values from 1 to 256, as said below
- parents: int32 [3, 64], P(None, 'grp'), parts along dimension 1, may hold values from 0 to 31, as said below
Outputs:
- out: bfloat16 [3, 64, 8192], P(None, 'grp', 'beam'), parts along dimension 1
The draws below stay inside these ranges and needn't reach their ends.
There are 2 independent parts, one for each index of `grp`. The reference program is written for one: setup_inputs(seed, part) draws one part's arguments, and reference() takes and returns one part's arrays. A program takes and returns all parts, laid end to end along the dimension named above; an argument that names none is the same for every part. Nothing has to cross between parts.
Inputs may be any that keep to these rules, and one draw needn't show every extreme that they name: `prefix_lens`: the shared prefix lengths; some prompt uses all 2048 positions. `tail_lens`: the tail lengths; some row fills all 256 positions. parents[t, r] is one of the 16 rows of r's prompt: from r - r % 16 to r - r % 16 + 15.
All inputs are finite; a program needn't handle non-finite values.
Results may differ from the reference program's by a relative error of at most 0.012.
The reference program's roundings to bfloat16 on the way count: a program that leaves them out, or rounds other values in their place, can miss the bound.
Values may be sent and summed in bfloat16 or wider, within the bound.
A program may use at most 192 MiB of HBM per device.

```python
import math
import jax
import jax.numpy as jnp
import numpy as np
from jax import lax

D = 8192
QUERY_HEADS = 64
KEY_HEADS = 8
HEAD_DIM = 128
BEAM_COUNT = 16
STEPS = 3
NPREF = 4
ROW_DEV = 2
PREFIX_PER_CHIP = 128
TAIL_LENGTH = 256
QW = 8192
KVW = 1024
GROUP_SIZE = 8
BEAM_ROWS = 32
PROMPTS = 2
PREFIX_LENGTH = 2048


def draw_prefix_key_cache(key, part):
    first_key = jax.random.fold_in(key, 0)
    base = jnp.clip(2.0 * jax.random.normal(first_key, (NPREF, PREFIX_LENGTH, KVW), jnp.float32), -12.0, 12.0)
    return base.astype(jnp.bfloat16)


def draw_prefix_index(key, part):
    order = jax.random.permutation(jax.random.fold_in(key, 17), NPREF).astype(jnp.int32)
    return order[jnp.arange(PROMPTS, dtype=jnp.int32) % NPREF].astype(jnp.int32)


def draw_prefix_lens(key, part):
    base_key = jax.random.fold_in(jax.random.fold_in(key, 4211), part)
    long_key = jax.random.fold_in(base_key, 1)
    short_key = jax.random.fold_in(base_key, 2)
    pick_key = jax.random.fold_in(base_key, 3)
    full_key = jax.random.fold_in(base_key, 4)
    short_top = min(17, PREFIX_LENGTH + 1)
    long_lens = jax.random.randint(long_key, (PROMPTS,), 8, PREFIX_LENGTH + 1).astype(jnp.int32)
    short_lens = jax.random.randint(short_key, (PROMPTS,), 8, short_top).astype(jnp.int32)
    pick = jax.random.randint(pick_key, (PROMPTS,), 0, 2).astype(jnp.int32)
    full = jax.random.randint(full_key, (), 0, PROMPTS).astype(jnp.int32)
    prompt_ids = jnp.arange(PROMPTS, dtype=jnp.int32)
    forced_short = prompt_ids == (full + 1) % PROMPTS
    lengths = jnp.where((pick == 1) | forced_short, short_lens, long_lens)
    return jnp.where(prompt_ids == full, PREFIX_LENGTH, lengths).astype(jnp.int32)


def draw_tail_lens(key, part):
    length_key = jax.random.fold_in(key, 31)
    short_key = jax.random.fold_in(key, 32)
    pick_key = jax.random.fold_in(key, 33)
    full_key = jax.random.fold_in(key, 34)
    long_lens = jax.random.randint(length_key, (BEAM_ROWS,), 1, TAIL_LENGTH + 1).astype(jnp.int32)
    short_lens = jax.random.randint(short_key, (BEAM_ROWS,), 1, min(5, TAIL_LENGTH + 1)).astype(jnp.int32)
    pick = jax.random.randint(pick_key, (BEAM_ROWS,), 0, 2).astype(jnp.int32)
    lengths = jnp.where(pick == 1, short_lens, long_lens)
    full = jax.random.randint(full_key, (), 0, BEAM_ROWS).astype(jnp.int32)
    return jnp.where(jnp.arange(BEAM_ROWS, dtype=jnp.int32) == full, TAIL_LENGTH, lengths).astype(jnp.int32)


def draw_parents(key, part):
    starts = jnp.arange(BEAM_ROWS, dtype=jnp.int32) // BEAM_COUNT * BEAM_COUNT
    offsets = jax.random.randint(key, (STEPS, BEAM_ROWS), 0, BEAM_COUNT)
    return (starts[None, :] + offsets).astype(jnp.int32)


def block_levels(key, extent, shards, least, high):
    def one(axis_at, parts):
        draws = jax.random.uniform(jax.random.fold_in(jax.random.fold_in(key, 6), axis_at), (parts,), jnp.float32, least / len(shards), high / len(shards))
        return jnp.repeat(jnp.exp(draws), extent[axis_at] // parts).reshape((-1,) + (1,) * (len(extent) - axis_at - 1))

    loudness = one(*shards[0])
    for cut in shards[1:]:
        loudness = loudness * one(*cut)
    return loudness


def bell_draw(key, dims, deviation, bound, cuts=(), held_as=jnp.bfloat16):
    entries = deviation * jax.random.normal(key, dims, jnp.float32)
    if cuts:
        entries = entries * block_levels(key, dims, cuts, -0.22, 0.18)
    return jnp.clip(entries, -bound, bound).astype(held_as)


def setup_inputs(seed: int = 0, part: int = 0) -> dict:
    splits = jax.random.split(jax.random.key(seed), 16)
    part_keys = jax.random.split(jax.random.fold_in(splits[15], part), 16)
    hidden = bell_draw(part_keys[0], (STEPS, BEAM_ROWS, D), 1.0, 6.0, ((1, 16),))
    norm_gain = jnp.clip(1.0 + 0.1 * jax.random.normal(splits[1], (D,), jnp.float32), 0.5, 1.5)
    q_weight = bell_draw(splits[2], (D, QW), D ** -0.5, 0.0625, ((1, 16),))
    q_bias = bell_draw(splits[3], (QW,), 0.5, 3.0, ((0, 16),), jnp.float32)
    kv_weight = bell_draw(splits[4], (D, 2, KVW), D ** -0.5, 0.0625, ((2, 16),))
    kv_bias = bell_draw(splits[5], (2, KVW), 1.0, 5.0, ((1, 16),), jnp.float32)
    o_weight = bell_draw(splits[6], (QW, D), QW ** -0.5, 0.0625, ((1, 16),))
    prefix_key_cache = draw_prefix_key_cache(jax.random.fold_in(jax.random.fold_in(splits[15], part), 71), part)
    prefix_value_cache = bell_draw(part_keys[8], (NPREF, PREFIX_LENGTH, KVW), 2.0, 12.0, ((1, 16),))
    prefix_index = draw_prefix_index(jax.random.fold_in(jax.random.fold_in(splits[15], part), 71), part)
    prefix_lens = draw_prefix_lens(jax.random.fold_in(jax.random.fold_in(splits[15], part), 71), part)
    tail_key_cache = bell_draw(part_keys[11], (BEAM_ROWS, TAIL_LENGTH, KVW), 2.0, 12.0, ((0, 16),))
    tail_value_cache = bell_draw(part_keys[12], (BEAM_ROWS, TAIL_LENGTH, KVW), 2.0, 12.0, ((0, 16),))
    tail_lens = draw_tail_lens(jax.random.fold_in(jax.random.fold_in(splits[15], part), 71), part)
    parents = draw_parents(jax.random.fold_in(jax.random.fold_in(splits[15], part), 71), part)
    return dict(hidden=hidden, norm_gain=norm_gain, q_weight=q_weight, q_bias=q_bias, kv_weight=kv_weight, kv_bias=kv_bias, o_weight=o_weight, prefix_key_cache=prefix_key_cache, prefix_value_cache=prefix_value_cache, prefix_index=prefix_index, prefix_lens=prefix_lens, tail_key_cache=tail_key_cache, tail_value_cache=tail_value_cache, tail_lens=tail_lens, parents=parents)


EPS = 1e-06
NEG = -1e+30
ROPE_BASE = 1000000.0

def rope_parts(positions, head_size):
    half = head_size // 2
    freqs = np.power(ROPE_BASE, -np.arange(half) * 2.0 / head_size)
    angle = positions.astype(jnp.float32)[:, None] * jnp.asarray(freqs, jnp.float32)[None, :]
    return (jnp.cos(angle), jnp.sin(angle))

def apply_rotation(value_rows, cosine_table, sine_table):
    half = value_rows.shape[-1] // 2
    first = value_rows[..., :half]
    second = value_rows[..., half:]
    cosine_table = cosine_table[:, None, :]
    sine_table = sine_table[:, None, :]
    return jnp.concatenate([first * cosine_table - second * sine_table, second * cosine_table + first * sine_table], axis=-1)

def reference(hidden, norm_gain, q_weight, q_bias, kv_weight, kv_bias, o_weight, prefix_key_cache, prefix_value_cache, prefix_index, prefix_lens, tail_key_cache, tail_value_cache, tail_lens, parents):
    head_groups = PREFIX_LENGTH // PREFIX_PER_CHIP
    score_scale = 1.0 / math.sqrt(HEAD_DIM)
    row_ids = jnp.arange(BEAM_ROWS, dtype=jnp.int32)
    prompt_of = row_ids // BEAM_COUNT
    ancestors = row_ids
    makers = []
    fresh_keys = []
    current_values = []
    results = []
    kv_matrix = kv_weight.reshape(D, 2 * KVW)
    kv_shift = kv_bias.reshape(2 * KVW)
    group_ids = jnp.arange(head_groups, dtype=jnp.int32)
    for step in range(STEPS):
        chosen = parents[step]
        ancestors = ancestors[chosen]
        makers = [item[chosen] for item in makers] + [row_ids]
        inputs = hidden[step].astype(jnp.float32)
        normed = (inputs * lax.rsqrt(lax.optimization_barrier(jnp.mean(inputs * inputs, axis=-1, keepdims=True)) + EPS) * norm_gain).astype(jnp.bfloat16)
        queries = (jnp.dot(normed, q_weight, preferred_element_type=jnp.float32) + q_bias).astype(jnp.bfloat16)
        current_key_value = (jnp.dot(normed, kv_matrix, preferred_element_type=jnp.float32) + kv_shift).astype(jnp.bfloat16).reshape(BEAM_ROWS, 2, KVW)
        positions = prefix_lens[prompt_of] + tail_lens[ancestors] + step
        cosine_table, sine_table = rope_parts(positions, HEAD_DIM)
        rotated_rows = apply_rotation(queries.astype(jnp.float32).reshape(BEAM_ROWS, QUERY_HEADS, HEAD_DIM), cosine_table, sine_table).astype(jnp.bfloat16)
        current_keys = apply_rotation(current_key_value[:, 0].astype(jnp.float32).reshape(BEAM_ROWS, KEY_HEADS, HEAD_DIM), cosine_table, sine_table).astype(jnp.bfloat16)
        fresh_keys.append(current_keys)
        current_values.append(current_key_value[:, 1].reshape(BEAM_ROWS, KEY_HEADS, HEAD_DIM))
        key_stack = jnp.stack(fresh_keys, 0)
        value_stack = jnp.stack(current_values, 0)
        lineage = jnp.stack(makers, 1)
        decode_depth = step + 1

        def attend(prompt):
            start_offset = prompt * BEAM_COUNT
            query_rows = lax.dynamic_slice_in_dim(rotated_rows, start_offset, BEAM_COUNT, 0).astype(jnp.float32).reshape(BEAM_COUNT, KEY_HEADS, GROUP_SIZE, HEAD_DIM)
            entry_point = prefix_index[prompt]
            length = prefix_lens[prompt]
            key_rows = lax.dynamic_index_in_dim(prefix_key_cache, entry_point, 0, keepdims=False).astype(jnp.float32).reshape(PREFIX_LENGTH, KEY_HEADS, HEAD_DIM)
            value_rows = lax.dynamic_index_in_dim(prefix_value_cache, entry_point, 0, keepdims=False).astype(jnp.float32).reshape(head_groups, PREFIX_PER_CHIP, KEY_HEADS, HEAD_DIM)
            valid = (jnp.arange(PREFIX_LENGTH, dtype=jnp.int32) < length).reshape(head_groups, PREFIX_PER_CHIP)
            score_matrix = jnp.einsum('cixw,eiw->cixe', query_rows, key_rows).reshape(BEAM_COUNT, KEY_HEADS, GROUP_SIZE, head_groups, PREFIX_PER_CHIP) * score_scale
            score_matrix = jnp.where(valid, score_matrix, NEG)
            owner_rows = lax.dynamic_slice_in_dim(ancestors, start_offset, BEAM_COUNT, 0)
            tail_key_rows = tail_key_cache[owner_rows].astype(jnp.float32).reshape(BEAM_COUNT, TAIL_LENGTH, KEY_HEADS, HEAD_DIM)
            tail_value_rows = tail_value_cache[owner_rows].astype(jnp.float32).reshape(BEAM_COUNT, TAIL_LENGTH, KEY_HEADS, HEAD_DIM)
            tail_ok = jnp.arange(TAIL_LENGTH, dtype=jnp.int32)[None, :] < tail_lens[owner_rows][:, None]
            tail_scores = jnp.einsum('bkgd,btkd->bkgt', query_rows, tail_key_rows) * score_scale
            tail_scores = jnp.where(tail_ok[:, None, None, :], tail_scores, NEG)
            tail_head_group = owner_rows // ROW_DEV
            tail_hot = tail_head_group[:, None] == group_ids[None, :]
            made = lax.dynamic_slice_in_dim(lineage, start_offset, BEAM_COUNT, 0)
            made_k = key_stack[jnp.arange(decode_depth, dtype=jnp.int32)[None, :], made].astype(jnp.float32)
            made_v = value_stack[jnp.arange(decode_depth, dtype=jnp.int32)[None, :], made].astype(jnp.float32)
            made_scores = jnp.einsum('bkgd,bjkd->bkgj', query_rows, made_k) * score_scale
            produced_group = made // ROW_DEV
            made_hot = produced_group[:, :, None] == group_ids[None, None, :]
            group_maximum = jnp.maximum(score_matrix.max(-1), jnp.where(tail_hot[:, None, None, :], tail_scores.max(-1)[..., None], NEG))
            group_maximum = jnp.maximum(group_maximum, jnp.where(made_hot[:, None, None, :, :], made_scores[..., None], NEG).max(3))
            weights = jnp.where(valid, jnp.exp(score_matrix - group_maximum[..., None]), 0.0)
            total = weights.sum(-1)
            numer = jnp.einsum('bkgns,nskd->bkgnd', weights.astype(jnp.bfloat16).astype(jnp.float32), value_rows)
            tail_maximum = jnp.take_along_axis(group_maximum, jnp.broadcast_to(tail_head_group[:, None, None, None], (BEAM_COUNT, KEY_HEADS, GROUP_SIZE, 1)), axis=3)
            tail_w = jnp.where(tail_ok[:, None, None, :], jnp.exp(tail_scores - tail_maximum), 0.0)
            tail_hot_f = tail_hot.astype(jnp.float32)
            total = total + tail_hot_f[:, None, None, :] * tail_w.sum(-1)[..., None]
            tail_num = jnp.einsum('bkgt,btkd->bkgd', tail_w.astype(jnp.bfloat16).astype(jnp.float32), tail_value_rows)
            numer = numer + tail_hot_f[:, None, None, :, None] * tail_num[:, :, :, None, :]
            produced_top = jnp.take_along_axis(group_maximum, jnp.broadcast_to(produced_group[:, None, None, :], (BEAM_COUNT, KEY_HEADS, GROUP_SIZE, decode_depth)), axis=3)
            made_w = jnp.exp(made_scores - produced_top)
            made_hot_f = made_hot.astype(jnp.float32)
            total = total + jnp.einsum('bkgj,bjn->bkgn', made_w, made_hot_f)
            numer = numer + jnp.einsum('bkgj,bjn,bjkd->bkgnd', made_w.astype(jnp.bfloat16).astype(jnp.float32), made_hot_f, made_v)
            rounded = lax.optimization_barrier(numer.astype(jnp.bfloat16))
            numer = rounded.astype(jnp.float32)
            top = group_maximum.max(-1)
            scaled = jnp.exp(group_maximum - top[..., None])
            denom = (scaled * total).sum(-1)
            result = jnp.einsum('bkgn,bkgnd->bkgd', scaled, numer) / denom[..., None]
            return result.reshape(BEAM_COUNT, QW).astype(jnp.bfloat16)
        attention = lax.map(attend, jnp.arange(PROMPTS, dtype=jnp.int32)).reshape(BEAM_ROWS, QW)
        results.append(jnp.dot(attention, o_weight, preferred_element_type=jnp.float32).astype(jnp.bfloat16))
    return jnp.stack(results, 0)
```

```python
import math

import jax
import jax.numpy as jnp
import numpy as np
from jax import lax
from jax.experimental import pallas as pl
from jax.experimental.pallas import tpu as pltpu
from jax.sharding import PartitionSpec as P

QUERY_HEADS = 64
KEY_HEADS = 8
HEAD_DIM = 128
BEAM_COUNT = 16
STEPS = 3


EPS = 1e-06
NEG = -1e30
ROPE_BASE = 1000000.0


def rope_parts(positions, head_size):
    half = head_size // 2
    freqs = np.power(ROPE_BASE, -np.arange(half) * 2.0 / head_size)
    angle = positions.astype(jnp.float32)[:, None] * jnp.asarray(freqs, jnp.float32)[None, :]
    return (jnp.cos(angle), jnp.sin(angle))


def apply_rotation(value_rows, cosine_table, sine_table):
    half = value_rows.shape[-1] // 2
    first = value_rows[..., :half]
    second = value_rows[..., half:]
    cosine_table = cosine_table[:, None, :]
    sine_table = sine_table[:, None, :]
    return jnp.concatenate(
        [first * cosine_table - second * sine_table, second * cosine_table + first * sine_table],
        axis=-1,
    )


def local_by_rows(
    hidden,
    norm_gain,
    q_weight,
    q_bias,
    kv_weight,
    kv_bias,
    o_weight,
    prefix_key_cache,
    prefix_value_cache,
    prefix_index,
    prefix_lens,
    tail_key_cache,
    tail_value_cache,
    tail_lens,
    parents,
):
    devices = lax.axis_size("beam")
    me = lax.axis_index("beam")
    rows_per_chip = hidden.shape[1]
    width = hidden.shape[2]
    all_rows = rows_per_chip * devices
    prompt_batch = all_rows // BEAM_COUNT
    head_group = QUERY_HEADS // KEY_HEADS
    q_width = QUERY_HEADS * HEAD_DIM
    q_cols = q_weight.shape[1]
    kv_cols = kv_weight.shape[2]
    prefix_slice = prefix_key_cache.shape[1]
    tail_cache = tail_key_cache.shape[1]
    score_scale = 1.0 / math.sqrt(HEAD_DIM)
    row_ids = jnp.arange(all_rows, dtype=jnp.int32)
    prompt_of = row_ids // BEAM_COUNT
    first_row = me * rows_per_chip
    my_prompt = first_row // BEAM_COUNT
    slot_ids = first_row + jnp.arange(rows_per_chip, dtype=jnp.int32)
    mine = (jnp.arange(prompt_batch, dtype=jnp.int32) == my_prompt)[:, None, None, None]
    joint = jnp.concatenate([q_weight, kv_weight.reshape(width, 2 * kv_cols)], axis=1)
    joint_bias = jnp.concatenate([q_bias, kv_bias.reshape(2 * kv_cols)])
    shared = lambda cache: jnp.stack(
        [lax.dynamic_index_in_dim(cache, prefix_index[p], 0, keepdims=False) for p in range(prompt_batch)], 0
    ).reshape(prompt_batch, prefix_slice, KEY_HEADS, HEAD_DIM)
    slice_keys = shared(prefix_key_cache)
    slice_values = shared(prefix_value_cache)
    slab_ok = (me * prefix_slice + jnp.arange(prefix_slice, dtype=jnp.int32))[
        None, :
    ] < prefix_lens[:, None]
    slab_ok = slab_ok[:, None, None, None, :]
    tail_key_rows = tail_key_cache.reshape(rows_per_chip, tail_cache, KEY_HEADS, HEAD_DIM)
    tail_value_rows = tail_value_cache.reshape(rows_per_chip, tail_cache, KEY_HEADS, HEAD_DIM)
    own_lens = lax.dynamic_slice_in_dim(tail_lens, first_row, rows_per_chip, 0)
    tail_ok = jnp.arange(tail_cache, dtype=jnp.int32)[None, :] < own_lens[:, None]
    ancestors = row_ids
    makers = []
    fresh_keys = []
    current_values = []
    results = []
    for step in range(STEPS):
        chosen = parents[step]
        ancestors = ancestors[chosen]
        makers = [item[chosen] for item in makers] + [row_ids]
        value_rows = lax.all_gather(hidden[step], "beam", axis=0, tiled=True).astype(jnp.float32)
        normed = (
            value_rows
            * lax.rsqrt(jnp.mean(value_rows * value_rows, axis=-1, keepdims=True) + EPS)
            * norm_gain
        ).astype(jnp.bfloat16)
        projected = jnp.dot(normed, joint, preferred_element_type=jnp.float32) + joint_bias
        q_part = projected[:, :q_cols].astype(jnp.bfloat16)
        kv_part = projected[:, q_cols:].astype(jnp.bfloat16).reshape(all_rows, 2, kv_cols)
        positions = prefix_lens[prompt_of] + tail_lens[ancestors] + step
        cosine_table, sine_table = rope_parts(positions, HEAD_DIM)
        q_full, kv_full = (
            lax.all_gather(q_part[:, None, :], "beam", axis=2, tiled=True),
            lax.all_gather(kv_part, "beam", axis=2, tiled=True),
        )
        q_all = q_full[:, 0, :]
        owned_key_value = lax.dynamic_slice_in_dim(kv_full, first_row, rows_per_chip, 0)
        rotated_rows = apply_rotation(
            q_all.astype(jnp.float32).reshape(all_rows, QUERY_HEADS, HEAD_DIM),
            cosine_table,
            sine_table,
        ).astype(jnp.bfloat16)
        local_cosine = lax.dynamic_slice_in_dim(cosine_table, first_row, rows_per_chip, 0)
        local_sine = lax.dynamic_slice_in_dim(sine_table, first_row, rows_per_chip, 0)
        new_key = apply_rotation(
            owned_key_value[:, 0].astype(jnp.float32).reshape(rows_per_chip, KEY_HEADS, HEAD_DIM),
            local_cosine,
            local_sine,
        ).astype(jnp.bfloat16)
        fresh_keys.append(new_key)
        current_values.append(owned_key_value[:, 1].reshape(rows_per_chip, KEY_HEADS, HEAD_DIM))
        query_rows = rotated_rows.reshape(prompt_batch, BEAM_COUNT, KEY_HEADS, head_group, HEAD_DIM)
        pre_scores = (
            jnp.einsum(
                "pbkgd,pskd->pbkgs", query_rows, slice_keys, preferred_element_type=jnp.float32
            )
            * score_scale
        )
        pre_scores = jnp.where(slab_ok, pre_scores, NEG)
        local_q = lax.dynamic_index_in_dim(query_rows, my_prompt, 0, keepdims=False)
        local_anc = lax.dynamic_slice_in_dim(ancestors, my_prompt * BEAM_COUNT, BEAM_COUNT, 0)
        t_scores = (
            jnp.einsum(
                "bkgd,itkd->bkgit", local_q, tail_key_rows, preferred_element_type=jnp.float32
            )
            * score_scale
        )
        t_valid = (local_anc[:, None] == slot_ids[None, :])[:, None, None, :, None] & tail_ok[
            None, None, None, :, :
        ]
        t_scores = jnp.where(t_valid, t_scores, NEG)
        f_keys = jnp.stack(fresh_keys, 0)
        f_values = jnp.stack(current_values, 0)
        local_made = jnp.stack(
            [
                lax.dynamic_slice_in_dim(item, my_prompt * BEAM_COUNT, BEAM_COUNT, 0)
                for item in makers
            ],
            1,
        )
        f_valid = (local_made[:, :, None] == slot_ids[None, None, :])[:, None, None, :, :]
        f_scores = (
            jnp.einsum("bkgd,jikd->bkgji", local_q, f_keys, preferred_element_type=jnp.float32)
            * score_scale
        )
        f_scores = jnp.where(f_valid, f_scores, NEG)
        local_max = jnp.maximum(t_scores.max(axis=(3, 4)), f_scores.max(axis=(3, 4)))
        pre_max = pre_scores.max(-1)
        group_maximum = jnp.where(mine, jnp.maximum(pre_max, local_max[None]), pre_max)
        mine_max = lax.dynamic_index_in_dim(group_maximum, my_prompt, 0, keepdims=False)
        pre_w = jnp.where(slab_ok, jnp.exp(pre_scores - group_maximum[..., None]), 0.0)
        totals = pre_w.sum(-1)
        numer = jnp.einsum(
            "pbkgs,pskd->pbkgd",
            pre_w.astype(jnp.bfloat16),
            slice_values,
            preferred_element_type=jnp.float32,
        )
        t_w = jnp.where(t_valid, jnp.exp(t_scores - mine_max[..., None, None]), 0.0)
        f_w = jnp.where(f_valid, jnp.exp(f_scores - mine_max[..., None, None]), 0.0)
        local_total = t_w.sum(axis=(3, 4)) + f_w.sum(axis=(3, 4))
        local_num = jnp.einsum(
            "bkgit,itkd->bkgd",
            t_w.astype(jnp.bfloat16),
            tail_value_rows,
            preferred_element_type=jnp.float32,
        )
        local_num = local_num + jnp.einsum(
            "bkgji,jikd->bkgd",
            f_w.astype(jnp.bfloat16),
            f_values,
            preferred_element_type=jnp.float32,
        )
        totals = jnp.where(mine, totals + local_total[None], totals)
        numer = jnp.where(mine[..., None], numer + local_num[None], numer)
        sending = numer.astype(jnp.bfloat16).reshape(devices, rows_per_chip, q_width)
        parts = lax.all_to_all(sending, "beam", split_axis=0, concat_axis=0, tiled=True)
        maxima, sums = (
            lax.all_to_all(
                group_maximum.reshape(devices, rows_per_chip, QUERY_HEADS),
                "beam",
                split_axis=0,
                concat_axis=0,
                tiled=True,
            ),
            lax.all_to_all(
                totals.reshape(devices, rows_per_chip, QUERY_HEADS),
                "beam",
                split_axis=0,
                concat_axis=0,
                tiled=True,
            ),
        )
        top = maxima.max(0)
        factors = jnp.exp(maxima - top[None])
        denom = (factors * sums).sum(0)
        combined = jnp.einsum(
            "srh,srhd->rhd",
            factors,
            parts.reshape(devices, rows_per_chip, QUERY_HEADS, HEAD_DIM),
            preferred_element_type=jnp.float32,
        )
        attention = (
            (combined / denom[..., None]).reshape(rows_per_chip, q_width).astype(jnp.bfloat16)
        )
        out_cols = jnp.dot(
            lax.all_gather(attention, "beam", axis=0, tiled=True),
            o_weight,
            preferred_element_type=jnp.float32,
        )
        results.append(out_cols.astype(jnp.bfloat16))
    return jnp.stack(results, 0)


MESH = pl.DeviceIdType.MESH
CONTRACT_LAST = (((1,), (1,)), ((), ()))
LOW = -1e29


def place():
    me = lax.axis_index("beam")
    return me, me // 4, me // 2 % 2, me % 2


def at(z, y, c):
    return (z * 2 + y) * 2 + c


def line(z):
    near = z + 1 - 2 * (z % 2)
    return [(near, 3 - z), (2 - z // 2, near), (3 - 3 * (z // 2), near)]


def middle(z):
    return (z + 1) // 2 == 1


def remote(src, dst, send, recv, target):
    return pltpu.make_async_remote_copy(
        src_ref=src, dst_ref=dst, send_sem=send, recv_sem=recv,
        device_id={"beam": target}, device_id_type=MESH,
    )


class Sends:
    def __init__(self, send):
        self.send, self.sent = send, []

    def push(self, src, dst, recv, target, only=None):
        copy = remote(src, dst, self.send.at[len(self.sent)], recv, target)
        if only is None:
            copy.start()
        else:
            pl.when(only)(copy.start)
        self.sent.append((copy, only))

    def finish(self):
        for copy, only in self.sent:
            if only is None:
                copy.wait_send()
            else:
                pl.when(only)(copy.wait_send)


class Gather:
    def __init__(self, parts, send, recv):
        self.parts, self.recv = parts, recv
        self.sends = Sends(send)
        self.me, self.z, self.y, self.c = place()

    def push(self, part, shard, target, only=None):
        ref = self.parts[part].at[shard]
        self.sends.push(ref, ref, self.recv.at[part, shard], target, only)

    def arrive(self, part, shard):
        ref = self.parts[part].at[shard]
        remote(ref, ref, self.sends.send.at[0], self.recv.at[part, shard], at(self.z, self.y, 1 - self.c)).wait_recv()

    def start(self, part):
        z, y, c = self.z, self.y, self.c
        self.push(part, self.me, at(3 - z, y, c), middle(z))
        self.push(part, self.me, at(line(z)[0][0], y, c))
        self.push(part, self.me, at(z, 1 - y, c))
        self.push(part, self.me, at(z, y, 1 - c))

    def hop(self, part, k):
        z, y, c = self.z, self.y, self.c
        w, onward = line(z)[k]
        shard = at(w, y, c)
        self.arrive(part, shard)
        self.push(part, shard, at(onward, y, c), middle(z))
        self.push(part, shard, at(z, 1 - y, c))
        self.push(part, shard, at(z, y, 1 - c))

    def planes(self):
        return [self.z] + [w for w, _ in line(self.z)]

    def cross(self, part, w):
        shard = at(w, 1 - self.y, self.c)
        self.arrive(part, shard)
        self.push(part, shard, at(self.z, self.y, 1 - self.c))

    def other(self, part, w, v):
        self.arrive(part, at(w, v, 1 - self.c))


def one_hot(mask):
    return jnp.where(mask, 1.0, 0.0).astype(jnp.bfloat16)


def iota(shape, axis):
    return lax.broadcasted_iota(jnp.int32, shape, axis)


def dot(a, b):
    return jnp.dot(a, b, preferred_element_type=jnp.float32)


def dot_t(a, b):
    return lax.dot_general(a, b, CONTRACT_LAST, preferred_element_type=jnp.float32)


def layer_kernel(
    scale,
    x_ref, gain_ref, wq_hbm, qb_ref, wkv_hbm, kvb_ref, wo_hbm, pk_hbm, pv_hbm, tk_hbm, tv_hbm,
    pidx_ref, plen_ref, tlen_ref, tlen_row_ref, par_ref, freq_ref,
    out_ref,
    full, nrm, lhs, wq, wkv, wo, qacc, kvacc, qs, kvx, pk, pv, tk, tv, vtp, vtt, atl, fm, bias, tables,
    own, own_st, yin, yin_st, mg, mg_st, zin, zin_st, fatt,
    asend, arecv, wsem, lsem, xsend, xrecv, qsend, qrecv, ysend, yrecv, zsend, zrecv, fsend, frecv,
):
    me, z, y, c = place()
    core, over = at(z, y, 1 - c), at(z, 1 - y, c)
    parts = full.shape[0]
    width = lhs.shape[1] // parts
    keep = width * 3 // 4
    tail_w = width // 4
    K2 = scale * math.log2(math.e)
    my = z // 2

    total = None
    for t in range(STEPS):
        xt = x_ref[t].astype(jnp.float32)
        ms = jnp.mean(xt * xt, axis=-1, keepdims=True)
        nrm[2 * t : 2 * t + 2, :] = xt * lax.rsqrt(ms + EPS) * gain_ref[...]
    for q in range(parts):
        base = q * width
        rest = nrm[0:6, base + keep : base + width]
        rows67 = [
            jnp.concatenate([rest[3 * h + j : 3 * h + j + 1] for j in range(3)], 1) for h in range(2)
        ]
        block = jnp.concatenate([nrm[0:6, base : base + keep]] + rows67, 0)
        full[q, me] = block.astype(jnp.bfloat16)

    barrier = pltpu.get_barrier_semaphore()
    partners = [at((z + k) % 4, y, p) for k in range(1, 4) for p in range(2)]
    partners += [core, over, at(z, 1 - y, 1 - c)]
    for other in partners:
        pl.semaphore_signal(barrier, inc=1, device_id={"beam": other}, device_id_type=MESH)
    pl.semaphore_wait(barrier, len(partners))

    ga = Gather([full.at[q] for q in range(parts)], asend, arecv)
    for q in range(parts):
        ga.start(q)

    half = wq_hbm.shape[0] // 2
    loads = []
    for src, dst in (
        (wq_hbm.at[0:half], wq.at[0:half]),
        (wkv_hbm, wkv),
        (wq_hbm.at[half : 2 * half], wq.at[half : 2 * half]),
    ):
        loads.append(pltpu.make_async_copy(src, dst, wsem.at[len(loads)]))
        loads[-1].start()
    cache_loads = []
    exchange = Sends(xsend)
    for n, (src, dst) in enumerate(((pk_hbm, pk), (pv_hbm, pv), (tk_hbm, tk), (tv_hbm, tv))):
        for wl in range(2):
            cols = slice(wl * 256, wl * 256 + 256)
            mine = pl.ds(pl.multiple_of(wl * 512 + c * 256, 256), 256)
            theirs = pl.ds(pl.multiple_of(wl * 512 + (1 - c) * 256, 256), 256)
            lead = (slice(None),) * (len(src.shape) - 1)
            cache_loads.append(
                pltpu.make_async_copy(src.at[lead + (mine,)], dst.at[(c,) + lead + (cols,)], lsem.at[n, wl])
            )
            cache_loads[-1].start()
            exchange.push(src.at[lead + (theirs,)], dst.at[(c,) + lead + (cols,)], xrecv.at[n, wl], core)
    out_load = pltpu.make_async_copy(wo_hbm, wo, wsem.at[3])
    out_load.start()

    eye32 = one_hot(iota((32, 32), 0) == iota((32, 32), 1))
    step = [one_hot(iota((32, 32), 0) == par_ref[t : t + 1, :]) for t in range(STEPS)]
    m20 = dot(step[1], step[2]).astype(jnp.bfloat16)
    made = {(0, 0): eye32, (1, 1): eye32, (2, 2): eye32, (1, 0): step[1], (2, 1): step[2], (2, 0): m20}
    anc = [step[0], dot(step[0], step[1]).astype(jnp.bfloat16), dot(step[0], m20).astype(jnp.bfloat16)]
    rho = iota((96, 32), 0)
    prompt = jnp.where(rho >= 48, 1, 0)
    when = lax.shift_right_logical(rho - 48 * prompt, 4)
    row = prompt * 16 + (rho & 15)
    lines = None
    for t in range(STEPS):
        sel = one_hot((when == t) & (row == iota((96, 32), 1)))
        term = dot_t(sel, anc[t])
        lines = term if lines is None else lines + term
    lens = jnp.sum(lines * tlen_row_ref[...].astype(jnp.float32), axis=1, keepdims=True)
    col = iota((96, 1), 0)
    second = col >= 48
    turn = lax.shift_right_logical(col - 48 * jnp.where(second, 1, 0), 4)
    pos = lens + jnp.where(second, plen_ref[1], plen_ref[0]).astype(jnp.float32) + turn.astype(jnp.float32)
    angle = pos * freq_ref[...]
    tables[0] = jnp.cos(angle)
    sine = jnp.sin(angle)
    tables[1] = jnp.where(iota((96, HEAD_DIM), 1) < HEAD_DIM // 2, -sine, sine)
    lane = iota((32, 384), 1)
    sixteen = lax.shift_right_logical(lane, 4)
    lane_step = sixteen - 3 * lax.shift_right_logical(sixteen * 11, 5)
    lane_beam = lane & 15
    pick = lambda p: [
        one_hot((lane_step == t) & (iota((32, 384), 0) == p * 16 + lane_beam)) for t in range(STEPS)
    ]
    here = pick(my)
    atl[...] = dot(anc[0], here[0]) + dot(anc[1], here[1]) + dot(anc[2], here[2])
    dest = pick(c)
    key_row = iota((48, 32), 0)
    fresh = None
    for j in range(STEPS):
        reach = None
        for t in range(j, STEPS):
            term = dot(made[t, j], dest[t])
            reach = term if reach is None else reach + term
        sel = one_hot(
            (lax.shift_right_logical(key_row, 4) == j) & (iota((48, 32), 1) == c * 16 + (key_row & 15))
        )
        term = dot(sel, reach.astype(jnp.bfloat16))
        fresh = term if fresh is None else fresh + term
    fm[...] = jnp.where(fresh > 0.5, 0.0, NEG)

    def tail_bias(i):
        a = (z * 2 + y) * 4 + i
        on = atl[pl.ds(a, 1), :] > 0.5
        ok = iota((256, 384), 0) < tlen_ref[a]
        bias[i] = jnp.where(on & ok, 0.0, NEG)

    for k in range(3):
        for q in range(parts):
            ga.hop(q, k)
        tail_bias(k)
    tail_bias(3)
    for w in ga.planes():
        for q in range(parts):
            ga.cross(q, w)

    for copy in cache_loads:
        copy.wait()
    for copy, _ in exchange.sent:
        copy.wait_recv()
    eye = one_hot(iota((128, 128), 0) == iota((128, 128), 1))

    def turn_values(kvh, carry):
        cols = pl.ds(pl.multiple_of(kvh * 128, 128), 128)
        for p in range(2):
            for s in range(2):
                vtp[kvh, p, :, s * 128 : s * 128 + 128] = dot_t(eye, pv[s, pidx_ref[p], :, cols]).astype(jnp.bfloat16)
        for i in range(4):
            vtt[kvh, i] = dot_t(eye, tv[i // 2, i % 2, :, cols]).astype(jnp.bfloat16)
        return carry

    lax.fori_loop(0, 4, turn_values, 0)

    pr = iota((96, 128), 0)
    pp = jnp.where(pr >= 48, 1, 0)
    local_row = 2 * lax.shift_right_logical(pr - 48 * pp, 4) + (pr & 1)
    shard_row = (pp * 8 + lax.shift_right_logical(pr & 15, 1)) * 8
    high = jnp.where(local_row >= 3, 1, 0)
    source = iota((96, 128), 1)
    first = one_hot(source == shard_row + local_row)
    thirds = [one_hot((source == shard_row + 6 + high) & (local_row - 3 * high == j)) for j in range(3)]
    qacc[...] = jnp.zeros_like(qacc)
    kvacc[...] = jnp.zeros_like(kvacc)
    block = 1024
    for q in range(parts):
        for w in ga.planes():
            for v in (y, 1 - y):
                ga.other(q, w, v)
        tails = None
        for j in range(3):
            got = full[q, :, :, j * tail_w : (j + 1) * tail_w].reshape(128, tail_w)
            both = dot(jnp.concatenate([first, thirds[j]], 0), got)
            lhs[:, q * width + j * tail_w : q * width + (j + 1) * tail_w] = both[:96].astype(jnp.bfloat16)
            tails = both[96:] if tails is None else tails + both[96:]
        lhs[:, q * width + keep : (q + 1) * width] = tails.astype(jnp.bfloat16)
        if q == 0:
            for copy in loads:
                copy.wait()

        def project(k, carry):
            ks = pl.ds(pl.multiple_of(q * width + k * block, block), block)
            a = lhs[:, ks]
            qacc[...] += dot(a, wq[ks, :])
            kvacc[...] += dot_t(a, wkv[:, ks])
            return carry

        lax.fori_loop(0, width // block, project, 0)

    cosine, signed = tables[0], tables[1]

    def rotate(v, co, si):
        return v * co + pltpu.roll(v, HEAD_DIM // 2, 1) * si

    kvx[c] = (kvacc[...] + kvb_ref[...]).astype(jnp.bfloat16)
    pair = Sends(qsend)
    pair.push(kvx.at[c], kvx.at[c], qrecv.at[5, c], core)
    heads = qs.shape[2]
    for h in range(heads):
        cols = slice(h * HEAD_DIM, (h + 1) * HEAD_DIM)
        v = (qacc[:, cols] + qb_ref[:, cols]).astype(jnp.bfloat16).astype(jnp.float32)
        qs[4, c, h] = rotate(v, cosine, signed).astype(jnp.bfloat16)

    target = z % 2
    mine_slot = (z // 2) * 2 + y
    mine_q = qs.at[4, c]
    here_own = target == c
    near_w = z // 2
    pair.push(mine_q, qs.at[4, c], qrecv.at[4, c], core)
    pair.push(mine_q, qs.at[mine_slot, c], qrecv.at[mine_slot, c], at(jnp.minimum(z + 1, 3), y, target), z < 3)
    pair.push(mine_q, qs.at[mine_slot, c], qrecv.at[mine_slot, c], at(jnp.maximum(z - 1, 0), y, target), z > 0)
    pair.push(mine_q, qs.at[mine_slot, c], qrecv.at[mine_slot, c], at(z, 1 - y, target))

    def q_arrive(slot, half_):
        ref = qs.at[slot, half_]
        remote(ref, ref, qsend.at[0], qrecv.at[slot, half_], core).wait_recv()

    def forward(slot, z_to, z_only, only=None):
        for half_ in range(2):
            ref = qs.at[slot, half_]
            pair.push(ref, ref, qrecv.at[slot, half_], at(z_to, y, c), z_only)
            pair.push(ref, ref, qrecv.at[slot, half_], over, only)

    near_slot = near_w * 2 + y
    far_slot = (1 - near_w) * 2 + y

    @pl.when(jnp.logical_not(here_own))
    def _():
        q_arrive(near_slot, 0)
        q_arrive(near_slot, 1)

    away = jnp.logical_not(here_own)
    forward(near_slot, 3 - z, away & middle(z), away)
    q_arrive(4, 1 - c)

    def stat_block(top, total):
        rid = iota((8, 128), 0)
        out = jnp.zeros((8, 128), jnp.float32)
        for n in range(3):
            out = jnp.where(rid == n, top[:, n * 128 : n * 128 + 128], out)
            out = jnp.where(rid == 4 + n, total[:, n * 128 : n * 128 + 128], out)
        return out

    def stats_of(st):
        return (
            jnp.concatenate([st[0:1], st[1:2], st[2:3]], 1),
            jnp.concatenate([st[4:5], st[5:6], st[6:7]], 1),
        )

    def softmax(scores, values):
        top = None
        for s in scores:
            m = jnp.max(s, axis=0, keepdims=True)
            top = m if top is None else jnp.maximum(top, m)
        safe = jnp.maximum(top, LOW)
        num = total = None
        for s, v in zip(scores, values):
            e = jnp.exp2((s - safe) * K2)
            part = jnp.sum(e, axis=0, keepdims=True)
            term = dot(v, e.astype(jnp.bfloat16))
            num = term if num is None else num + term
            total = part if total is None else total + part
        return num, top, total

    def queries(slot, p):
        start = pl.ds(pl.multiple_of(p * 48, 16), 48)
        return qs[slot, :, :, start, :].reshape(384, HEAD_DIM)

    ahead = Sends(ysend)
    back = Sends(zsend)

    def merge(n):
        w = c + 2 * (near_w if n == 0 else 1 - near_w)
        for p in range(2):
            a, b = own.at[2 * n, p], yin.at[n, p]
            for lane_, (src, dst) in enumerate(((a, b), (own_st.at[2 * n, p], yin_st.at[n, p]))):
                remote(dst, dst, ysend.at[0], yrecv.at[n, p, lane_], over).wait_recv()
            ta, sa = stats_of(own_st[2 * n, p])
            tb, sb = stats_of(yin_st[n, p])
            top = jnp.maximum(ta, tb)
            ea, eb = jnp.exp2((ta - top) * K2), jnp.exp2((tb - top) * K2)
            mg[n, p] = (a[...].astype(jnp.float32) * ea + b[...].astype(jnp.float32) * eb).astype(jnp.bfloat16)
            mg_st[n, p] = stat_block(top, sa * ea + sb * eb)
            stay = (w == z) & (c == p)
            go = jnp.logical_not(stay)
            to = jnp.where(stay, core, at(w, y, p))
            back.push(mg.at[n, p], zin.at[z], zrecv.at[z, 0], to, go)
            back.push(mg_st.at[n, p], zin_st.at[z], zrecv.at[z, 1], to, go)

            @pl.when(stay)
            def _():
                zin[z] = mg[n, p]
                zin_st[z] = mg_st[n, p]

    def attend(i, carry):
        odd = i % 2
        late = i // 2
        wl = near_w + late * (1 - 2 * near_w)
        v = y + odd * (1 - 2 * y)
        kvh = wl * 2 + v
        is_pair = here_own & (i == 0)
        slot = jnp.where(is_pair, 4, kvh)

        @pl.when((odd == 1) | (i == 4))
        def _():
            q_arrive(kvh, 0)
            q_arrive(kvh, 1)

        cols = pl.ds(pl.multiple_of(kvh * 128, 128), 128)

        def prefix(p, q):
            out = []
            for s in range(2):
                keys = pk[s, pidx_ref[p], :, cols]
                ok = iota((128, 384), 0) + (at(z, y, s) * 128) < plen_ref[p]
                out.append(jnp.where(ok, dot_t(keys, q), NEG))
            return out, [vtp[kvh, p, :, s * 128 : s * 128 + 128] for s in range(2)]

        p = 1 - my
        num, top, tot = softmax(*prefix(p, queries(slot, p)))
        own[i, p] = num.astype(jnp.bfloat16)
        own_st[i, p] = stat_block(top, tot)
        q = queries(slot, my)
        scores, values = prefix(my, q)
        for n in range(4):
            scores.append(dot_t(tk[n // 2, n % 2, :, cols], q) + bias[n])
            values.append(vtt[kvh, n])
        num, top, tot = softmax(scores, values)
        own[i, my] = num.astype(jnp.bfloat16)
        own_st[i, my] = stat_block(top, tot)
        return carry

    def y_send(n):
        for p in range(2):
            ahead.push(own.at[2 * n + 1, p], yin.at[n, p], yrecv.at[n, p, 0], over)
            ahead.push(own_st.at[2 * n + 1, p], yin_st.at[n, p], yrecv.at[n, p, 1], over)

    lax.fori_loop(0, 1, attend, 0)
    q_arrive(far_slot, 0)
    q_arrive(far_slot, 1)
    forward(far_slot, jnp.clip(3 * (z - 1), 0, 3), middle(z))
    lax.fori_loop(1, 2, attend, 0)
    y_send(0)
    lax.fori_loop(2, 3, attend, 0)
    merge(0)
    lax.fori_loop(3, 4, attend, 0)
    y_send(1)
    merge(1)

    remote(kvx.at[1 - c], kvx.at[1 - c], qsend.at[0], qrecv.at[5, 1 - c], core).wait_recv()
    rows = pl.ds(pl.multiple_of(c * 48, 16), 48)
    lo, hi = kvx[0, rows, :].astype(jnp.float32), kvx[1, rows, :].astype(jnp.float32)
    left = iota((48, HEAD_DIM), 1) < HEAD_DIM // 2
    key = jnp.where(left, lo, pltpu.roll(hi, HEAD_DIM // 2, 1))
    value = jnp.where(left, pltpu.roll(lo, HEAD_DIM // 2, 1), hi)
    key = rotate(key, tables[0, rows, :], tables[1, rows, :]).astype(jnp.bfloat16)
    value_t = dot_t(eye, value.astype(jnp.bfloat16)).astype(jnp.bfloat16)
    score = dot_t(key, queries(4, c)) + fm[...]
    f_num, f_top, f_tot = softmax([score], [value_t])

    for k in range(4):
        w = (z + k) % 4

        def landed():
            remote(zin.at[w], zin.at[w], zsend.at[0], zrecv.at[w, 0], core).wait_recv()
            remote(zin_st.at[w], zin_st.at[w], zsend.at[0], zrecv.at[w, 1], core).wait_recv()

        if k:
            landed()
        else:
            pl.when(jnp.logical_not(here_own))(landed)
    stats = [stats_of(zin_st[k]) for k in range(4)]
    top = f_top
    for t_, _ in stats:
        top = jnp.maximum(top, t_)
    e = jnp.exp2((f_top - top) * K2)
    num, tot = f_num * e, f_tot * e
    for k in range(4):
        e = jnp.exp2((stats[k][0] - top) * K2)
        num = num + zin[k].astype(jnp.float32) * e
        tot = tot + stats[k][1] * e
    att_t = (num / tot).astype(jnp.bfloat16)
    eye384 = one_hot(iota((384, 384), 0) == iota((384, 384), 1))
    att = dot_t(eye384, att_t).astype(jnp.bfloat16)
    for h in range(8):
        fatt[me, :, h * HEAD_DIM : (h + 1) * HEAD_DIM] = att[h * 48 : h * 48 + 48]

    out_load.wait()
    gf = Gather([fatt], fsend, frecv)
    gf.start(0)
    depth = fatt.shape[2]
    result = [None]

    def use(w, v):
        k = (w * 2 + v) * depth
        term = dot(
            jnp.concatenate([fatt[at(w, v, 0)], fatt[at(w, v, 1)]], 0),
            wo[pl.ds(pl.multiple_of(k, depth), depth), :],
        )
        result[0] = term if result[0] is None else result[0] + term

    planes = gf.planes()
    for k in range(3):
        gf.hop(0, k)
        gf.other(0, planes[k], y)
        use(planes[k], y)
    gf.other(0, planes[3], y)
    for w in planes:
        gf.cross(0, w)
    use(planes[3], y)
    for w in planes:
        gf.other(0, w, 1 - y)
        use(w, 1 - y)
    done = result[0].astype(jnp.bfloat16)
    for p in range(2):
        for t in range(STEPS):
            out_ref[t * 32 + p * 16 : t * 32 + p * 16 + 16, :] = done[p * 48 + t * 16 : p * 48 + t * 16 + 16]
    for sends in (ga.sends, exchange, pair, ahead, back, gf.sends):
        sends.finish()


PARTS = 2


def layer(args, scale, devices):
    vmem = pl.BlockSpec(memory_space=pltpu.VMEM)
    smem = pl.BlockSpec(memory_space=pltpu.SMEM)
    hbm = pl.BlockSpec(memory_space=pl.ANY)
    bf = lambda *shape: pltpu.VMEM(shape, jnp.bfloat16)
    fl = lambda *shape: pltpu.VMEM(shape, jnp.float32)
    dma = lambda *shape: pltpu.SemaphoreType.DMA(shape)
    width = args[2].shape[0]
    cols = args[2].shape[1]
    return pl.pallas_call(
        lambda *refs: layer_kernel(scale, *refs),
        out_shape=jax.ShapeDtypeStruct((96, cols), jnp.bfloat16),
        in_specs=[vmem, vmem, hbm, vmem, hbm, vmem, hbm, hbm, hbm, hbm, hbm, smem, smem, smem, vmem, vmem, vmem],
        out_specs=vmem,
        scratch_shapes=[
            bf(PARTS, devices, 8, width * 3 // 4 // PARTS), fl(8, width), bf(96, width),
            bf(width, cols), bf(128, width), bf(width, cols), fl(96, cols), fl(96, 128),
            bf(5, 2, 4, 96, 128), bf(2, 96, 128),
            bf(2, 4, 128, 512), bf(2, 4, 128, 512), bf(2, 2, 256, 512), bf(2, 2, 256, 512),
            bf(4, 2, 128, 256), bf(4, 4, 128, 256), fl(32, 384), fl(48, 384), fl(4, 256, 384), fl(2, 96, 128),
            bf(4, 2, 128, 384), fl(4, 2, 8, 128), bf(2, 2, 128, 384), fl(2, 2, 8, 128),
            bf(2, 2, 128, 384), fl(2, 2, 8, 128), bf(4, 128, 384), fl(4, 8, 128), bf(devices, 48, 1024),
            dma(19 * PARTS), dma(PARTS, devices), dma(4), dma(4, 2), dma(8), dma(4, 2),
            dma(13), dma(6, 2), dma(8), dma(2, 2, 2), dma(8), dma(4, 2), dma(19), dma(1, devices),
        ],
        compiler_params=pltpu.CompilerParams(
            collective_id=0, has_side_effects=True, vmem_limit_bytes=60 * 2**20
        ),
    )(*args)


def local(
    hidden,
    norm_gain,
    q_weight,
    q_bias,
    kv_weight,
    kv_bias,
    o_weight,
    prefix_key_cache,
    prefix_value_cache,
    prefix_index,
    prefix_lens,
    tail_key_cache,
    tail_value_cache,
    tail_lens,
    parents,
):
    devices = lax.axis_size("beam")
    rpc = hidden.shape[1]
    width = hidden.shape[2]
    fits = (
        devices == 16 and rpc == 2 and hidden.shape[0] == STEPS and width == 8192 and q_weight.shape[1] == 512
        and kv_weight.shape[2] == 64 and prefix_index.shape[0] == 2 and prefix_key_cache.shape == (4, 128, 1024)
        and tail_key_cache.shape[1] == 256
    )
    if not fits:
        return local_by_rows(
            hidden, norm_gain, q_weight, q_bias, kv_weight, kv_bias, o_weight, prefix_key_cache,
            prefix_value_cache, prefix_index, prefix_lens, tail_key_cache, tail_value_cache, tail_lens, parents,
        )
    half = np.power(ROPE_BASE, -np.arange(HEAD_DIM // 2) * 2.0 / HEAD_DIM)
    freqs = jnp.asarray(np.concatenate([half, half])[None, :], jnp.float32)
    out = layer(
        (
            hidden, norm_gain[None, :], q_weight, q_bias[None, :],
            jnp.transpose(kv_weight, (1, 2, 0)).reshape(128, width), kv_bias.reshape(1, 128), o_weight,
            prefix_key_cache, prefix_value_cache, tail_key_cache, tail_value_cache,
            prefix_index, prefix_lens, tail_lens, tail_lens[None, :], parents, freqs,
        ),
        1.0 / math.sqrt(HEAD_DIM), devices,
    )
    return out.reshape(STEPS, 32, out.shape[1])


def solution(mesh):
    return jax.shard_map(
        local,
        mesh=mesh,
        in_specs=(
            P(None, ("grp", "beam"), None),
            P(),
            P(None, "beam"),
            P("beam"),
            P(None, None, "beam"),
            P(None, "beam"),
            P(None, "beam"),
            P("grp", "beam", None),
            P("grp", "beam", None),
            P("grp"),
            P("grp"),
            P(("grp", "beam"), None, None),
            P(("grp", "beam"), None, None),
            P("grp"),
            P(None, "grp"),
        ),
        out_specs=P(None, "grp", "beam"),
        check_vma=False,
    )
```

```python
import math

import jax
import jax.numpy as jnp
import numpy as np
from jax import lax
from jax.experimental import pallas as pl
from jax.experimental.pallas import tpu as pltpu
from jax.sharding import PartitionSpec as P

QUERY_HEADS = 64
KEY_HEADS = 8
HEAD_DIM = 128
BEAM_COUNT = 16
STEPS = 3


EPS = 1e-06
NEG = -1e30
ROPE_BASE = 1000000.0


def rope_parts(positions, head_size):
    half = head_size // 2
    freqs = np.power(ROPE_BASE, -np.arange(half) * 2.0 / head_size)
    angle = positions.astype(jnp.float32)[:, None] * jnp.asarray(freqs, jnp.float32)[None, :]
    return (jnp.cos(angle), jnp.sin(angle))


def apply_rotation(value_rows, cosine_table, sine_table):
    half = value_rows.shape[-1] // 2
    first = value_rows[..., :half]
    second = value_rows[..., half:]
    cosine_table = cosine_table[:, None, :]
    sine_table = sine_table[:, None, :]
    return jnp.concatenate(
        [first * cosine_table - second * sine_table, second * cosine_table + first * sine_table],
        axis=-1,
    )


def local_by_rows(
    hidden,
    norm_gain,
    q_weight,
    q_bias,
    kv_weight,
    kv_bias,
    o_weight,
    prefix_key_cache,
    prefix_value_cache,
    prefix_index,
    prefix_lens,
    tail_key_cache,
    tail_value_cache,
    tail_lens,
    parents,
):
    devices = lax.axis_size("beam")
    me = lax.axis_index("beam")
    rows_per_chip = hidden.shape[1]
    width = hidden.shape[2]
    all_rows = rows_per_chip * devices
    prompt_batch = all_rows // BEAM_COUNT
    head_group = QUERY_HEADS // KEY_HEADS
    q_width = QUERY_HEADS * HEAD_DIM
    q_cols = q_weight.shape[1]
    kv_cols = kv_weight.shape[2]
    prefix_slice = prefix_key_cache.shape[1]
    tail_cache = tail_key_cache.shape[1]
    score_scale = 1.0 / math.sqrt(HEAD_DIM)
    row_ids = jnp.arange(all_rows, dtype=jnp.int32)
    prompt_of = row_ids // BEAM_COUNT
    first_row = me * rows_per_chip
    my_prompt = first_row // BEAM_COUNT
    slot_ids = first_row + jnp.arange(rows_per_chip, dtype=jnp.int32)
    mine = (jnp.arange(prompt_batch, dtype=jnp.int32) == my_prompt)[:, None, None, None]
    joint = jnp.concatenate([q_weight, kv_weight.reshape(width, 2 * kv_cols)], axis=1)
    joint_bias = jnp.concatenate([q_bias, kv_bias.reshape(2 * kv_cols)])
    shared = lambda cache: jnp.stack(
        [lax.dynamic_index_in_dim(cache, prefix_index[p], 0, keepdims=False) for p in range(prompt_batch)], 0
    ).reshape(prompt_batch, prefix_slice, KEY_HEADS, HEAD_DIM)
    slice_keys = shared(prefix_key_cache)
    slice_values = shared(prefix_value_cache)
    slab_ok = (me * prefix_slice + jnp.arange(prefix_slice, dtype=jnp.int32))[
        None, :
    ] < prefix_lens[:, None]
    slab_ok = slab_ok[:, None, None, None, :]
    tail_key_rows = tail_key_cache.reshape(rows_per_chip, tail_cache, KEY_HEADS, HEAD_DIM)
    tail_value_rows = tail_value_cache.reshape(rows_per_chip, tail_cache, KEY_HEADS, HEAD_DIM)
    own_lens = lax.dynamic_slice_in_dim(tail_lens, first_row, rows_per_chip, 0)
    tail_ok = jnp.arange(tail_cache, dtype=jnp.int32)[None, :] < own_lens[:, None]
    ancestors = row_ids
    makers = []
    fresh_keys = []
    current_values = []
    results = []
    for step in range(STEPS):
        chosen = parents[step]
        ancestors = ancestors[chosen]
        makers = [item[chosen] for item in makers] + [row_ids]
        value_rows = lax.all_gather(hidden[step], "beam", axis=0, tiled=True).astype(jnp.float32)
        normed = (
            value_rows
            * lax.rsqrt(jnp.mean(value_rows * value_rows, axis=-1, keepdims=True) + EPS)
            * norm_gain
        ).astype(jnp.bfloat16)
        projected = jnp.dot(normed, joint, preferred_element_type=jnp.float32) + joint_bias
        q_part = projected[:, :q_cols].astype(jnp.bfloat16)
        kv_part = projected[:, q_cols:].astype(jnp.bfloat16).reshape(all_rows, 2, kv_cols)
        positions = prefix_lens[prompt_of] + tail_lens[ancestors] + step
        cosine_table, sine_table = rope_parts(positions, HEAD_DIM)
        q_full, kv_full = (
            lax.all_gather(q_part[:, None, :], "beam", axis=2, tiled=True),
            lax.all_gather(kv_part, "beam", axis=2, tiled=True),
        )
        q_all = q_full[:, 0, :]
        owned_key_value = lax.dynamic_slice_in_dim(kv_full, first_row, rows_per_chip, 0)
        rotated_rows = apply_rotation(
            q_all.astype(jnp.float32).reshape(all_rows, QUERY_HEADS, HEAD_DIM),
            cosine_table,
            sine_table,
        ).astype(jnp.bfloat16)
        local_cosine = lax.dynamic_slice_in_dim(cosine_table, first_row, rows_per_chip, 0)
        local_sine = lax.dynamic_slice_in_dim(sine_table, first_row, rows_per_chip, 0)
        new_key = apply_rotation(
            owned_key_value[:, 0].astype(jnp.float32).reshape(rows_per_chip, KEY_HEADS, HEAD_DIM),
            local_cosine,
            local_sine,
        ).astype(jnp.bfloat16)
        fresh_keys.append(new_key)
        current_values.append(owned_key_value[:, 1].reshape(rows_per_chip, KEY_HEADS, HEAD_DIM))
        query_rows = rotated_rows.reshape(prompt_batch, BEAM_COUNT, KEY_HEADS, head_group, HEAD_DIM)
        pre_scores = (
            jnp.einsum(
                "pbkgd,pskd->pbkgs", query_rows, slice_keys, preferred_element_type=jnp.float32
            )
            * score_scale
        )
        pre_scores = jnp.where(slab_ok, pre_scores, NEG)
        local_q = lax.dynamic_index_in_dim(query_rows, my_prompt, 0, keepdims=False)
        local_anc = lax.dynamic_slice_in_dim(ancestors, my_prompt * BEAM_COUNT, BEAM_COUNT, 0)
        t_scores = (
            jnp.einsum(
                "bkgd,itkd->bkgit", local_q, tail_key_rows, preferred_element_type=jnp.float32
            )
            * score_scale
        )
        t_valid = (local_anc[:, None] == slot_ids[None, :])[:, None, None, :, None] & tail_ok[
            None, None, None, :, :
        ]
        t_scores = jnp.where(t_valid, t_scores, NEG)
        f_keys = jnp.stack(fresh_keys, 0)
        f_values = jnp.stack(current_values, 0)
        local_made = jnp.stack(
            [
                lax.dynamic_slice_in_dim(item, my_prompt * BEAM_COUNT, BEAM_COUNT, 0)
                for item in makers
            ],
            1,
        )
        f_valid = (local_made[:, :, None] == slot_ids[None, None, :])[:, None, None, :, :]
        f_scores = (
            jnp.einsum("bkgd,jikd->bkgji", local_q, f_keys, preferred_element_type=jnp.float32)
            * score_scale
        )
        f_scores = jnp.where(f_valid, f_scores, NEG)
        local_max = jnp.maximum(t_scores.max(axis=(3, 4)), f_scores.max(axis=(3, 4)))
        pre_max = pre_scores.max(-1)
        group_maximum = jnp.where(mine, jnp.maximum(pre_max, local_max[None]), pre_max)
        mine_max = lax.dynamic_index_in_dim(group_maximum, my_prompt, 0, keepdims=False)
        pre_w = jnp.where(slab_ok, jnp.exp(pre_scores - group_maximum[..., None]), 0.0)
        totals = pre_w.sum(-1)
        numer = jnp.einsum(
            "pbkgs,pskd->pbkgd",
            pre_w.astype(jnp.bfloat16),
            slice_values,
            preferred_element_type=jnp.float32,
        )
        t_w = jnp.where(t_valid, jnp.exp(t_scores - mine_max[..., None, None]), 0.0)
        f_w = jnp.where(f_valid, jnp.exp(f_scores - mine_max[..., None, None]), 0.0)
        local_total = t_w.sum(axis=(3, 4)) + f_w.sum(axis=(3, 4))
        local_num = jnp.einsum(
            "bkgit,itkd->bkgd",
            t_w.astype(jnp.bfloat16),
            tail_value_rows,
            preferred_element_type=jnp.float32,
        )
        local_num = local_num + jnp.einsum(
            "bkgji,jikd->bkgd",
            f_w.astype(jnp.bfloat16),
            f_values,
            preferred_element_type=jnp.float32,
        )
        totals = jnp.where(mine, totals + local_total[None], totals)
        numer = jnp.where(mine[..., None], numer + local_num[None], numer)
        sending = numer.astype(jnp.bfloat16).reshape(devices, rows_per_chip, q_width)
        parts = lax.all_to_all(sending, "beam", split_axis=0, concat_axis=0, tiled=True)
        maxima, sums = (
            lax.all_to_all(
                group_maximum.reshape(devices, rows_per_chip, QUERY_HEADS),
                "beam",
                split_axis=0,
                concat_axis=0,
                tiled=True,
            ),
            lax.all_to_all(
                totals.reshape(devices, rows_per_chip, QUERY_HEADS),
                "beam",
                split_axis=0,
                concat_axis=0,
                tiled=True,
            ),
        )
        top = maxima.max(0)
        factors = jnp.exp(maxima - top[None])
        denom = (factors * sums).sum(0)
        combined = jnp.einsum(
            "srh,srhd->rhd",
            factors,
            parts.reshape(devices, rows_per_chip, QUERY_HEADS, HEAD_DIM),
            preferred_element_type=jnp.float32,
        )
        attention = (
            (combined / denom[..., None]).reshape(rows_per_chip, q_width).astype(jnp.bfloat16)
        )
        out_cols = jnp.dot(
            lax.all_gather(attention, "beam", axis=0, tiled=True),
            o_weight,
            preferred_element_type=jnp.float32,
        )
        results.append(out_cols.astype(jnp.bfloat16))
    return jnp.stack(results, 0)


MESH = pl.DeviceIdType.MESH
CONTRACT_LAST = (((1,), (1,)), ((), ()))
LOW = -1e29


def place():
    me = lax.axis_index("beam")
    return me, me // 4, me // 2 % 2, me % 2


def at(z, y, c):
    return (z * 2 + y) * 2 + c


def line(z):
    return [z + 1 - 2 * (z % 2), 3 - z, (z + 2) % 4]


def middle(z):
    return (z + 1) // 2 == 1


def remote(src, dst, send, recv, target):
    return pltpu.make_async_remote_copy(
        src_ref=src, dst_ref=dst, send_sem=send, recv_sem=recv,
        device_id={"beam": target}, device_id_type=MESH,
    )


class Sends:
    def __init__(self, send):
        self.send, self.sent = send, []

    def push(self, src, dst, recv, target, only=None):
        copy = remote(src, dst, self.send.at[len(self.sent)], recv, target)
        if only is None:
            copy.start()
        else:
            pl.when(only)(copy.start)
        self.sent.append((copy, only))

    def finish(self):
        for copy, only in self.sent:
            if only is None:
                copy.wait_send()
            else:
                pl.when(only)(copy.wait_send)


class Gather:
    def __init__(self, parts, send, recv):
        self.parts, self.recv = parts, recv
        self.sends = Sends(send)
        self.me, self.z, self.y, self.c = place()

    def push(self, part, shard, target, only=None):
        ref = self.parts[part].at[shard]
        self.sends.push(ref, ref, self.recv.at[part, shard], target, only)

    def arrive(self, part, shard):
        ref = self.parts[part].at[shard]
        remote(ref, ref, self.sends.send.at[0], self.recv.at[part, shard], at(self.z, self.y, 1 - self.c)).wait_recv()

    def start(self, part):
        z, y, c = self.z, self.y, self.c
        self.push(part, self.me, at(line(z)[0], y, c))
        self.push(part, self.me, at(3 - z, y, c))
        self.push(part, self.me, at(z, 1 - y, c))
        self.push(part, self.me, at(z, y, 1 - c))

    def hop(self, part, k):
        z, y, c = self.z, self.y, self.c
        shard = at(line(z)[k], y, c)
        self.arrive(part, shard)
        if k < 2:
            self.push(part, shard, at(line(z)[1 - k], y, c), middle(z))
        self.push(part, shard, at(z, 1 - y, c))
        self.push(part, shard, at(z, y, 1 - c))

    def planes(self):
        return [self.z] + line(self.z)

    def cross(self, part, w):
        shard = at(w, 1 - self.y, self.c)
        self.arrive(part, shard)
        self.push(part, shard, at(self.z, self.y, 1 - self.c))

    def other(self, part, w, v):
        self.arrive(part, at(w, v, 1 - self.c))


def one_hot(mask):
    return jnp.where(mask, 1.0, 0.0).astype(jnp.bfloat16)


def iota(shape, axis):
    return lax.broadcasted_iota(jnp.int32, shape, axis)


def dot(a, b):
    return jnp.dot(a, b, preferred_element_type=jnp.float32)


def dot_t(a, b):
    return lax.dot_general(a, b, CONTRACT_LAST, preferred_element_type=jnp.float32)


def layer_kernel(
    scale,
    x_hbm, gain_hbm, wq_hbm, qb_hbm, wkv_hbm, kvb_hbm, wo_hbm, pk_hbm, pv_hbm, tk_hbm, tv_hbm,
    pidx_ref, plen_ref, tlen_ref, tlen_hbm, par_hbm, freq_hbm,
    out_ref,
    x_ref, gain_ref, par_ref, tlen_row_ref, freq_ref, qb_ref, kvb_ref, ssem,
    full, nrm, lhs, wq, wkv, wo, qacc, kvacc, qs, kvx, pk, pv, tk, tv, vtp, vtt, atl, fm, bias, tables,
    own, own_st, yin, yin_st, mg, mg_st, zin, zin_st, fatt,
    asend, arecv, wsem, lsem, xsend, xrecv, qsend, qrecv, ysend, yrecv, zsend, zrecv, fsend, frecv,
):
    me, z, y, c = place()
    core, over = at(z, y, 1 - c), at(z, 1 - y, c)
    parts = full.shape[0]
    width = lhs.shape[1] // parts
    keep = width * 3 // 4
    tail_w = width // 4
    K2 = scale * math.log2(math.e)
    my = z // 2

    barrier = pltpu.get_barrier_semaphore()
    partners = [at((z + k) % 4, y, p) for k in range(1, 4) for p in range(2)]
    partners += [core, over, at(z, 1 - y, 1 - c)]
    for other in partners:
        pl.semaphore_signal(barrier, inc=1, device_id={"beam": other}, device_id_type=MESH)
    smalls = []
    for src, dst in (
        (x_hbm, x_ref), (gain_hbm, gain_ref), (par_hbm, par_ref), (tlen_hbm, tlen_row_ref), (freq_hbm, freq_ref),
        (qb_hbm, qb_ref), (kvb_hbm, kvb_ref),
    ):
        smalls.append(pltpu.make_async_copy(src, dst, ssem.at[len(smalls)]))
        smalls[-1].start()
    smalls[0].wait()
    smalls[1].wait()

    total = None
    for t in range(STEPS):
        xt = x_ref[t].astype(jnp.float32)
        ms = jnp.mean(xt * xt, axis=-1, keepdims=True)
        nrm[2 * t : 2 * t + 2, :] = xt * lax.rsqrt(ms + EPS) * gain_ref[...]
    for q in range(parts):
        base = q * width
        rest = nrm[0:6, base + keep : base + width]
        rows67 = [
            jnp.concatenate([rest[3 * h + j : 3 * h + j + 1] for j in range(3)], 1) for h in range(2)
        ]
        block = jnp.concatenate([nrm[0:6, base : base + keep]] + rows67, 0)
        full[q, me] = block.astype(jnp.bfloat16)

    pl.semaphore_wait(barrier, len(partners))

    ga = Gather([full.at[q] for q in range(parts)], asend, arecv)
    for q in range(parts):
        ga.start(q)

    half = wq_hbm.shape[0] // 2
    loads = []
    for src, dst in (
        (wq_hbm.at[0:half], wq.at[0:half]),
        (wkv_hbm, wkv),
        (wq_hbm.at[half : 2 * half], wq.at[half : 2 * half]),
    ):
        loads.append(pltpu.make_async_copy(src, dst, wsem.at[len(loads)]))
        loads[-1].start()
    cache_loads = []
    exchange = Sends(xsend)
    for n, (src, dst) in enumerate(((pk_hbm, pk), (pv_hbm, pv), (tk_hbm, tk), (tv_hbm, tv))):
        for wl in range(2):
            cols = slice(wl * 256, wl * 256 + 256)
            mine = pl.ds(pl.multiple_of(wl * 512 + c * 256, 256), 256)
            theirs = pl.ds(pl.multiple_of(wl * 512 + (1 - c) * 256, 256), 256)
            lead = (slice(None),) * (len(src.shape) - 1)
            cache_loads.append(
                pltpu.make_async_copy(src.at[lead + (mine,)], dst.at[(c,) + lead + (cols,)], lsem.at[n, wl])
            )
            cache_loads[-1].start()
            exchange.push(src.at[lead + (theirs,)], dst.at[(c,) + lead + (cols,)], xrecv.at[n, wl], core)
    out_load = pltpu.make_async_copy(wo_hbm, wo, wsem.at[3])
    out_load.start()

    for copy in smalls[2:]:
        copy.wait()
    eye32 = one_hot(iota((32, 32), 0) == iota((32, 32), 1))
    step = [one_hot(iota((32, 32), 0) == par_ref[t : t + 1, :]) for t in range(STEPS)]
    m20 = dot(step[1], step[2]).astype(jnp.bfloat16)
    made = {(0, 0): eye32, (1, 1): eye32, (2, 2): eye32, (1, 0): step[1], (2, 1): step[2], (2, 0): m20}
    anc = [step[0], dot(step[0], step[1]).astype(jnp.bfloat16), dot(step[0], m20).astype(jnp.bfloat16)]
    rho = iota((96, 32), 0)
    prompt = jnp.where(rho >= 48, 1, 0)
    when = lax.shift_right_logical(rho - 48 * prompt, 4)
    row = prompt * 16 + (rho & 15)
    lines = None
    for t in range(STEPS):
        sel = one_hot((when == t) & (row == iota((96, 32), 1)))
        term = dot_t(sel, anc[t])
        lines = term if lines is None else lines + term
    lens = jnp.sum(lines * tlen_row_ref[...].astype(jnp.float32), axis=1, keepdims=True)
    col = iota((96, 1), 0)
    second = col >= 48
    turn = lax.shift_right_logical(col - 48 * jnp.where(second, 1, 0), 4)
    pos = lens + jnp.where(second, plen_ref[1], plen_ref[0]).astype(jnp.float32) + turn.astype(jnp.float32)
    angle = pos * freq_ref[...]
    tables[0] = jnp.cos(angle)
    sine = jnp.sin(angle)
    tables[1] = jnp.where(iota((96, HEAD_DIM), 1) < HEAD_DIM // 2, -sine, sine)
    lane = iota((32, 384), 1)
    sixteen = lax.shift_right_logical(lane, 4)
    lane_step = sixteen - 3 * lax.shift_right_logical(sixteen * 11, 5)
    lane_beam = lane & 15
    pick = lambda p: [
        one_hot((lane_step == t) & (iota((32, 384), 0) == p * 16 + lane_beam)) for t in range(STEPS)
    ]
    here = pick(my)
    atl[...] = dot(anc[0], here[0]) + dot(anc[1], here[1]) + dot(anc[2], here[2])
    dest = pick(c)
    key_row = iota((48, 32), 0)
    fresh = None
    for j in range(STEPS):
        reach = None
        for t in range(j, STEPS):
            term = dot(made[t, j], dest[t])
            reach = term if reach is None else reach + term
        sel = one_hot(
            (lax.shift_right_logical(key_row, 4) == j) & (iota((48, 32), 1) == c * 16 + (key_row & 15))
        )
        term = dot(sel, reach.astype(jnp.bfloat16))
        fresh = term if fresh is None else fresh + term
    fm[...] = jnp.where(fresh > 0.5, 0.0, NEG)

    def tail_bias(i):
        a = (z * 2 + y) * 4 + i
        on = atl[pl.ds(a, 1), :] > 0.5
        ok = iota((256, 384), 0) < tlen_ref[a]
        bias[i] = jnp.where(on & ok, 0.0, NEG)

    for q in range(parts):
        ga.hop(q, 0)
        ga.hop(q, 1)
    tail_bias(0)
    tail_bias(1)
    for q in range(parts):
        ga.hop(q, 2)
    tail_bias(2)
    tail_bias(3)
    for w in ga.planes():
        for q in range(parts):
            ga.cross(q, w)

    for copy in cache_loads:
        copy.wait()
    for copy, _ in exchange.sent:
        copy.wait_recv()
    eye = one_hot(iota((128, 128), 0) == iota((128, 128), 1))

    def turn_values(kvh, carry):
        cols = pl.ds(pl.multiple_of(kvh * 128, 128), 128)
        for p in range(2):
            for s in range(2):
                vtp[kvh, p, :, s * 128 : s * 128 + 128] = dot_t(eye, pv[s, pidx_ref[p], :, cols]).astype(jnp.bfloat16)
        for i in range(4):
            vtt[kvh, i] = dot_t(eye, tv[i // 2, i % 2, :, cols]).astype(jnp.bfloat16)
        return carry

    lax.fori_loop(0, 4, turn_values, 0)

    pr = iota((96, 128), 0)
    pp = jnp.where(pr >= 48, 1, 0)
    local_row = 2 * lax.shift_right_logical(pr - 48 * pp, 4) + (pr & 1)
    shard_row = (pp * 8 + lax.shift_right_logical(pr & 15, 1)) * 8
    high = jnp.where(local_row >= 3, 1, 0)
    source = iota((96, 128), 1)
    first = one_hot(source == shard_row + local_row)
    thirds = [one_hot((source == shard_row + 6 + high) & (local_row - 3 * high == j)) for j in range(3)]
    qacc[...] = jnp.zeros_like(qacc)
    kvacc[...] = jnp.zeros_like(kvacc)
    block = 1024
    for q in range(parts):
        for w in ga.planes():
            for v in (y, 1 - y):
                ga.other(q, w, v)
        tails = None
        for j in range(3):
            got = full[q, :, :, j * tail_w : (j + 1) * tail_w].reshape(128, tail_w)
            both = dot(jnp.concatenate([first, thirds[j]], 0), got)
            lhs[:, q * width + j * tail_w : q * width + (j + 1) * tail_w] = both[:96].astype(jnp.bfloat16)
            tails = both[96:] if tails is None else tails + both[96:]
        lhs[:, q * width + keep : (q + 1) * width] = tails.astype(jnp.bfloat16)
        if q == 0:
            for copy in loads:
                copy.wait()

        def project(k, carry):
            ks = pl.ds(pl.multiple_of(q * width + k * block, block), block)
            a = lhs[:, ks]
            qacc[...] += dot(a, wq[ks, :])
            kvacc[...] += dot_t(a, wkv[:, ks])
            return carry

        lax.fori_loop(0, width // block, project, 0)

    cosine, signed = tables[0], tables[1]

    def rotate(v, co, si):
        return v * co + pltpu.roll(v, HEAD_DIM // 2, 1) * si

    kvx[c] = (kvacc[...] + jnp.concatenate([kvb_ref[0:1], kvb_ref[1:2]], 1)).astype(jnp.bfloat16)
    pair = Sends(qsend)
    pair.push(kvx.at[c], kvx.at[c], qrecv.at[5, c], core)
    heads = qs.shape[2]
    for h in range(heads):
        cols = slice(h * HEAD_DIM, (h + 1) * HEAD_DIM)
        v = (qacc[:, cols] + qb_ref[:, cols]).astype(jnp.bfloat16).astype(jnp.float32)
        qs[4, c, h] = rotate(v, cosine, signed).astype(jnp.bfloat16)

    target = z % 2
    mine_slot = (z // 2) * 2 + y
    mine_q = qs.at[4, c]
    here_own = target == c
    near_w = z // 2
    pair.push(mine_q, qs.at[mine_slot, c], qrecv.at[mine_slot, c], at(line(z)[0], y, target))
    pair.push(mine_q, qs.at[4, c], qrecv.at[4, c], core)
    pair.push(mine_q, qs.at[mine_slot, c], qrecv.at[mine_slot, c], at(z, 1 - y, target))
    pair.push(mine_q, qs.at[mine_slot, c], qrecv.at[mine_slot, c], at(3 - z, y, target))

    def q_arrive(slot, half_):
        ref = qs.at[slot, half_]
        remote(ref, ref, qsend.at[0], qrecv.at[slot, half_], core).wait_recv()

    def forward(slot, z_to, z_only, only):
        for half_ in range(2):
            pl.when(only)(lambda: q_arrive(slot, half_))
            ref = qs.at[slot, half_]
            if z_to is not None:
                pair.push(ref, ref, qrecv.at[slot, half_], at(z_to, y, c), z_only)
            pair.push(ref, ref, qrecv.at[slot, half_], over, only)

    near_slot = near_w * 2 + y
    far_slot = (1 - near_w) * 2 + y
    away = jnp.logical_not(here_own)
    both = away & middle(z)
    forward(near_slot, line(z)[1], both, away)
    forward(far_slot, line(z)[0], both, both)
    q_arrive(4, 1 - c)

    def stat_block(top, total):
        rid = iota((8, 128), 0)
        out = jnp.zeros((8, 128), jnp.float32)
        for n in range(3):
            out = jnp.where(rid == n, top[:, n * 128 : n * 128 + 128], out)
            out = jnp.where(rid == 4 + n, total[:, n * 128 : n * 128 + 128], out)
        return out

    def stats_of(st):
        return (
            jnp.concatenate([st[0:1], st[1:2], st[2:3]], 1),
            jnp.concatenate([st[4:5], st[5:6], st[6:7]], 1),
        )

    def softmax(scores, values):
        top = None
        for s in scores:
            m = jnp.max(s, axis=0, keepdims=True)
            top = m if top is None else jnp.maximum(top, m)
        safe = jnp.maximum(top, LOW)
        num = total = None
        for s, v in zip(scores, values):
            e = jnp.exp2((s - safe) * K2)
            part = jnp.sum(e, axis=0, keepdims=True)
            term = dot(v, e.astype(jnp.bfloat16))
            num = term if num is None else num + term
            total = part if total is None else total + part
        return num, top, total

    def queries(slot, p):
        start = pl.ds(pl.multiple_of(p * 48, 16), 48)
        return qs[slot, :, :, start, :].reshape(384, HEAD_DIM)

    ahead = Sends(ysend)
    back = Sends(zsend)

    def merge(n):
        w = c + 2 * (near_w if n == 0 else 1 - near_w)
        for p in range(2):
            a, b = own.at[2 * n, p], yin.at[n, p]
            for lane_, (src, dst) in enumerate(((a, b), (own_st.at[2 * n, p], yin_st.at[n, p]))):
                remote(dst, dst, ysend.at[0], yrecv.at[n, p, lane_], over).wait_recv()
            ta, sa = stats_of(own_st[2 * n, p])
            tb, sb = stats_of(yin_st[n, p])
            top = jnp.maximum(ta, tb)
            ea, eb = jnp.exp2((ta - top) * K2), jnp.exp2((tb - top) * K2)
            mg[n, p] = (a[...].astype(jnp.float32) * ea + b[...].astype(jnp.float32) * eb).astype(jnp.bfloat16)
            mg_st[n, p] = stat_block(top, sa * ea + sb * eb)
            stay = (w == z) & (c == p)
            go = jnp.logical_not(stay)
            to = jnp.where(stay, core, at(w, y, p))
            back.push(mg.at[n, p], zin.at[z], zrecv.at[z, 0], to, go)
            back.push(mg_st.at[n, p], zin_st.at[z], zrecv.at[z, 1], to, go)

            @pl.when(stay)
            def _():
                zin[z] = mg[n, p]
                zin_st[z] = mg_st[n, p]

    def attend(i, carry):
        odd = i % 2
        late = i // 2
        wl = near_w + late * (1 - 2 * near_w)
        v = y + odd * (1 - 2 * y)
        kvh = wl * 2 + v
        is_pair = here_own & (i == 0)
        slot = jnp.where(is_pair, 4, kvh)

        @pl.when((odd == 1) | (i == 4))
        def _():
            q_arrive(kvh, 0)
            q_arrive(kvh, 1)

        cols = pl.ds(pl.multiple_of(kvh * 128, 128), 128)

        def prefix(p, q):
            out = []
            for s in range(2):
                keys = pk[s, pidx_ref[p], :, cols]
                ok = iota((128, 384), 0) + (at(z, y, s) * 128) < plen_ref[p]
                out.append(jnp.where(ok, dot_t(keys, q), NEG))
            return out, [vtp[kvh, p, :, s * 128 : s * 128 + 128] for s in range(2)]

        p = 1 - my
        num, top, tot = softmax(*prefix(p, queries(slot, p)))
        own[i, p] = num.astype(jnp.bfloat16)
        own_st[i, p] = stat_block(top, tot)
        q = queries(slot, my)
        scores, values = prefix(my, q)
        for n in range(4):
            scores.append(dot_t(tk[n // 2, n % 2, :, cols], q) + bias[n])
            values.append(vtt[kvh, n])
        num, top, tot = softmax(scores, values)
        own[i, my] = num.astype(jnp.bfloat16)
        own_st[i, my] = stat_block(top, tot)
        return carry

    def y_send(n):
        for p in range(2):
            ahead.push(own.at[2 * n + 1, p], yin.at[n, p], yrecv.at[n, p, 0], over)
            ahead.push(own_st.at[2 * n + 1, p], yin_st.at[n, p], yrecv.at[n, p, 1], over)

    lax.fori_loop(0, 1, attend, 0)
    forward(far_slot, None, None, jnp.logical_not(both))
    lax.fori_loop(1, 4, attend, 0)
    y_send(1)
    y_send(0)
    merge(1)
    merge(0)

    remote(kvx.at[1 - c], kvx.at[1 - c], qsend.at[0], qrecv.at[5, 1 - c], core).wait_recv()
    rows = pl.ds(pl.multiple_of(c * 48, 16), 48)
    lo, hi = kvx[0, rows, :].astype(jnp.float32), kvx[1, rows, :].astype(jnp.float32)
    left = iota((48, HEAD_DIM), 1) < HEAD_DIM // 2
    key = jnp.where(left, lo, pltpu.roll(hi, HEAD_DIM // 2, 1))
    value = jnp.where(left, pltpu.roll(lo, HEAD_DIM // 2, 1), hi)
    key = rotate(key, tables[0, rows, :], tables[1, rows, :]).astype(jnp.bfloat16)
    value_t = dot_t(eye, value.astype(jnp.bfloat16)).astype(jnp.bfloat16)
    score = dot_t(key, queries(4, c)) + fm[...]
    f_num, f_top, f_tot = softmax([score], [value_t])

    for k in range(4):
        w = (z + k) % 4

        def landed():
            remote(zin.at[w], zin.at[w], zsend.at[0], zrecv.at[w, 0], core).wait_recv()
            remote(zin_st.at[w], zin_st.at[w], zsend.at[0], zrecv.at[w, 1], core).wait_recv()

        if k:
            landed()
        else:
            pl.when(jnp.logical_not(here_own))(landed)
    stats = [stats_of(zin_st[k]) for k in range(4)]
    top = f_top
    for t_, _ in stats:
        top = jnp.maximum(top, t_)
    e = jnp.exp2((f_top - top) * K2)
    num, tot = f_num * e, f_tot * e
    for k in range(4):
        e = jnp.exp2((stats[k][0] - top) * K2)
        num = num + zin[k].astype(jnp.float32) * e
        tot = tot + stats[k][1] * e
    att_t = (num / tot).astype(jnp.bfloat16)
    eye384 = one_hot(iota((384, 384), 0) == iota((384, 384), 1))
    att = dot_t(eye384, att_t).astype(jnp.bfloat16)
    for h in range(8):
        fatt[me, :, h * HEAD_DIM : (h + 1) * HEAD_DIM] = att[h * 48 : h * 48 + 48]

    out_load.wait()
    gf = Gather([fatt], fsend, frecv)
    gf.start(0)
    depth = fatt.shape[2]
    result = [None]

    def use(w, v):
        k = (w * 2 + v) * depth
        term = dot(
            jnp.concatenate([fatt[at(w, v, 0)], fatt[at(w, v, 1)]], 0),
            wo[pl.ds(pl.multiple_of(k, depth), depth), :],
        )
        result[0] = term if result[0] is None else result[0] + term

    planes = gf.planes()
    for k in range(3):
        gf.hop(0, k)
        gf.other(0, planes[k], y)
        use(planes[k], y)
    gf.other(0, planes[3], y)
    for w in planes:
        gf.cross(0, w)
    use(planes[3], y)
    for w in planes:
        gf.other(0, w, 1 - y)
        use(w, 1 - y)
    done = result[0].astype(jnp.bfloat16)
    for p in range(2):
        for t in range(STEPS):
            out_ref[t * 32 + p * 16 : t * 32 + p * 16 + 16, :] = done[p * 48 + t * 16 : p * 48 + t * 16 + 16]
    for sends in (ga.sends, exchange, pair, ahead, back, gf.sends):
        sends.finish()


PARTS = 2


def layer(args, scale, devices):
    vmem = pl.BlockSpec(memory_space=pltpu.VMEM)
    smem = pl.BlockSpec(memory_space=pltpu.SMEM)
    hbm = pl.BlockSpec(memory_space=pltpu.HBM)
    bf = lambda *shape: pltpu.VMEM(shape, jnp.bfloat16)
    fl = lambda *shape: pltpu.VMEM(shape, jnp.float32)
    dma = lambda *shape: pltpu.SemaphoreType.DMA(shape)
    width = args[2].shape[0]
    cols = args[2].shape[1]
    return pl.pallas_call(
        lambda *refs: layer_kernel(scale, *refs),
        out_shape=jax.ShapeDtypeStruct((96, cols), jnp.bfloat16),
        in_specs=[hbm] * 11 + [smem] * 3 + [hbm] * 3,
        out_specs=vmem,
        scratch_shapes=[
            bf(STEPS, 2, width), fl(1, width), pltpu.VMEM((STEPS, 32), jnp.int32), pltpu.VMEM((1, 32), jnp.int32),
            fl(1, HEAD_DIM), fl(1, cols), fl(2, 64), dma(7),
            bf(PARTS, devices, 8, width * 3 // 4 // PARTS), fl(8, width), bf(96, width),
            bf(width, cols), bf(128, width), bf(width, cols), fl(96, cols), fl(96, 128),
            bf(5, 2, 4, 96, 128), bf(2, 96, 128),
            bf(2, 4, 128, 512), bf(2, 4, 128, 512), bf(2, 2, 256, 512), bf(2, 2, 256, 512),
            bf(4, 2, 128, 256), bf(4, 4, 128, 256), fl(32, 384), fl(48, 384), fl(4, 256, 384), fl(2, 96, 128),
            bf(4, 2, 128, 384), fl(4, 2, 8, 128), bf(2, 2, 128, 384), fl(2, 2, 8, 128),
            bf(2, 2, 128, 384), fl(2, 2, 8, 128), bf(4, 128, 384), fl(4, 8, 128), bf(devices, 48, 1024),
            dma(19 * PARTS), dma(PARTS, devices), dma(4), dma(4, 2), dma(8), dma(4, 2),
            dma(15), dma(6, 2), dma(8), dma(2, 2, 2), dma(8), dma(4, 2), dma(19), dma(1, devices),
        ],
        compiler_params=pltpu.CompilerParams(
            collective_id=0, has_side_effects=True, vmem_limit_bytes=60 * 2**20
        ),
    )(*args)


def local(
    hidden,
    norm_gain,
    q_weight,
    q_bias,
    kv_weight,
    kv_bias,
    o_weight,
    prefix_key_cache,
    prefix_value_cache,
    prefix_index,
    prefix_lens,
    tail_key_cache,
    tail_value_cache,
    tail_lens,
    parents,
):
    devices = lax.axis_size("beam")
    rpc = hidden.shape[1]
    width = hidden.shape[2]
    fits = (
        devices == 16 and rpc == 2 and hidden.shape[0] == STEPS and width == 8192 and q_weight.shape[1] == 512
        and kv_weight.shape[2] == 64 and prefix_index.shape[0] == 2 and prefix_key_cache.shape == (4, 128, 1024)
        and tail_key_cache.shape[1] == 256
    )
    if not fits:
        return local_by_rows(
            hidden, norm_gain, q_weight, q_bias, kv_weight, kv_bias, o_weight, prefix_key_cache,
            prefix_value_cache, prefix_index, prefix_lens, tail_key_cache, tail_value_cache, tail_lens, parents,
        )
    half = np.power(ROPE_BASE, -np.arange(HEAD_DIM // 2) * 2.0 / HEAD_DIM)
    freqs = jnp.asarray(np.concatenate([half, half])[None, :], jnp.float32)
    out = layer(
        (
            hidden, norm_gain[None, :], q_weight, q_bias[None, :],
            jnp.transpose(kv_weight, (1, 2, 0)).reshape(128, width), kv_bias, o_weight,
            prefix_key_cache, prefix_value_cache, tail_key_cache, tail_value_cache,
            prefix_index, prefix_lens, tail_lens, tail_lens[None, :], parents, freqs,
        ),
        1.0 / math.sqrt(HEAD_DIM), devices,
    )
    return out.reshape(STEPS, 32, out.shape[1])


def solution(mesh):
    return jax.shard_map(
        local,
        mesh=mesh,
        in_specs=(
            P(None, ("grp", "beam"), None),
            P(),
            P(None, "beam"),
            P("beam"),
            P(None, None, "beam"),
            P(None, "beam"),
            P(None, "beam"),
            P("grp", "beam", None),
            P("grp", "beam", None),
            P("grp"),
            P("grp"),
            P(("grp", "beam"), None, None),
            P(("grp", "beam"), None, None),
            P("grp"),
            P(None, "grp"),
        ),
        out_specs=P(None, "grp", "beam"),
        check_vma=False,
    )
```

```python
import math

import jax
import jax.numpy as jnp
import numpy as np
from jax import lax
from jax.experimental import pallas as pl
from jax.experimental.pallas import tpu as pltpu
from jax.sharding import PartitionSpec as P

QUERY_HEADS = 64
KEY_HEADS = 8
HEAD_DIM = 128
BEAM_COUNT = 16
STEPS = 3


EPS = 1e-06
NEG = -1e30
ROPE_BASE = 1000000.0


def rope_parts(positions, head_size):
    half = head_size // 2
    freqs = np.power(ROPE_BASE, -np.arange(half) * 2.0 / head_size)
    angle = positions.astype(jnp.float32)[:, None] * jnp.asarray(freqs, jnp.float32)[None, :]
    return (jnp.cos(angle), jnp.sin(angle))


def apply_rotation(value_rows, cosine_table, sine_table):
    half = value_rows.shape[-1] // 2
    first = value_rows[..., :half]
    second = value_rows[..., half:]
    cosine_table = cosine_table[:, None, :]
    sine_table = sine_table[:, None, :]
    return jnp.concatenate(
        [first * cosine_table - second * sine_table, second * cosine_table + first * sine_table],
        axis=-1,
    )


def local_by_rows(
    hidden,
    norm_gain,
    q_weight,
    q_bias,
    kv_weight,
    kv_bias,
    o_weight,
    prefix_key_cache,
    prefix_value_cache,
    prefix_index,
    prefix_lens,
    tail_key_cache,
    tail_value_cache,
    tail_lens,
    parents,
):
    devices = lax.axis_size("beam")
    me = lax.axis_index("beam")
    rows_per_chip = hidden.shape[1]
    width = hidden.shape[2]
    all_rows = rows_per_chip * devices
    prompt_batch = all_rows // BEAM_COUNT
    head_group = QUERY_HEADS // KEY_HEADS
    q_width = QUERY_HEADS * HEAD_DIM
    q_cols = q_weight.shape[1]
    kv_cols = kv_weight.shape[2]
    prefix_slice = prefix_key_cache.shape[1]
    tail_cache = tail_key_cache.shape[1]
    score_scale = 1.0 / math.sqrt(HEAD_DIM)
    row_ids = jnp.arange(all_rows, dtype=jnp.int32)
    prompt_of = row_ids // BEAM_COUNT
    first_row = me * rows_per_chip
    my_prompt = first_row // BEAM_COUNT
    slot_ids = first_row + jnp.arange(rows_per_chip, dtype=jnp.int32)
    mine = (jnp.arange(prompt_batch, dtype=jnp.int32) == my_prompt)[:, None, None, None]
    joint = jnp.concatenate([q_weight, kv_weight.reshape(width, 2 * kv_cols)], axis=1)
    joint_bias = jnp.concatenate([q_bias, kv_bias.reshape(2 * kv_cols)])
    shared = lambda cache: jnp.stack(
        [lax.dynamic_index_in_dim(cache, prefix_index[p], 0, keepdims=False) for p in range(prompt_batch)], 0
    ).reshape(prompt_batch, prefix_slice, KEY_HEADS, HEAD_DIM)
    slice_keys = shared(prefix_key_cache)
    slice_values = shared(prefix_value_cache)
    slab_ok = (me * prefix_slice + jnp.arange(prefix_slice, dtype=jnp.int32))[
        None, :
    ] < prefix_lens[:, None]
    slab_ok = slab_ok[:, None, None, None, :]
    tail_key_rows = tail_key_cache.reshape(rows_per_chip, tail_cache, KEY_HEADS, HEAD_DIM)
    tail_value_rows = tail_value_cache.reshape(rows_per_chip, tail_cache, KEY_HEADS, HEAD_DIM)
    own_lens = lax.dynamic_slice_in_dim(tail_lens, first_row, rows_per_chip, 0)
    tail_ok = jnp.arange(tail_cache, dtype=jnp.int32)[None, :] < own_lens[:, None]
    ancestors = row_ids
    makers = []
    fresh_keys = []
    current_values = []
    results = []
    for step in range(STEPS):
        chosen = parents[step]
        ancestors = ancestors[chosen]
        makers = [item[chosen] for item in makers] + [row_ids]
        value_rows = lax.all_gather(hidden[step], "beam", axis=0, tiled=True).astype(jnp.float32)
        normed = (
            value_rows
            * lax.rsqrt(jnp.mean(value_rows * value_rows, axis=-1, keepdims=True) + EPS)
            * norm_gain
        ).astype(jnp.bfloat16)
        projected = jnp.dot(normed, joint, preferred_element_type=jnp.float32) + joint_bias
        q_part = projected[:, :q_cols].astype(jnp.bfloat16)
        kv_part = projected[:, q_cols:].astype(jnp.bfloat16).reshape(all_rows, 2, kv_cols)
        positions = prefix_lens[prompt_of] + tail_lens[ancestors] + step
        cosine_table, sine_table = rope_parts(positions, HEAD_DIM)
        q_full, kv_full = (
            lax.all_gather(q_part[:, None, :], "beam", axis=2, tiled=True),
            lax.all_gather(kv_part, "beam", axis=2, tiled=True),
        )
        q_all = q_full[:, 0, :]
        owned_key_value = lax.dynamic_slice_in_dim(kv_full, first_row, rows_per_chip, 0)
        rotated_rows = apply_rotation(
            q_all.astype(jnp.float32).reshape(all_rows, QUERY_HEADS, HEAD_DIM),
            cosine_table,
            sine_table,
        ).astype(jnp.bfloat16)
        local_cosine = lax.dynamic_slice_in_dim(cosine_table, first_row, rows_per_chip, 0)
        local_sine = lax.dynamic_slice_in_dim(sine_table, first_row, rows_per_chip, 0)
        new_key = apply_rotation(
            owned_key_value[:, 0].astype(jnp.float32).reshape(rows_per_chip, KEY_HEADS, HEAD_DIM),
            local_cosine,
            local_sine,
        ).astype(jnp.bfloat16)
        fresh_keys.append(new_key)
        current_values.append(owned_key_value[:, 1].reshape(rows_per_chip, KEY_HEADS, HEAD_DIM))
        query_rows = rotated_rows.reshape(prompt_batch, BEAM_COUNT, KEY_HEADS, head_group, HEAD_DIM)
        pre_scores = (
            jnp.einsum(
                "pbkgd,pskd->pbkgs", query_rows, slice_keys, preferred_element_type=jnp.float32
            )
            * score_scale
        )
        pre_scores = jnp.where(slab_ok, pre_scores, NEG)
        local_q = lax.dynamic_index_in_dim(query_rows, my_prompt, 0, keepdims=False)
        local_anc = lax.dynamic_slice_in_dim(ancestors, my_prompt * BEAM_COUNT, BEAM_COUNT, 0)
        t_scores = (
            jnp.einsum(
                "bkgd,itkd->bkgit", local_q, tail_key_rows, preferred_element_type=jnp.float32
            )
            * score_scale
        )
        t_valid = (local_anc[:, None] == slot_ids[None, :])[:, None, None, :, None] & tail_ok[
            None, None, None, :, :
        ]
        t_scores = jnp.where(t_valid, t_scores, NEG)
        f_keys = jnp.stack(fresh_keys, 0)
        f_values = jnp.stack(current_values, 0)
        local_made = jnp.stack(
            [
                lax.dynamic_slice_in_dim(item, my_prompt * BEAM_COUNT, BEAM_COUNT, 0)
                for item in makers
            ],
            1,
        )
        f_valid = (local_made[:, :, None] == slot_ids[None, None, :])[:, None, None, :, :]
        f_scores = (
            jnp.einsum("bkgd,jikd->bkgji", local_q, f_keys, preferred_element_type=jnp.float32)
            * score_scale
        )
        f_scores = jnp.where(f_valid, f_scores, NEG)
        local_max = jnp.maximum(t_scores.max(axis=(3, 4)), f_scores.max(axis=(3, 4)))
        pre_max = pre_scores.max(-1)
        group_maximum = jnp.where(mine, jnp.maximum(pre_max, local_max[None]), pre_max)
        mine_max = lax.dynamic_index_in_dim(group_maximum, my_prompt, 0, keepdims=False)
        pre_w = jnp.where(slab_ok, jnp.exp(pre_scores - group_maximum[..., None]), 0.0)
        totals = pre_w.sum(-1)
        numer = jnp.einsum(
            "pbkgs,pskd->pbkgd",
            pre_w.astype(jnp.bfloat16),
            slice_values,
            preferred_element_type=jnp.float32,
        )
        t_w = jnp.where(t_valid, jnp.exp(t_scores - mine_max[..., None, None]), 0.0)
        f_w = jnp.where(f_valid, jnp.exp(f_scores - mine_max[..., None, None]), 0.0)
        local_total = t_w.sum(axis=(3, 4)) + f_w.sum(axis=(3, 4))
        local_num = jnp.einsum(
            "bkgit,itkd->bkgd",
            t_w.astype(jnp.bfloat16),
            tail_value_rows,
            preferred_element_type=jnp.float32,
        )
        local_num = local_num + jnp.einsum(
            "bkgji,jikd->bkgd",
            f_w.astype(jnp.bfloat16),
            f_values,
            preferred_element_type=jnp.float32,
        )
        totals = jnp.where(mine, totals + local_total[None], totals)
        numer = jnp.where(mine[..., None], numer + local_num[None], numer)
        sending = numer.astype(jnp.bfloat16).reshape(devices, rows_per_chip, q_width)
        parts = lax.all_to_all(sending, "beam", split_axis=0, concat_axis=0, tiled=True)
        maxima, sums = (
            lax.all_to_all(
                group_maximum.reshape(devices, rows_per_chip, QUERY_HEADS),
                "beam",
                split_axis=0,
                concat_axis=0,
                tiled=True,
            ),
            lax.all_to_all(
                totals.reshape(devices, rows_per_chip, QUERY_HEADS),
                "beam",
                split_axis=0,
                concat_axis=0,
                tiled=True,
            ),
        )
        top = maxima.max(0)
        factors = jnp.exp(maxima - top[None])
        denom = (factors * sums).sum(0)
        combined = jnp.einsum(
            "srh,srhd->rhd",
            factors,
            parts.reshape(devices, rows_per_chip, QUERY_HEADS, HEAD_DIM),
            preferred_element_type=jnp.float32,
        )
        attention = (
            (combined / denom[..., None]).reshape(rows_per_chip, q_width).astype(jnp.bfloat16)
        )
        out_cols = jnp.dot(
            lax.all_gather(attention, "beam", axis=0, tiled=True),
            o_weight,
            preferred_element_type=jnp.float32,
        )
        results.append(out_cols.astype(jnp.bfloat16))
    return jnp.stack(results, 0)


MESH = pl.DeviceIdType.MESH
CONTRACT_LAST = (((1,), (1,)), ((), ()))
LOW = -1e29


def place():
    me = lax.axis_index("beam")
    return me, me // 4, me // 2 % 2, me % 2


def at(z, y, c):
    return (z * 2 + y) * 2 + c


def line(z):
    return [z + 1 - 2 * (z % 2), 3 - z, (z + 2) % 4]


def middle(z):
    return (z + 1) // 2 == 1


def outer(z):
    return (z + 1) // 2 != 1


def remote(src, dst, send, recv, target):
    return pltpu.make_async_remote_copy(
        src_ref=src, dst_ref=dst, send_sem=send, recv_sem=recv,
        device_id={"beam": target}, device_id_type=MESH,
    )


class Sends:
    def __init__(self, send):
        self.send, self.sent = send, []

    def push(self, src, dst, recv, target, only=None):
        copy = remote(src, dst, self.send.at[len(self.sent)], recv, target)
        if only is None:
            copy.start()
        else:
            pl.when(only)(copy.start)
        self.sent.append((copy, only))

    def finish(self):
        for copy, only in self.sent:
            if only is None:
                copy.wait_send()
            else:
                pl.when(only)(copy.wait_send)


class Gather:
    def __init__(self, parts, send, recv):
        self.parts, self.recv = parts, recv
        self.sends = Sends(send)
        self.me, self.z, self.y, self.c = place()

    def push(self, part, shard, target, only=None):
        ref = self.parts[part].at[shard]
        self.sends.push(ref, ref, self.recv.at[part, shard], target, only)

    def arrive(self, part, shard):
        ref = self.parts[part].at[shard]
        remote(ref, ref, self.sends.send.at[0], self.recv.at[part, shard], at(self.z, self.y, 1 - self.c)).wait_recv()

    def start(self, part):
        z, y, c = self.z, self.y, self.c
        self.push(part, self.me, at(line(z)[0], y, c))
        self.push(part, self.me, at(3 - z, y, c))
        self.push(part, self.me, at(z, 1 - y, c))
        self.push(part, self.me, at(z, y, 1 - c))

    def hop(self, part, k):
        z, y, c = self.z, self.y, self.c
        shard = at(line(z)[k], y, c)
        self.arrive(part, shard)
        if k < 2:
            self.push(part, shard, at(line(z)[1 - k], y, c), middle(z))
        self.push(part, shard, at(z, 1 - y, c))
        self.push(part, shard, at(z, y, 1 - c))

    def planes(self):
        return [self.z] + line(self.z)

    def cross(self, part, w):
        shard = at(w, 1 - self.y, self.c)
        self.arrive(part, shard)
        self.push(part, shard, at(self.z, self.y, 1 - self.c))

    def other(self, part, w, v):
        self.arrive(part, at(w, v, 1 - self.c))


def one_hot(mask):
    return jnp.where(mask, 1.0, 0.0).astype(jnp.bfloat16)


def iota(shape, axis):
    return lax.broadcasted_iota(jnp.int32, shape, axis)


def dot(a, b):
    return jnp.dot(a, b, preferred_element_type=jnp.float32)


def dot_t(a, b):
    return lax.dot_general(a, b, CONTRACT_LAST, preferred_element_type=jnp.float32)


def layer_kernel(
    scale,
    x_hbm, gain_hbm, wq_hbm, qb_hbm, wkv_hbm, kvb_hbm, wo_hbm, pk_hbm, pv_hbm, tk_hbm, tv_hbm,
    pidx_hbm, plen_hbm, tlens_hbm, tlen_hbm, par_hbm, freq_hbm,
    out_ref,
    pidx_ref, plen_ref, tlen_ref,
    x_ref, gain_ref, par_ref, tlen_row_ref, freq_ref, qb_ref, kvb_ref, ssem,
    full, nrm, lhs, wq, wkv, wo, qacc, kvacc, qs, kvx, pk, pv, tk, tv, vtp, vtt, atl, fm, bias, tables,
    own, own_st, yin, yin_st, mg, mg_st, zin, zin_st, fatt,
    asend, arecv, wsem, lsem, xsend, xrecv, qsend, qrecv, ysend, yrecv, zsend, zrecv, fsend, frecv,
):
    me, z, y, c = place()
    core, over = at(z, y, 1 - c), at(z, 1 - y, c)
    parts = full.shape[0]
    width = lhs.shape[1] // parts
    keep = width * 3 // 4
    tail_w = width // 4
    K2 = scale * math.log2(math.e)
    my = z // 2

    smalls = []
    for src, dst in (
        (x_hbm, x_ref), (gain_hbm, gain_ref), (par_hbm, par_ref), (tlen_hbm, tlen_row_ref), (freq_hbm, freq_ref),
        (qb_hbm, qb_ref), (kvb_hbm, kvb_ref), (pidx_hbm, pidx_ref), (plen_hbm, plen_ref), (tlens_hbm, tlen_ref),
    ):
        smalls.append(pltpu.make_async_copy(src, dst, ssem.at[len(smalls)]))
        smalls[-1].start()
    barrier = pltpu.get_barrier_semaphore()
    partners = [at((z + k) % 4, y, p) for k in range(1, 4) for p in range(2)]
    partners += [core, over, at(z, 1 - y, 1 - c)]
    for other in partners:
        pl.semaphore_signal(barrier, inc=1, device_id={"beam": other}, device_id_type=MESH)
    smalls[0].wait()
    smalls[1].wait()

    total = None
    for t in range(STEPS):
        xt = x_ref[t].astype(jnp.float32)
        ms = jnp.mean(xt * xt, axis=-1, keepdims=True)
        nrm[2 * t : 2 * t + 2, :] = xt * lax.rsqrt(ms + EPS) * gain_ref[...]
    for q in range(parts):
        base = q * width
        rest = nrm[0:6, base + keep : base + width]
        rows67 = [
            jnp.concatenate([rest[3 * h + j : 3 * h + j + 1] for j in range(3)], 1) for h in range(2)
        ]
        block = jnp.concatenate([nrm[0:6, base : base + keep]] + rows67, 0)
        full[q, me] = block.astype(jnp.bfloat16)

    pl.semaphore_wait(barrier, len(partners))

    ga = Gather([full.at[q] for q in range(parts)], asend, arecv)
    for q in range(parts):
        ga.start(q)

    half = wq_hbm.shape[0] // 2
    loads = []
    for src, dst in (
        (wq_hbm.at[0:half], wq.at[0:half]),
        (wkv_hbm, wkv),
        (wq_hbm.at[half : 2 * half], wq.at[half : 2 * half]),
    ):
        loads.append(pltpu.make_async_copy(src, dst, wsem.at[len(loads)]))
        loads[-1].start()
    cache_loads = []
    exchange = Sends(xsend)
    for n, (src, dst) in enumerate(((pk_hbm, pk), (pv_hbm, pv), (tk_hbm, tk), (tv_hbm, tv))):
        for wl in range(2):
            cols = slice(wl * 256, wl * 256 + 256)
            mine = pl.ds(pl.multiple_of(wl * 512 + c * 256, 256), 256)
            theirs = pl.ds(pl.multiple_of(wl * 512 + (1 - c) * 256, 256), 256)
            lead = (slice(None),) * (len(src.shape) - 1)
            cache_loads.append(
                pltpu.make_async_copy(src.at[lead + (mine,)], dst.at[(c,) + lead + (cols,)], lsem.at[n, wl])
            )
            cache_loads[-1].start()
            exchange.push(src.at[lead + (theirs,)], dst.at[(c,) + lead + (cols,)], xrecv.at[n, wl], core)
    out_load = pltpu.make_async_copy(wo_hbm, wo, wsem.at[3])
    out_load.start()

    for copy in smalls[2:]:
        copy.wait()
    eye32 = one_hot(iota((32, 32), 0) == iota((32, 32), 1))
    step = [one_hot(iota((32, 32), 0) == par_ref[t : t + 1, :]) for t in range(STEPS)]
    m20 = dot(step[1], step[2]).astype(jnp.bfloat16)
    made = {(0, 0): eye32, (1, 1): eye32, (2, 2): eye32, (1, 0): step[1], (2, 1): step[2], (2, 0): m20}
    anc = [step[0], dot(step[0], step[1]).astype(jnp.bfloat16), dot(step[0], m20).astype(jnp.bfloat16)]
    rho = iota((96, 32), 0)
    prompt = jnp.where(rho >= 48, 1, 0)
    when = lax.shift_right_logical(rho - 48 * prompt, 4)
    row = prompt * 16 + (rho & 15)
    lines = None
    for t in range(STEPS):
        sel = one_hot((when == t) & (row == iota((96, 32), 1)))
        term = dot_t(sel, anc[t])
        lines = term if lines is None else lines + term
    lens = jnp.sum(lines * tlen_row_ref[...].astype(jnp.float32), axis=1, keepdims=True)
    col = iota((96, 1), 0)
    second = col >= 48
    turn = lax.shift_right_logical(col - 48 * jnp.where(second, 1, 0), 4)
    pos = lens + jnp.where(second, plen_ref[1], plen_ref[0]).astype(jnp.float32) + turn.astype(jnp.float32)
    angle = pos * freq_ref[...]
    tables[0] = jnp.cos(angle)
    sine = jnp.sin(angle)
    tables[1] = jnp.where(iota((96, HEAD_DIM), 1) < HEAD_DIM // 2, -sine, sine)
    lane = iota((32, 384), 1)
    sixteen = lax.shift_right_logical(lane, 4)
    lane_step = sixteen - 3 * lax.shift_right_logical(sixteen * 11, 5)
    lane_beam = lane & 15
    pick = lambda p: [
        one_hot((lane_step == t) & (iota((32, 384), 0) == p * 16 + lane_beam)) for t in range(STEPS)
    ]
    here = pick(my)
    atl[...] = dot(anc[0], here[0]) + dot(anc[1], here[1]) + dot(anc[2], here[2])
    dest = pick(c)
    key_row = iota((48, 32), 0)
    fresh = None
    for j in range(STEPS):
        reach = None
        for t in range(j, STEPS):
            term = dot(made[t, j], dest[t])
            reach = term if reach is None else reach + term
        sel = one_hot(
            (lax.shift_right_logical(key_row, 4) == j) & (iota((48, 32), 1) == c * 16 + (key_row & 15))
        )
        term = dot(sel, reach.astype(jnp.bfloat16))
        fresh = term if fresh is None else fresh + term
    fm[...] = jnp.where(fresh > 0.5, 0.0, NEG)

    def tail_bias(i):
        a = (z * 2 + y) * 4 + i
        on = atl[pl.ds(a, 1), :] > 0.5
        ok = iota((256, 384), 0) < tlen_ref[a]
        bias[i] = jnp.where(on & ok, 0.0, NEG)

    for q in range(parts):
        ga.hop(q, 0)
        ga.hop(q, 1)
    tail_bias(0)
    tail_bias(1)
    for q in range(parts):
        ga.hop(q, 2)
    tail_bias(2)
    tail_bias(3)
    for w in ga.planes():
        for q in range(parts):
            ga.cross(q, w)

    for copy in cache_loads:
        copy.wait()
    for copy, _ in exchange.sent:
        copy.wait_recv()
    eye = one_hot(iota((128, 128), 0) == iota((128, 128), 1))

    def turn_values(kvh, carry):
        cols = pl.ds(pl.multiple_of(kvh * 128, 128), 128)
        for p in range(2):
            for s in range(2):
                vtp[kvh, p, :, s * 128 : s * 128 + 128] = dot_t(eye, pv[s, pidx_ref[p], :, cols]).astype(jnp.bfloat16)
        for i in range(4):
            vtt[kvh, i] = dot_t(eye, tv[i // 2, i % 2, :, cols]).astype(jnp.bfloat16)
        return carry

    lax.fori_loop(0, 4, turn_values, 0)

    pr = iota((96, 128), 0)
    pp = jnp.where(pr >= 48, 1, 0)
    local_row = 2 * lax.shift_right_logical(pr - 48 * pp, 4) + (pr & 1)
    shard_row = (pp * 8 + lax.shift_right_logical(pr & 15, 1)) * 8
    high = jnp.where(local_row >= 3, 1, 0)
    source = iota((96, 128), 1)
    first = one_hot(source == shard_row + local_row)
    thirds = [one_hot((source == shard_row + 6 + high) & (local_row - 3 * high == j)) for j in range(3)]
    qacc[...] = jnp.zeros_like(qacc)
    kvacc[...] = jnp.zeros_like(kvacc)
    block = 2048
    for q in range(parts):
        for w in ga.planes():
            for v in (y, 1 - y):
                ga.other(q, w, v)
        tails = None
        for j in range(3):
            got = full[q, :, :, j * tail_w : (j + 1) * tail_w].reshape(128, tail_w)
            both = dot(jnp.concatenate([first, thirds[j]], 0), got)
            lhs[:, q * width + j * tail_w : q * width + (j + 1) * tail_w] = both[:96].astype(jnp.bfloat16)
            tails = both[96:] if tails is None else tails + both[96:]
        lhs[:, q * width + keep : (q + 1) * width] = tails.astype(jnp.bfloat16)
        if q == 0:
            for copy in loads:
                copy.wait()

        def project(k, carry):
            ks = pl.ds(pl.multiple_of(q * width + k * block, block), block)
            a = lhs[:, ks]
            qacc[...] += dot(a, wq[ks, :])
            kvacc[...] += dot_t(a, wkv[:, ks])
            return carry

        lax.fori_loop(0, width // block, project, 0)

    cosine, signed = tables[0], tables[1]

    def rotate(v, co, si):
        return v * co + pltpu.roll(v, HEAD_DIM // 2, 1) * si

    kvx[c] = (kvacc[...] + jnp.concatenate([kvb_ref[0:1], kvb_ref[1:2]], 1)).astype(jnp.bfloat16)
    pair = Sends(qsend)
    pair.push(kvx.at[c], kvx.at[c], qrecv.at[5, c, 0], core)
    heads = qs.shape[2]
    for h in range(heads):
        cols = slice(h * HEAD_DIM, (h + 1) * HEAD_DIM)
        v = (qacc[:, cols] + qb_ref[:, cols]).astype(jnp.bfloat16).astype(jnp.float32)
        qs[4, c, h] = rotate(v, cosine, signed).astype(jnp.bfloat16)

    target = z % 2
    mine_slot = (z // 2) * 2 + y
    here_own = target == c
    near_w = z // 2
    near_z, facing_z, third_z = line(z)

    def piece(slot, half_, n):
        return qs.at[slot, half_, 2 * n : 2 * n + 2]

    for n in range(2):
        def give(slot, to, only=None):
            pair.push(piece(4, c, n), piece(slot, c, n), qrecv.at[slot, c, n], to, only)

        give(mine_slot, at(near_z, y, target))
        give(4, core)
        give(mine_slot, at(z, 1 - y, target))
        give(mine_slot, at(third_z, y, target), outer(z))
        give(mine_slot, at(facing_z, y, target))

    def q_landed(slot, half_, n):
        ref = piece(slot, half_, n)
        remote(ref, ref, qsend.at[0], qrecv.at[slot, half_, n], core).wait_recv()

    def q_arrive(slot, half_):
        for n in range(2):
            q_landed(slot, half_, n)

    def relay(slot, only, targets):
        for n in range(2):
            for half_ in range(2):
                pl.when(only)(lambda: q_landed(slot, half_, n))
                for to, go in targets:
                    ref = piece(slot, half_, n)
                    pair.push(ref, ref, qrecv.at[slot, half_, n], to, go)

    near_slot = near_w * 2 + y
    far_slot = (1 - near_w) * 2 + y
    away = jnp.logical_not(here_own)
    inner_away = away & middle(z)
    relay(near_slot, away, [(over, away & outer(z))])
    relay(far_slot, inner_away, [(at(near_z, y, c), inner_away), (over, inner_away)])
    q_arrive(4, 1 - c)

    def stat_block(top, total):
        rid = iota((8, 128), 0)
        out = jnp.zeros((8, 128), jnp.float32)
        for n in range(3):
            out = jnp.where(rid == n, top[:, n * 128 : n * 128 + 128], out)
            out = jnp.where(rid == 4 + n, total[:, n * 128 : n * 128 + 128], out)
        return out

    def stats_of(st):
        return (
            jnp.concatenate([st[0:1], st[1:2], st[2:3]], 1),
            jnp.concatenate([st[4:5], st[5:6], st[6:7]], 1),
        )

    def softmax(scores, values):
        top = None
        for s in scores:
            m = jnp.max(s, axis=0, keepdims=True)
            top = m if top is None else jnp.maximum(top, m)
        safe = jnp.maximum(top, LOW)
        num = total = None
        for s, v in zip(scores, values):
            e = jnp.exp2((s - safe) * K2)
            part = jnp.sum(e, axis=0, keepdims=True)
            term = dot(v, e.astype(jnp.bfloat16))
            num = term if num is None else num + term
            total = part if total is None else total + part
        return num, top, total

    def queries(slot, p):
        start = pl.ds(pl.multiple_of(p * 48, 16), 48)
        return qs[slot, :, :, start, :].reshape(384, HEAD_DIM)

    ahead = Sends(ysend)
    back = Sends(zsend)

    def merge(n):
        w = c + 2 * (near_w if n == 0 else 1 - near_w)
        for p in range(2):
            a, b = own.at[2 * n, p], yin.at[n, p]
            for lane_, (src, dst) in enumerate(((a, b), (own_st.at[2 * n, p], yin_st.at[n, p]))):
                remote(dst, dst, ysend.at[0], yrecv.at[n, p, lane_], over).wait_recv()
            ta, sa = stats_of(own_st[2 * n, p])
            tb, sb = stats_of(yin_st[n, p])
            top = jnp.maximum(ta, tb)
            ea, eb = jnp.exp2((ta - top) * K2), jnp.exp2((tb - top) * K2)
            mg[n, p] = (a[...].astype(jnp.float32) * ea + b[...].astype(jnp.float32) * eb).astype(jnp.bfloat16)
            mg_st[n, p] = stat_block(top, sa * ea + sb * eb)
            stay = (w == z) & (c == p)
            go = jnp.logical_not(stay)
            to = jnp.where(stay, core, at(w, y, p))
            back.push(mg.at[n, p], zin.at[z], zrecv.at[z, 0], to, go)
            back.push(mg_st.at[n, p], zin_st.at[z], zrecv.at[z, 1], to, go)

            @pl.when(stay)
            def _():
                zin[z] = mg[n, p]
                zin_st[z] = mg_st[n, p]

    def attend(i, carry):
        odd = i % 2
        late = i // 2
        wl = near_w + late * (1 - 2 * near_w)
        v = y + odd * (1 - 2 * y)
        kvh = wl * 2 + v
        is_pair = here_own & (i == 0)
        slot = jnp.where(is_pair, 4, kvh)

        @pl.when((i == 3) | ((i == 1) & away))
        def _():
            q_arrive(kvh, 0)
            q_arrive(kvh, 1)

        cols = pl.ds(pl.multiple_of(kvh * 128, 128), 128)

        def prefix(p, q):
            out = []
            for s in range(2):
                keys = pk[s, pidx_ref[p], :, cols]
                ok = iota((128, 384), 0) + (at(z, y, s) * 128) < plen_ref[p]
                out.append(jnp.where(ok, dot_t(keys, q), NEG))
            return out, [vtp[kvh, p, :, s * 128 : s * 128 + 128] for s in range(2)]

        p = 1 - my
        num, top, tot = softmax(*prefix(p, queries(slot, p)))
        own[i, p] = num.astype(jnp.bfloat16)
        own_st[i, p] = stat_block(top, tot)
        q = queries(slot, my)
        scores, values = prefix(my, q)
        for n in range(4):
            scores.append(dot_t(tk[n // 2, n % 2, :, cols], q) + bias[n])
            values.append(vtt[kvh, n])
        num, top, tot = softmax(scores, values)
        own[i, my] = num.astype(jnp.bfloat16)
        own_st[i, my] = stat_block(top, tot)
        return carry

    def y_send(n):
        for p in range(2):
            ahead.push(own.at[2 * n + 1, p], yin.at[n, p], yrecv.at[n, p, 0], over)
            ahead.push(own_st.at[2 * n + 1, p], yin_st.at[n, p], yrecv.at[n, p, 1], over)

    lax.fori_loop(0, 1, attend, 0)
    relay(near_w * 2 + 1 - y, here_own, [(at(jnp.where(middle(z), third_z, near_z), y, c), here_own)])
    relay(far_slot, jnp.logical_not(inner_away), [(over, (away & outer(z)) | (here_own & middle(z)))])
    lax.fori_loop(1, 4, attend, 0)
    y_send(1)
    y_send(0)
    merge(1)
    merge(0)

    for sends in (ga.sends, exchange, pair):
        sends.finish()

    remote(kvx.at[1 - c], kvx.at[1 - c], qsend.at[0], qrecv.at[5, 1 - c, 0], core).wait_recv()
    rows = pl.ds(pl.multiple_of(c * 48, 16), 48)
    lo, hi = kvx[0, rows, :].astype(jnp.float32), kvx[1, rows, :].astype(jnp.float32)
    left = iota((48, HEAD_DIM), 1) < HEAD_DIM // 2
    key = jnp.where(left, lo, pltpu.roll(hi, HEAD_DIM // 2, 1))
    value = jnp.where(left, pltpu.roll(lo, HEAD_DIM // 2, 1), hi)
    key = rotate(key, tables[0, rows, :], tables[1, rows, :]).astype(jnp.bfloat16)
    value_t = dot_t(eye, value.astype(jnp.bfloat16)).astype(jnp.bfloat16)
    score = dot_t(key, queries(4, c)) + fm[...]
    f_num, f_top, f_tot = softmax([score], [value_t])

    for k in range(4):
        w = (z + k) % 4

        def landed():
            remote(zin.at[w], zin.at[w], zsend.at[0], zrecv.at[w, 0], core).wait_recv()
            remote(zin_st.at[w], zin_st.at[w], zsend.at[0], zrecv.at[w, 1], core).wait_recv()

        if k:
            landed()
        else:
            pl.when(jnp.logical_not(here_own))(landed)
    stats = [stats_of(zin_st[k]) for k in range(4)]
    top = f_top
    for t_, _ in stats:
        top = jnp.maximum(top, t_)
    e = jnp.exp2((f_top - top) * K2)
    num, tot = f_num * e, f_tot * e
    for k in range(4):
        e = jnp.exp2((stats[k][0] - top) * K2)
        num = num + zin[k].astype(jnp.float32) * e
        tot = tot + stats[k][1] * e
    att_t = (num / tot).astype(jnp.bfloat16)
    eye384 = one_hot(iota((384, 384), 0) == iota((384, 384), 1))
    att = dot_t(eye384, att_t).astype(jnp.bfloat16)
    for h in range(8):
        fatt[h // 4, me, :, h % 4 * HEAD_DIM : (h % 4 + 1) * HEAD_DIM] = att[h * 48 : h * 48 + 48]

    out_load.wait()
    halves = range(fatt.shape[0])
    gf = Gather([fatt.at[n] for n in halves], fsend, frecv)
    for n in halves:
        gf.start(n)
    ahead.finish()
    back.finish()
    depth = fatt.shape[3]
    result = [None]

    def use(n, w, v):
        k = ((w * 2 + v) * 2 + n) * depth
        term = dot(
            jnp.concatenate([fatt[n, at(w, v, 0)], fatt[n, at(w, v, 1)]], 0),
            wo[pl.ds(pl.multiple_of(k, depth), depth), :],
        )
        result[0] = term if result[0] is None else result[0] + term

    planes = gf.planes()
    for n in halves:
        gf.hop(n, 0)
        gf.hop(n, 1)
    for n in halves:
        gf.cross(n, z)
        for w in planes[:2]:
            gf.other(n, w, y)
            use(n, w, y)
    for n in halves:
        gf.hop(n, 2)
    for w in planes[1:]:
        for n in halves:
            gf.cross(n, w)
    for w in planes[2:]:
        for n in halves:
            gf.other(n, w, y)
            use(n, w, y)
    for w in planes:
        for n in halves:
            gf.other(n, w, 1 - y)
            use(n, w, 1 - y)
    done = result[0].astype(jnp.bfloat16)
    for p in range(2):
        for t in range(STEPS):
            out_ref[t * 32 + p * 16 : t * 32 + p * 16 + 16, :] = done[p * 48 + t * 16 : p * 48 + t * 16 + 16]
    gf.sends.finish()


PARTS = 2


def layer(args, scale, devices):
    vmem = pl.BlockSpec(memory_space=pltpu.VMEM)
    hbm = pl.BlockSpec(memory_space=pltpu.HBM)
    bf = lambda *shape: pltpu.VMEM(shape, jnp.bfloat16)
    fl = lambda *shape: pltpu.VMEM(shape, jnp.float32)
    dma = lambda *shape: pltpu.SemaphoreType.DMA(shape)
    width = args[2].shape[0]
    cols = args[2].shape[1]
    return pl.pallas_call(
        lambda *refs: layer_kernel(scale, *refs),
        out_shape=jax.ShapeDtypeStruct((96, cols), jnp.bfloat16),
        in_specs=[hbm] * 17,
        out_specs=vmem,
        scratch_shapes=[
            pltpu.SMEM((2,), jnp.int32), pltpu.SMEM((2,), jnp.int32), pltpu.SMEM((32,), jnp.int32),
            bf(STEPS, 2, width), fl(1, width), pltpu.VMEM((STEPS, 32), jnp.int32), pltpu.VMEM((1, 32), jnp.int32),
            fl(1, HEAD_DIM), fl(1, cols), fl(2, 64), dma(10),
            bf(PARTS, devices, 8, width * 3 // 4 // PARTS), fl(8, width), bf(96, width),
            bf(width, cols), bf(128, width), bf(width, cols), fl(96, cols), fl(96, 128),
            bf(5, 2, 4, 96, 128), bf(2, 96, 128),
            bf(2, 4, 128, 512), bf(2, 4, 128, 512), bf(2, 2, 256, 512), bf(2, 2, 256, 512),
            bf(4, 2, 128, 256), bf(4, 4, 128, 256), fl(32, 384), fl(48, 384), fl(4, 256, 384), fl(2, 96, 128),
            bf(4, 2, 128, 384), fl(4, 2, 8, 128), bf(2, 2, 128, 384), fl(2, 2, 8, 128),
            bf(2, 2, 128, 384), fl(2, 2, 8, 128), bf(4, 128, 384), fl(4, 8, 128), bf(2, devices, 48, 512),
            dma(19 * PARTS), dma(PARTS, devices), dma(4), dma(4, 2), dma(8), dma(4, 2),
            dma(31), dma(6, 2, 2), dma(8), dma(2, 2, 2), dma(8), dma(4, 2), dma(38), dma(2, devices),
        ],
        compiler_params=pltpu.CompilerParams(
            collective_id=0, has_side_effects=True, vmem_limit_bytes=60 * 2**20
        ),
    )(*args)


def local(
    hidden,
    norm_gain,
    q_weight,
    q_bias,
    kv_weight,
    kv_bias,
    o_weight,
    prefix_key_cache,
    prefix_value_cache,
    prefix_index,
    prefix_lens,
    tail_key_cache,
    tail_value_cache,
    tail_lens,
    parents,
):
    devices = lax.axis_size("beam")
    rpc = hidden.shape[1]
    width = hidden.shape[2]
    fits = (
        devices == 16 and rpc == 2 and hidden.shape[0] == STEPS and width == 8192 and q_weight.shape[1] == 512
        and kv_weight.shape[2] == 64 and prefix_index.shape[0] == 2 and prefix_key_cache.shape == (4, 128, 1024)
        and tail_key_cache.shape[1] == 256
    )
    if not fits:
        return local_by_rows(
            hidden, norm_gain, q_weight, q_bias, kv_weight, kv_bias, o_weight, prefix_key_cache,
            prefix_value_cache, prefix_index, prefix_lens, tail_key_cache, tail_value_cache, tail_lens, parents,
        )
    half = np.power(ROPE_BASE, -np.arange(HEAD_DIM // 2) * 2.0 / HEAD_DIM)
    freqs = jnp.asarray(np.concatenate([half, half])[None, :], jnp.float32)
    out = layer(
        (
            hidden, norm_gain[None, :], q_weight, q_bias[None, :],
            jnp.transpose(kv_weight, (1, 2, 0)).reshape(128, width), kv_bias, o_weight,
            prefix_key_cache, prefix_value_cache, tail_key_cache, tail_value_cache,
            prefix_index, prefix_lens, tail_lens, tail_lens[None, :], parents, freqs,
        ),
        1.0 / math.sqrt(HEAD_DIM), devices,
    )
    return out.reshape(STEPS, 32, out.shape[1])


def solution(mesh):
    return jax.shard_map(
        local,
        mesh=mesh,
        in_specs=(
            P(None, ("grp", "beam"), None),
            P(),
            P(None, "beam"),
            P("beam"),
            P(None, None, "beam"),
            P(None, "beam"),
            P(None, "beam"),
            P("grp", "beam", None),
            P("grp", "beam", None),
            P("grp"),
            P("grp"),
            P(("grp", "beam"), None, None),
            P(("grp", "beam"), None, None),
            P("grp"),
            P(None, "grp"),
        ),
        out_specs=P(None, "grp", "beam"),
        check_vma=False,
    )
```

```python
import math

import jax
import jax.numpy as jnp
import numpy as np
from jax import lax
from jax.experimental import pallas as pl
from jax.experimental.pallas import tpu as pltpu
from jax.sharding import PartitionSpec as P

QUERY_HEADS = 64
KEY_HEADS = 8
HEAD_DIM = 128
BEAM_COUNT = 16
STEPS = 3


EPS = 1e-06
NEG = -1e30
ROPE_BASE = 1000000.0


def rope_parts(positions, head_size):
    half = head_size // 2
    freqs = np.power(ROPE_BASE, -np.arange(half) * 2.0 / head_size)
    angle = positions.astype(jnp.float32)[:, None] * jnp.asarray(freqs, jnp.float32)[None, :]
    return (jnp.cos(angle), jnp.sin(angle))


def apply_rotation(value_rows, cosine_table, sine_table):
    half = value_rows.shape[-1] // 2
    first = value_rows[..., :half]
    second = value_rows[..., half:]
    cosine_table = cosine_table[:, None, :]
    sine_table = sine_table[:, None, :]
    return jnp.concatenate(
        [first * cosine_table - second * sine_table, second * cosine_table + first * sine_table],
        axis=-1,
    )


def local_by_rows(
    hidden,
    norm_gain,
    q_weight,
    q_bias,
    kv_weight,
    kv_bias,
    o_weight,
    prefix_key_cache,
    prefix_value_cache,
    prefix_index,
    prefix_lens,
    tail_key_cache,
    tail_value_cache,
    tail_lens,
    parents,
):
    devices = lax.axis_size("beam")
    me = lax.axis_index("beam")
    rows_per_chip = hidden.shape[1]
    width = hidden.shape[2]
    all_rows = rows_per_chip * devices
    prompt_batch = all_rows // BEAM_COUNT
    head_group = QUERY_HEADS // KEY_HEADS
    q_width = QUERY_HEADS * HEAD_DIM
    q_cols = q_weight.shape[1]
    kv_cols = kv_weight.shape[2]
    prefix_slice = prefix_key_cache.shape[1]
    tail_cache = tail_key_cache.shape[1]
    score_scale = 1.0 / math.sqrt(HEAD_DIM)
    row_ids = jnp.arange(all_rows, dtype=jnp.int32)
    prompt_of = row_ids // BEAM_COUNT
    first_row = me * rows_per_chip
    my_prompt = first_row // BEAM_COUNT
    slot_ids = first_row + jnp.arange(rows_per_chip, dtype=jnp.int32)
    mine = (jnp.arange(prompt_batch, dtype=jnp.int32) == my_prompt)[:, None, None, None]
    joint = jnp.concatenate([q_weight, kv_weight.reshape(width, 2 * kv_cols)], axis=1)
    joint_bias = jnp.concatenate([q_bias, kv_bias.reshape(2 * kv_cols)])
    shared = lambda cache: jnp.stack(
        [lax.dynamic_index_in_dim(cache, prefix_index[p], 0, keepdims=False) for p in range(prompt_batch)], 0
    ).reshape(prompt_batch, prefix_slice, KEY_HEADS, HEAD_DIM)
    slice_keys = shared(prefix_key_cache)
    slice_values = shared(prefix_value_cache)
    slab_ok = (me * prefix_slice + jnp.arange(prefix_slice, dtype=jnp.int32))[
        None, :
    ] < prefix_lens[:, None]
    slab_ok = slab_ok[:, None, None, None, :]
    tail_key_rows = tail_key_cache.reshape(rows_per_chip, tail_cache, KEY_HEADS, HEAD_DIM)
    tail_value_rows = tail_value_cache.reshape(rows_per_chip, tail_cache, KEY_HEADS, HEAD_DIM)
    own_lens = lax.dynamic_slice_in_dim(tail_lens, first_row, rows_per_chip, 0)
    tail_ok = jnp.arange(tail_cache, dtype=jnp.int32)[None, :] < own_lens[:, None]
    ancestors = row_ids
    makers = []
    fresh_keys = []
    current_values = []
    results = []
    for step in range(STEPS):
        chosen = parents[step]
        ancestors = ancestors[chosen]
        makers = [item[chosen] for item in makers] + [row_ids]
        value_rows = lax.all_gather(hidden[step], "beam", axis=0, tiled=True).astype(jnp.float32)
        normed = (
            value_rows
            * lax.rsqrt(jnp.mean(value_rows * value_rows, axis=-1, keepdims=True) + EPS)
            * norm_gain
        ).astype(jnp.bfloat16)
        projected = jnp.dot(normed, joint, preferred_element_type=jnp.float32) + joint_bias
        q_part = projected[:, :q_cols].astype(jnp.bfloat16)
        kv_part = projected[:, q_cols:].astype(jnp.bfloat16).reshape(all_rows, 2, kv_cols)
        positions = prefix_lens[prompt_of] + tail_lens[ancestors] + step
        cosine_table, sine_table = rope_parts(positions, HEAD_DIM)
        q_full, kv_full = (
            lax.all_gather(q_part[:, None, :], "beam", axis=2, tiled=True),
            lax.all_gather(kv_part, "beam", axis=2, tiled=True),
        )
        q_all = q_full[:, 0, :]
        owned_key_value = lax.dynamic_slice_in_dim(kv_full, first_row, rows_per_chip, 0)
        rotated_rows = apply_rotation(
            q_all.astype(jnp.float32).reshape(all_rows, QUERY_HEADS, HEAD_DIM),
            cosine_table,
            sine_table,
        ).astype(jnp.bfloat16)
        local_cosine = lax.dynamic_slice_in_dim(cosine_table, first_row, rows_per_chip, 0)
        local_sine = lax.dynamic_slice_in_dim(sine_table, first_row, rows_per_chip, 0)
        new_key = apply_rotation(
            owned_key_value[:, 0].astype(jnp.float32).reshape(rows_per_chip, KEY_HEADS, HEAD_DIM),
            local_cosine,
            local_sine,
        ).astype(jnp.bfloat16)
        fresh_keys.append(new_key)
        current_values.append(owned_key_value[:, 1].reshape(rows_per_chip, KEY_HEADS, HEAD_DIM))
        query_rows = rotated_rows.reshape(prompt_batch, BEAM_COUNT, KEY_HEADS, head_group, HEAD_DIM)
        pre_scores = (
            jnp.einsum(
                "pbkgd,pskd->pbkgs", query_rows, slice_keys, preferred_element_type=jnp.float32
            )
            * score_scale
        )
        pre_scores = jnp.where(slab_ok, pre_scores, NEG)
        local_q = lax.dynamic_index_in_dim(query_rows, my_prompt, 0, keepdims=False)
        local_anc = lax.dynamic_slice_in_dim(ancestors, my_prompt * BEAM_COUNT, BEAM_COUNT, 0)
        t_scores = (
            jnp.einsum(
                "bkgd,itkd->bkgit", local_q, tail_key_rows, preferred_element_type=jnp.float32
            )
            * score_scale
        )
        t_valid = (local_anc[:, None] == slot_ids[None, :])[:, None, None, :, None] & tail_ok[
            None, None, None, :, :
        ]
        t_scores = jnp.where(t_valid, t_scores, NEG)
        f_keys = jnp.stack(fresh_keys, 0)
        f_values = jnp.stack(current_values, 0)
        local_made = jnp.stack(
            [
                lax.dynamic_slice_in_dim(item, my_prompt * BEAM_COUNT, BEAM_COUNT, 0)
                for item in makers
            ],
            1,
        )
        f_valid = (local_made[:, :, None] == slot_ids[None, None, :])[:, None, None, :, :]
        f_scores = (
            jnp.einsum("bkgd,jikd->bkgji", local_q, f_keys, preferred_element_type=jnp.float32)
            * score_scale
        )
        f_scores = jnp.where(f_valid, f_scores, NEG)
        local_max = jnp.maximum(t_scores.max(axis=(3, 4)), f_scores.max(axis=(3, 4)))
        pre_max = pre_scores.max(-1)
        group_maximum = jnp.where(mine, jnp.maximum(pre_max, local_max[None]), pre_max)
        mine_max = lax.dynamic_index_in_dim(group_maximum, my_prompt, 0, keepdims=False)
        pre_w = jnp.where(slab_ok, jnp.exp(pre_scores - group_maximum[..., None]), 0.0)
        totals = pre_w.sum(-1)
        numer = jnp.einsum(
            "pbkgs,pskd->pbkgd",
            pre_w.astype(jnp.bfloat16),
            slice_values,
            preferred_element_type=jnp.float32,
        )
        t_w = jnp.where(t_valid, jnp.exp(t_scores - mine_max[..., None, None]), 0.0)
        f_w = jnp.where(f_valid, jnp.exp(f_scores - mine_max[..., None, None]), 0.0)
        local_total = t_w.sum(axis=(3, 4)) + f_w.sum(axis=(3, 4))
        local_num = jnp.einsum(
            "bkgit,itkd->bkgd",
            t_w.astype(jnp.bfloat16),
            tail_value_rows,
            preferred_element_type=jnp.float32,
        )
        local_num = local_num + jnp.einsum(
            "bkgji,jikd->bkgd",
            f_w.astype(jnp.bfloat16),
            f_values,
            preferred_element_type=jnp.float32,
        )
        totals = jnp.where(mine, totals + local_total[None], totals)
        numer = jnp.where(mine[..., None], numer + local_num[None], numer)
        sending = numer.astype(jnp.bfloat16).reshape(devices, rows_per_chip, q_width)
        parts = lax.all_to_all(sending, "beam", split_axis=0, concat_axis=0, tiled=True)
        maxima, sums = (
            lax.all_to_all(
                group_maximum.reshape(devices, rows_per_chip, QUERY_HEADS),
                "beam",
                split_axis=0,
                concat_axis=0,
                tiled=True,
            ),
            lax.all_to_all(
                totals.reshape(devices, rows_per_chip, QUERY_HEADS),
                "beam",
                split_axis=0,
                concat_axis=0,
                tiled=True,
            ),
        )
        top = maxima.max(0)
        factors = jnp.exp(maxima - top[None])
        denom = (factors * sums).sum(0)
        combined = jnp.einsum(
            "srh,srhd->rhd",
            factors,
            parts.reshape(devices, rows_per_chip, QUERY_HEADS, HEAD_DIM),
            preferred_element_type=jnp.float32,
        )
        attention = (
            (combined / denom[..., None]).reshape(rows_per_chip, q_width).astype(jnp.bfloat16)
        )
        out_cols = jnp.dot(
            lax.all_gather(attention, "beam", axis=0, tiled=True),
            o_weight,
            preferred_element_type=jnp.float32,
        )
        results.append(out_cols.astype(jnp.bfloat16))
    return jnp.stack(results, 0)


MESH = pl.DeviceIdType.MESH
CONTRACT_LAST = (((1,), (1,)), ((), ()))
LOW = -1e29


def place():
    me = lax.axis_index("beam")
    return me, me // 4, me // 2 % 2, me % 2


def at(z, y, c):
    return (z * 2 + y) * 2 + c


def line(z):
    return [z + 1 - 2 * (z % 2), 3 - z, (z + 2) % 4]


def middle(z):
    return (z + 1) // 2 == 1


def outer(z):
    return (z + 1) // 2 != 1


def remote(src, dst, send, recv, target):
    return pltpu.make_async_remote_copy(
        src_ref=src, dst_ref=dst, send_sem=send, recv_sem=recv,
        device_id={"beam": target}, device_id_type=MESH,
    )


class Sends:
    def __init__(self, send):
        self.send, self.sent = send, []

    def push(self, src, dst, recv, target, only=None):
        copy = remote(src, dst, self.send.at[len(self.sent)], recv, target)
        if only is None:
            copy.start()
        else:
            pl.when(only)(copy.start)
        self.sent.append((copy, only))

    def finish(self):
        for copy, only in self.sent:
            if only is None:
                copy.wait_send()
            else:
                pl.when(only)(copy.wait_send)


class Gather:
    def __init__(self, parts, send, recv):
        self.parts, self.recv = parts, recv
        self.sends = Sends(send)
        self.me, self.z, self.y, self.c = place()

    def push(self, part, shard, target, only=None):
        ref = self.parts[part].at[shard]
        self.sends.push(ref, ref, self.recv.at[part, shard], target, only)

    def arrive(self, part, shard):
        ref = self.parts[part].at[shard]
        remote(ref, ref, self.sends.send.at[0], self.recv.at[part, shard], at(self.z, self.y, 1 - self.c)).wait_recv()

    def start(self, part):
        z, y, c = self.z, self.y, self.c
        self.push(part, self.me, at(line(z)[0], y, c))
        self.push(part, self.me, at(3 - z, y, c))
        self.push(part, self.me, at(z, 1 - y, c))
        self.push(part, self.me, at(z, y, 1 - c))

    def hop(self, part, k):
        z, y, c = self.z, self.y, self.c
        shard = at(line(z)[k], y, c)
        self.arrive(part, shard)
        if k < 2:
            self.push(part, shard, at(line(z)[1 - k], y, c), middle(z))
        self.push(part, shard, at(z, 1 - y, c))
        self.push(part, shard, at(z, y, 1 - c))

    def planes(self):
        return [self.z] + line(self.z)

    def cross(self, part, w):
        shard = at(w, 1 - self.y, self.c)
        self.arrive(part, shard)
        self.push(part, shard, at(self.z, self.y, 1 - self.c))

    def other(self, part, w, v):
        self.arrive(part, at(w, v, 1 - self.c))


def one_hot(mask):
    return jnp.where(mask, 1.0, 0.0).astype(jnp.bfloat16)


def iota(shape, axis):
    return lax.broadcasted_iota(jnp.int32, shape, axis)


def dot(a, b):
    return jnp.dot(a, b, preferred_element_type=jnp.float32)


def dot_t(a, b):
    return lax.dot_general(a, b, CONTRACT_LAST, preferred_element_type=jnp.float32)


def layer_kernel(
    scale,
    x_hbm, gain_hbm, wq_hbm, qb_hbm, wkv_hbm, kvb_hbm, wo_hbm, pk_hbm, pv_hbm, tk_hbm, tv_hbm,
    pidx_hbm, plen_hbm, tlens_hbm, tlen_hbm, par_hbm, freq_hbm,
    out_ref,
    pidx_ref, plen_ref, tlen_ref,
    x_ref, gain_ref, par_ref, tlen_row_ref, freq_ref, qb_ref, kvb_ref, ssem,
    full, nrm, lhs, wq, wkv, wo, qacc, kvacc, qs, kvx, pk, pv, tk, tv, vtp, vtt, atl, fm, bias, tables,
    own, own_st, yin, yin_st, mg, mg_st, zin, zin_st, fatt,
    asend, arecv, wsem, lsem, xsend, xrecv, qsend, qrecv, ysend, yrecv, zsend, zrecv, fsend, frecv,
):
    me, z, y, c = place()
    core, over = at(z, y, 1 - c), at(z, 1 - y, c)
    parts = full.shape[0]
    width = lhs.shape[1] // parts
    keep = width * 3 // 4
    tail_w = width // 4
    K2 = scale * math.log2(math.e)
    my = z // 2

    smalls = []
    for src, dst in (
        (x_hbm, x_ref), (gain_hbm, gain_ref), (par_hbm, par_ref), (tlen_hbm, tlen_row_ref), (freq_hbm, freq_ref),
        (qb_hbm, qb_ref), (kvb_hbm, kvb_ref), (pidx_hbm, pidx_ref), (plen_hbm, plen_ref), (tlens_hbm, tlen_ref),
    ):
        smalls.append(pltpu.make_async_copy(src, dst, ssem.at[len(smalls)]))
        smalls[-1].start()
    barrier = pltpu.get_barrier_semaphore()
    partners = [at((z + k) % 4, y, p) for k in range(1, 4) for p in range(2)]
    partners += [core, over, at(z, 1 - y, 1 - c)]
    for other in partners:
        pl.semaphore_signal(barrier, inc=1, device_id={"beam": other}, device_id_type=MESH)
    smalls[0].wait()
    smalls[1].wait()

    total = None
    for t in range(STEPS):
        xt = x_ref[t].astype(jnp.float32)
        ms = jnp.mean(xt * xt, axis=-1, keepdims=True)
        nrm[2 * t : 2 * t + 2, :] = xt * lax.rsqrt(ms + EPS) * gain_ref[...]
    for q in range(parts):
        base = q * width
        rest = nrm[0:6, base + keep : base + width]
        rows67 = [
            jnp.concatenate([rest[3 * h + j : 3 * h + j + 1] for j in range(3)], 1) for h in range(2)
        ]
        block = jnp.concatenate([nrm[0:6, base : base + keep]] + rows67, 0)
        full[q, me] = block.astype(jnp.bfloat16)

    pl.semaphore_wait(barrier, len(partners))

    ga = Gather([full.at[q] for q in range(parts)], asend, arecv)
    for q in range(parts):
        ga.start(q)

    half = wq_hbm.shape[0] // 2
    loads = []
    for src, dst in (
        (wq_hbm.at[0:half], wq.at[0:half]),
        (wkv_hbm, wkv),
        (wq_hbm.at[half : 2 * half], wq.at[half : 2 * half]),
    ):
        loads.append(pltpu.make_async_copy(src, dst, wsem.at[len(loads)]))
        loads[-1].start()
    cache_loads = []
    exchange = Sends(xsend)
    for n, (src, dst) in enumerate(((pk_hbm, pk), (pv_hbm, pv), (tk_hbm, tk), (tv_hbm, tv))):
        for wl in range(2):
            cols = slice(wl * 256, wl * 256 + 256)
            mine = pl.ds(pl.multiple_of(wl * 512 + c * 256, 256), 256)
            theirs = pl.ds(pl.multiple_of(wl * 512 + (1 - c) * 256, 256), 256)
            lead = (slice(None),) * (len(src.shape) - 1)
            cache_loads.append(
                pltpu.make_async_copy(src.at[lead + (mine,)], dst.at[(c,) + lead + (cols,)], lsem.at[n, wl])
            )
            cache_loads[-1].start()
            exchange.push(src.at[lead + (theirs,)], dst.at[(c,) + lead + (cols,)], xrecv.at[n, wl], core)
    out_load = pltpu.make_async_copy(wo_hbm, wo, wsem.at[3])
    out_load.start()

    for copy in smalls[2:]:
        copy.wait()
    eye32 = one_hot(iota((32, 32), 0) == iota((32, 32), 1))
    step = [one_hot(iota((32, 32), 0) == par_ref[t : t + 1, :]) for t in range(STEPS)]
    m20 = dot(step[1], step[2]).astype(jnp.bfloat16)
    made = {(0, 0): eye32, (1, 1): eye32, (2, 2): eye32, (1, 0): step[1], (2, 1): step[2], (2, 0): m20}
    anc = [step[0], dot(step[0], step[1]).astype(jnp.bfloat16), dot(step[0], m20).astype(jnp.bfloat16)]
    rho = iota((96, 32), 0)
    prompt = jnp.where(rho >= 48, 1, 0)
    when = lax.shift_right_logical(rho - 48 * prompt, 4)
    row = prompt * 16 + (rho & 15)
    lines = None
    for t in range(STEPS):
        sel = one_hot((when == t) & (row == iota((96, 32), 1)))
        term = dot_t(sel, anc[t])
        lines = term if lines is None else lines + term
    lens = jnp.sum(lines * tlen_row_ref[...].astype(jnp.float32), axis=1, keepdims=True)
    col = iota((96, 1), 0)
    second = col >= 48
    turn = lax.shift_right_logical(col - 48 * jnp.where(second, 1, 0), 4)
    pos = lens + jnp.where(second, plen_ref[1], plen_ref[0]).astype(jnp.float32) + turn.astype(jnp.float32)
    angle = pos * freq_ref[...]
    tables[0] = jnp.cos(angle)
    sine = jnp.sin(angle)
    tables[1] = jnp.where(iota((96, HEAD_DIM), 1) < HEAD_DIM // 2, -sine, sine)
    lane = iota((32, 384), 1)
    sixteen = lax.shift_right_logical(lane, 4)
    lane_step = sixteen - 3 * lax.shift_right_logical(sixteen * 11, 5)
    lane_beam = lane & 15
    pick = lambda p: [
        one_hot((lane_step == t) & (iota((32, 384), 0) == p * 16 + lane_beam)) for t in range(STEPS)
    ]
    here = pick(my)
    atl[...] = dot(anc[0], here[0]) + dot(anc[1], here[1]) + dot(anc[2], here[2])
    dest = pick(c)
    key_row = iota((48, 32), 0)
    fresh = None
    for j in range(STEPS):
        reach = None
        for t in range(j, STEPS):
            term = dot(made[t, j], dest[t])
            reach = term if reach is None else reach + term
        sel = one_hot(
            (lax.shift_right_logical(key_row, 4) == j) & (iota((48, 32), 1) == c * 16 + (key_row & 15))
        )
        term = dot(sel, reach.astype(jnp.bfloat16))
        fresh = term if fresh is None else fresh + term
    fm[...] = jnp.where(fresh > 0.5, 0.0, NEG)

    def tail_bias(i):
        a = (z * 2 + y) * 4 + i
        on = atl[pl.ds(a, 1), :] > 0.5
        ok = iota((256, 384), 0) < tlen_ref[a]
        bias[i] = jnp.where(on & ok, 0.0, NEG)

    for q in range(parts):
        ga.hop(q, 0)
        ga.hop(q, 1)
    tail_bias(0)
    tail_bias(1)
    for q in range(parts):
        ga.hop(q, 2)
    tail_bias(2)
    tail_bias(3)
    for w in ga.planes():
        for q in range(parts):
            ga.cross(q, w)

    for copy in cache_loads:
        copy.wait()
    for copy, _ in exchange.sent:
        copy.wait_recv()
    eye = one_hot(iota((128, 128), 0) == iota((128, 128), 1))

    def turn_values(kvh, carry):
        cols = pl.ds(pl.multiple_of(kvh * 128, 128), 128)
        for p in range(2):
            for s in range(2):
                vtp[kvh, p, :, s * 128 : s * 128 + 128] = dot_t(eye, pv[s, pidx_ref[p], :, cols]).astype(jnp.bfloat16)
        for i in range(4):
            vtt[kvh, i] = dot_t(eye, tv[i // 2, i % 2, :, cols]).astype(jnp.bfloat16)
        return carry

    lax.fori_loop(0, 4, turn_values, 0)

    pr = iota((96, 128), 0)
    pp = jnp.where(pr >= 48, 1, 0)
    local_row = 2 * lax.shift_right_logical(pr - 48 * pp, 4) + (pr & 1)
    shard_row = (pp * 8 + lax.shift_right_logical(pr & 15, 1)) * 8
    high = jnp.where(local_row >= 3, 1, 0)
    source = iota((96, 128), 1)
    first = one_hot(source == shard_row + local_row)
    thirds = [one_hot((source == shard_row + 6 + high) & (local_row - 3 * high == j)) for j in range(3)]
    qacc[...] = jnp.zeros_like(qacc)
    kvacc[...] = jnp.zeros_like(kvacc)
    block = min(2048, width)
    for q in range(parts):
        for w in ga.planes():
            for v in (y, 1 - y):
                ga.other(q, w, v)
        tails = None
        for j in range(3):
            got = full[q, :, :, j * tail_w : (j + 1) * tail_w].reshape(128, tail_w)
            both = dot(jnp.concatenate([first, thirds[j]], 0), got)
            lhs[:, q * width + j * tail_w : q * width + (j + 1) * tail_w] = both[:96].astype(jnp.bfloat16)
            tails = both[96:] if tails is None else tails + both[96:]
        lhs[:, q * width + keep : (q + 1) * width] = tails.astype(jnp.bfloat16)
        if q == 0:
            for copy in loads:
                copy.wait()

        def project(k, carry):
            ks = pl.ds(pl.multiple_of(q * width + k * block, block), block)
            a = lhs[:, ks]
            qacc[...] += dot(a, wq[ks, :])
            kvacc[...] += dot_t(a, wkv[:, ks])
            return carry

        lax.fori_loop(0, width // block, project, 0)

    cosine, signed = tables[0], tables[1]

    def rotate(v, co, si):
        return v * co + pltpu.roll(v, HEAD_DIM // 2, 1) * si

    kvx[c] = (kvacc[...] + jnp.concatenate([kvb_ref[0:1], kvb_ref[1:2]], 1)).astype(jnp.bfloat16)
    pair = Sends(qsend)
    pair.push(kvx.at[c], kvx.at[c], qrecv.at[5, c, 0], core)
    heads = qs.shape[2]
    for h in range(heads):
        cols = slice(h * HEAD_DIM, (h + 1) * HEAD_DIM)
        v = (qacc[:, cols] + qb_ref[:, cols]).astype(jnp.bfloat16).astype(jnp.float32)
        qs[4, c, h] = rotate(v, cosine, signed).astype(jnp.bfloat16)

    target = z % 2
    mine_slot = (z // 2) * 2 + y
    here_own = target == c
    near_w = z // 2
    near_z, facing_z, third_z = line(z)

    def piece(slot, half_, n):
        return qs.at[slot, half_, 2 * n : 2 * n + 2]

    for n in range(2):
        def give(slot, to, only=None):
            pair.push(piece(4, c, n), piece(slot, c, n), qrecv.at[slot, c, n], to, only)

        give(mine_slot, at(near_z, y, target))
        give(4, core)
        give(mine_slot, at(z, 1 - y, target))
        give(mine_slot, at(third_z, y, target), outer(z))
        give(mine_slot, at(facing_z, y, target))

    def q_landed(slot, half_, n):
        ref = piece(slot, half_, n)
        remote(ref, ref, qsend.at[0], qrecv.at[slot, half_, n], core).wait_recv()

    def q_arrive(slot, half_):
        for n in range(2):
            q_landed(slot, half_, n)

    def relay(slot, only, targets):
        for n in range(2):
            for half_ in range(2):
                pl.when(only)(lambda: q_landed(slot, half_, n))
                for to, go in targets:
                    ref = piece(slot, half_, n)
                    pair.push(ref, ref, qrecv.at[slot, half_, n], to, go)

    near_slot = near_w * 2 + y
    far_slot = (1 - near_w) * 2 + y
    away = jnp.logical_not(here_own)
    inner_away = away & middle(z)
    relay(near_slot, away, [(over, away & outer(z))])
    relay(far_slot, inner_away, [(at(near_z, y, c), inner_away), (over, inner_away)])
    q_arrive(4, 1 - c)

    def stat_block(top, total):
        rid = iota((8, 128), 0)
        out = jnp.zeros((8, 128), jnp.float32)
        for n in range(3):
            out = jnp.where(rid == n, top[:, n * 128 : n * 128 + 128], out)
            out = jnp.where(rid == 4 + n, total[:, n * 128 : n * 128 + 128], out)
        return out

    def stats_of(st):
        return (
            jnp.concatenate([st[0:1], st[1:2], st[2:3]], 1),
            jnp.concatenate([st[4:5], st[5:6], st[6:7]], 1),
        )

    def softmax(scores, values):
        top = None
        for s in scores:
            m = jnp.max(s, axis=0, keepdims=True)
            top = m if top is None else jnp.maximum(top, m)
        safe = jnp.maximum(top, LOW)
        num = total = None
        for s, v in zip(scores, values):
            e = jnp.exp2((s - safe) * K2)
            part = jnp.sum(e, axis=0, keepdims=True)
            term = dot(v, e.astype(jnp.bfloat16))
            num = term if num is None else num + term
            total = part if total is None else total + part
        return num, top, total

    def queries(slot, p):
        start = pl.ds(pl.multiple_of(p * 48, 16), 48)
        return qs[slot, :, :, start, :].reshape(384, HEAD_DIM)

    ahead = Sends(ysend)
    back = Sends(zsend)

    cuts = [slice(n * 64, n * 64 + 64) for n in range(2)]

    def merge(n):
        w = c + 2 * (near_w if n == 0 else 1 - near_w)
        for p in range(2):
            stay = (w == z) & (c == p)
            go = jnp.logical_not(stay)
            to = jnp.where(stay, core, at(w, y, p))
            ref = yin_st.at[n, p]
            remote(ref, ref, ysend.at[0], yrecv.at[n, p, 2], over).wait_recv()
            ta, sa = stats_of(own_st[2 * n, p])
            tb, sb = stats_of(yin_st[n, p])
            top = jnp.maximum(ta, tb)
            ea, eb = jnp.exp2((ta - top) * K2), jnp.exp2((tb - top) * K2)
            mg_st[n, p] = stat_block(top, sa * ea + sb * eb)
            back.push(mg_st.at[n, p], zin_st.at[z], zrecv.at[z, 2], to, go)
            for h, cut in enumerate(cuts):
                ref = yin.at[n, p, cut]
                remote(ref, ref, ysend.at[0], yrecv.at[n, p, h], over).wait_recv()
                a, b = own[2 * n, p, cut].astype(jnp.float32), yin[n, p, cut].astype(jnp.float32)
                mg[n, p, cut] = (a * ea + b * eb).astype(jnp.bfloat16)
                back.push(mg.at[n, p, cut], zin.at[z, cut], zrecv.at[z, h], to, go)

            @pl.when(stay)
            def _():
                zin[z] = mg[n, p]
                zin_st[z] = mg_st[n, p]

    def attend(i, carry):
        odd = i % 2
        late = i // 2
        wl = near_w + late * (1 - 2 * near_w)
        v = y + odd * (1 - 2 * y)
        kvh = wl * 2 + v
        is_pair = here_own & (i == 0)
        slot = jnp.where(is_pair, 4, kvh)

        @pl.when((i == 3) | ((i == 1) & away))
        def _():
            q_arrive(kvh, 0)
            q_arrive(kvh, 1)

        cols = pl.ds(pl.multiple_of(kvh * 128, 128), 128)

        def prefix(p, q):
            out = []
            for s in range(2):
                keys = pk[s, pidx_ref[p], :, cols]
                ok = iota((128, 384), 0) + (at(z, y, s) * 128) < plen_ref[p]
                out.append(jnp.where(ok, dot_t(keys, q), NEG))
            return out, [vtp[kvh, p, :, s * 128 : s * 128 + 128] for s in range(2)]

        p = 1 - my
        num, top, tot = softmax(*prefix(p, queries(slot, p)))
        own[i, p] = num.astype(jnp.bfloat16)
        own_st[i, p] = stat_block(top, tot)
        q = queries(slot, my)
        scores, values = prefix(my, q)
        for n in range(4):
            scores.append(dot_t(tk[n // 2, n % 2, :, cols], q) + bias[n])
            values.append(vtt[kvh, n])
        num, top, tot = softmax(scores, values)
        own[i, my] = num.astype(jnp.bfloat16)
        own_st[i, my] = stat_block(top, tot)
        return carry

    def y_send(n):
        for p in range(2):
            ahead.push(own_st.at[2 * n + 1, p], yin_st.at[n, p], yrecv.at[n, p, 2], over)
            for h, cut in enumerate(cuts):
                ahead.push(own.at[2 * n + 1, p, cut], yin.at[n, p, cut], yrecv.at[n, p, h], over)

    lax.fori_loop(0, 1, attend, 0)
    relay(near_w * 2 + 1 - y, here_own, [(at(jnp.where(middle(z), third_z, near_z), y, c), here_own)])
    relay(far_slot, jnp.logical_not(inner_away), [(over, (away & outer(z)) | (here_own & middle(z)))])
    lax.fori_loop(1, 4, attend, 0)
    y_send(1)
    y_send(0)
    merge(1)
    merge(0)

    for sends in (ga.sends, exchange, pair):
        sends.finish()

    remote(kvx.at[1 - c], kvx.at[1 - c], qsend.at[0], qrecv.at[5, 1 - c, 0], core).wait_recv()
    rows = pl.ds(pl.multiple_of(c * 48, 16), 48)
    lo, hi = kvx[0, rows, :].astype(jnp.float32), kvx[1, rows, :].astype(jnp.float32)
    left = iota((48, HEAD_DIM), 1) < HEAD_DIM // 2
    key = jnp.where(left, lo, pltpu.roll(hi, HEAD_DIM // 2, 1))
    value = jnp.where(left, pltpu.roll(lo, HEAD_DIM // 2, 1), hi)
    key = rotate(key, tables[0, rows, :], tables[1, rows, :]).astype(jnp.bfloat16)
    value_t = dot_t(eye, value.astype(jnp.bfloat16)).astype(jnp.bfloat16)
    score = dot_t(key, queries(4, c)) + fm[...]
    f_num, f_top, f_tot = softmax([score], [value_t])

    for k in range(4):
        w = (z + k) % 4

        def landed():
            for h, cut in enumerate(cuts):
                ref = zin.at[w, cut]
                remote(ref, ref, zsend.at[0], zrecv.at[w, h], core).wait_recv()
            remote(zin_st.at[w], zin_st.at[w], zsend.at[0], zrecv.at[w, 2], core).wait_recv()

        if k:
            landed()
        else:
            pl.when(jnp.logical_not(here_own))(landed)
    stats = [stats_of(zin_st[k]) for k in range(4)]
    top = f_top
    for t_, _ in stats:
        top = jnp.maximum(top, t_)
    e = jnp.exp2((f_top - top) * K2)
    num, tot = f_num * e, f_tot * e
    for k in range(4):
        e = jnp.exp2((stats[k][0] - top) * K2)
        num = num + zin[k].astype(jnp.float32) * e
        tot = tot + stats[k][1] * e
    att_t = (num / tot).astype(jnp.bfloat16)
    eye384 = one_hot(iota((384, 384), 0) == iota((384, 384), 1))
    att = dot_t(eye384, att_t).astype(jnp.bfloat16)
    for h in range(8):
        fatt[h // 4, me, :, h % 4 * HEAD_DIM : (h % 4 + 1) * HEAD_DIM] = att[h * 48 : h * 48 + 48]

    out_load.wait()
    halves = range(fatt.shape[0])
    gf = Gather([fatt.at[n] for n in halves], fsend, frecv)
    for n in halves:
        gf.start(n)
    ahead.finish()
    back.finish()
    depth = fatt.shape[3]
    result = [None]

    def use(n, w, v):
        k = ((w * 2 + v) * 2 + n) * depth
        term = dot(
            jnp.concatenate([fatt[n, at(w, v, 0)], fatt[n, at(w, v, 1)]], 0),
            wo[pl.ds(pl.multiple_of(k, depth), depth), :],
        )
        result[0] = term if result[0] is None else result[0] + term

    planes = gf.planes()
    for n in halves:
        gf.hop(n, 0)
        gf.hop(n, 1)
    for n in halves:
        gf.cross(n, z)
        for w in planes[:2]:
            gf.other(n, w, y)
            use(n, w, y)
    for n in halves:
        gf.hop(n, 2)
    for w in planes[1:]:
        for n in halves:
            gf.cross(n, w)
    for w in planes[2:]:
        for n in halves:
            gf.other(n, w, y)
            use(n, w, y)
    for w in planes:
        for n in halves:
            gf.other(n, w, 1 - y)
            use(n, w, 1 - y)
    done = result[0].astype(jnp.bfloat16)
    for p in range(2):
        for t in range(STEPS):
            out_ref[t * 32 + p * 16 : t * 32 + p * 16 + 16, :] = done[p * 48 + t * 16 : p * 48 + t * 16 + 16]
    gf.sends.finish()


PARTS = 4


def layer(args, scale, devices):
    vmem = pl.BlockSpec(memory_space=pltpu.VMEM)
    hbm = pl.BlockSpec(memory_space=pltpu.HBM)
    bf = lambda *shape: pltpu.VMEM(shape, jnp.bfloat16)
    fl = lambda *shape: pltpu.VMEM(shape, jnp.float32)
    dma = lambda *shape: pltpu.SemaphoreType.DMA(shape)
    width = args[2].shape[0]
    cols = args[2].shape[1]
    return pl.pallas_call(
        lambda *refs: layer_kernel(scale, *refs),
        out_shape=jax.ShapeDtypeStruct((96, cols), jnp.bfloat16),
        in_specs=[hbm] * 17,
        out_specs=vmem,
        scratch_shapes=[
            pltpu.SMEM((2,), jnp.int32), pltpu.SMEM((2,), jnp.int32), pltpu.SMEM((32,), jnp.int32),
            bf(STEPS, 2, width), fl(1, width), pltpu.VMEM((STEPS, 32), jnp.int32), pltpu.VMEM((1, 32), jnp.int32),
            fl(1, HEAD_DIM), fl(1, cols), fl(2, 64), dma(10),
            bf(PARTS, devices, 8, width * 3 // 4 // PARTS), fl(8, width), bf(96, width),
            bf(width, cols), bf(128, width), bf(width, cols), fl(96, cols), fl(96, 128),
            bf(5, 2, 4, 96, 128), bf(2, 96, 128),
            bf(2, 4, 128, 512), bf(2, 4, 128, 512), bf(2, 2, 256, 512), bf(2, 2, 256, 512),
            bf(4, 2, 128, 256), bf(4, 4, 128, 256), fl(32, 384), fl(48, 384), fl(4, 256, 384), fl(2, 96, 128),
            bf(4, 2, 128, 384), fl(4, 2, 8, 128), bf(2, 2, 128, 384), fl(2, 2, 8, 128),
            bf(2, 2, 128, 384), fl(2, 2, 8, 128), bf(4, 128, 384), fl(4, 8, 128), bf(2, devices, 48, 512),
            dma(19 * PARTS), dma(PARTS, devices), dma(4), dma(4, 2), dma(8), dma(4, 2),
            dma(31), dma(6, 2, 2), dma(12), dma(2, 2, 3), dma(12), dma(4, 3), dma(38), dma(2, devices),
        ],
        compiler_params=pltpu.CompilerParams(
            collective_id=0, has_side_effects=True, vmem_limit_bytes=60 * 2**20
        ),
    )(*args)


def local(
    hidden,
    norm_gain,
    q_weight,
    q_bias,
    kv_weight,
    kv_bias,
    o_weight,
    prefix_key_cache,
    prefix_value_cache,
    prefix_index,
    prefix_lens,
    tail_key_cache,
    tail_value_cache,
    tail_lens,
    parents,
):
    devices = lax.axis_size("beam")
    rpc = hidden.shape[1]
    width = hidden.shape[2]
    fits = (
        devices == 16 and rpc == 2 and hidden.shape[0] == STEPS and width == 8192 and q_weight.shape[1] == 512
        and kv_weight.shape[2] == 64 and prefix_index.shape[0] == 2 and prefix_key_cache.shape == (4, 128, 1024)
        and tail_key_cache.shape[1] == 256
    )
    if not fits:
        return local_by_rows(
            hidden, norm_gain, q_weight, q_bias, kv_weight, kv_bias, o_weight, prefix_key_cache,
            prefix_value_cache, prefix_index, prefix_lens, tail_key_cache, tail_value_cache, tail_lens, parents,
        )
    half = np.power(ROPE_BASE, -np.arange(HEAD_DIM // 2) * 2.0 / HEAD_DIM)
    freqs = jnp.asarray(np.concatenate([half, half])[None, :], jnp.float32)
    out = layer(
        (
            hidden, norm_gain[None, :], q_weight, q_bias[None, :],
            jnp.transpose(kv_weight, (1, 2, 0)).reshape(128, width), kv_bias, o_weight,
            prefix_key_cache, prefix_value_cache, tail_key_cache, tail_value_cache,
            prefix_index, prefix_lens, tail_lens, tail_lens[None, :], parents, freqs,
        ),
        1.0 / math.sqrt(HEAD_DIM), devices,
    )
    return out.reshape(STEPS, 32, out.shape[1])


def solution(mesh):
    return jax.shard_map(
        local,
        mesh=mesh,
        in_specs=(
            P(None, ("grp", "beam"), None),
            P(),
            P(None, "beam"),
            P("beam"),
            P(None, None, "beam"),
            P(None, "beam"),
            P(None, "beam"),
            P("grp", "beam", None),
            P("grp", "beam", None),
            P("grp"),
            P("grp"),
            P(("grp", "beam"), None, None),
            P(("grp", "beam"), None, None),
            P("grp"),
            P(None, "grp"),
        ),
        out_specs=P(None, "grp", "beam"),
        check_vma=False,
    )
```

```python
import math

import jax
import jax.numpy as jnp
import numpy as np
from jax import lax
from jax.experimental import pallas as pl
from jax.experimental.pallas import tpu as pltpu
from jax.sharding import PartitionSpec as P

QUERY_HEADS = 64
KEY_HEADS = 8
HEAD_DIM = 128
BEAM_COUNT = 16
STEPS = 3


EPS = 1e-06
NEG = -1e30
ROPE_BASE = 1000000.0


def rope_parts(positions, head_size):
    half = head_size // 2
    freqs = np.power(ROPE_BASE, -np.arange(half) * 2.0 / head_size)
    angle = positions.astype(jnp.float32)[:, None] * jnp.asarray(freqs, jnp.float32)[None, :]
    return (jnp.cos(angle), jnp.sin(angle))


def apply_rotation(value_rows, cosine_table, sine_table):
    half = value_rows.shape[-1] // 2
    first = value_rows[..., :half]
    second = value_rows[..., half:]
    cosine_table = cosine_table[:, None, :]
    sine_table = sine_table[:, None, :]
    return jnp.concatenate(
        [first * cosine_table - second * sine_table, second * cosine_table + first * sine_table],
        axis=-1,
    )


def local_by_rows(
    hidden,
    norm_gain,
    q_weight,
    q_bias,
    kv_weight,
    kv_bias,
    o_weight,
    prefix_key_cache,
    prefix_value_cache,
    prefix_index,
    prefix_lens,
    tail_key_cache,
    tail_value_cache,
    tail_lens,
    parents,
):
    devices = lax.axis_size("beam")
    me = lax.axis_index("beam")
    rows_per_chip = hidden.shape[1]
    width = hidden.shape[2]
    all_rows = rows_per_chip * devices
    prompt_batch = all_rows // BEAM_COUNT
    head_group = QUERY_HEADS // KEY_HEADS
    q_width = QUERY_HEADS * HEAD_DIM
    q_cols = q_weight.shape[1]
    kv_cols = kv_weight.shape[2]
    prefix_slice = prefix_key_cache.shape[1]
    tail_cache = tail_key_cache.shape[1]
    score_scale = 1.0 / math.sqrt(HEAD_DIM)
    row_ids = jnp.arange(all_rows, dtype=jnp.int32)
    prompt_of = row_ids // BEAM_COUNT
    first_row = me * rows_per_chip
    my_prompt = first_row // BEAM_COUNT
    slot_ids = first_row + jnp.arange(rows_per_chip, dtype=jnp.int32)
    mine = (jnp.arange(prompt_batch, dtype=jnp.int32) == my_prompt)[:, None, None, None]
    joint = jnp.concatenate([q_weight, kv_weight.reshape(width, 2 * kv_cols)], axis=1)
    joint_bias = jnp.concatenate([q_bias, kv_bias.reshape(2 * kv_cols)])
    shared = lambda cache: jnp.stack(
        [lax.dynamic_index_in_dim(cache, prefix_index[p], 0, keepdims=False) for p in range(prompt_batch)], 0
    ).reshape(prompt_batch, prefix_slice, KEY_HEADS, HEAD_DIM)
    slice_keys = shared(prefix_key_cache)
    slice_values = shared(prefix_value_cache)
    slab_ok = (me * prefix_slice + jnp.arange(prefix_slice, dtype=jnp.int32))[
        None, :
    ] < prefix_lens[:, None]
    slab_ok = slab_ok[:, None, None, None, :]
    tail_key_rows = tail_key_cache.reshape(rows_per_chip, tail_cache, KEY_HEADS, HEAD_DIM)
    tail_value_rows = tail_value_cache.reshape(rows_per_chip, tail_cache, KEY_HEADS, HEAD_DIM)
    own_lens = lax.dynamic_slice_in_dim(tail_lens, first_row, rows_per_chip, 0)
    tail_ok = jnp.arange(tail_cache, dtype=jnp.int32)[None, :] < own_lens[:, None]
    ancestors = row_ids
    makers = []
    fresh_keys = []
    current_values = []
    results = []
    for step in range(STEPS):
        chosen = parents[step]
        ancestors = ancestors[chosen]
        makers = [item[chosen] for item in makers] + [row_ids]
        value_rows = lax.all_gather(hidden[step], "beam", axis=0, tiled=True).astype(jnp.float32)
        normed = (
            value_rows
            * lax.rsqrt(jnp.mean(value_rows * value_rows, axis=-1, keepdims=True) + EPS)
            * norm_gain
        ).astype(jnp.bfloat16)
        projected = jnp.dot(normed, joint, preferred_element_type=jnp.float32) + joint_bias
        q_part = projected[:, :q_cols].astype(jnp.bfloat16)
        kv_part = projected[:, q_cols:].astype(jnp.bfloat16).reshape(all_rows, 2, kv_cols)
        positions = prefix_lens[prompt_of] + tail_lens[ancestors] + step
        cosine_table, sine_table = rope_parts(positions, HEAD_DIM)
        q_full, kv_full = (
            lax.all_gather(q_part[:, None, :], "beam", axis=2, tiled=True),
            lax.all_gather(kv_part, "beam", axis=2, tiled=True),
        )
        q_all = q_full[:, 0, :]
        owned_key_value = lax.dynamic_slice_in_dim(kv_full, first_row, rows_per_chip, 0)
        rotated_rows = apply_rotation(
            q_all.astype(jnp.float32).reshape(all_rows, QUERY_HEADS, HEAD_DIM),
            cosine_table,
            sine_table,
        ).astype(jnp.bfloat16)
        local_cosine = lax.dynamic_slice_in_dim(cosine_table, first_row, rows_per_chip, 0)
        local_sine = lax.dynamic_slice_in_dim(sine_table, first_row, rows_per_chip, 0)
        new_key = apply_rotation(
            owned_key_value[:, 0].astype(jnp.float32).reshape(rows_per_chip, KEY_HEADS, HEAD_DIM),
            local_cosine,
            local_sine,
        ).astype(jnp.bfloat16)
        fresh_keys.append(new_key)
        current_values.append(owned_key_value[:, 1].reshape(rows_per_chip, KEY_HEADS, HEAD_DIM))
        query_rows = rotated_rows.reshape(prompt_batch, BEAM_COUNT, KEY_HEADS, head_group, HEAD_DIM)
        pre_scores = (
            jnp.einsum(
                "pbkgd,pskd->pbkgs", query_rows, slice_keys, preferred_element_type=jnp.float32
            )
            * score_scale
        )
        pre_scores = jnp.where(slab_ok, pre_scores, NEG)
        local_q = lax.dynamic_index_in_dim(query_rows, my_prompt, 0, keepdims=False)
        local_anc = lax.dynamic_slice_in_dim(ancestors, my_prompt * BEAM_COUNT, BEAM_COUNT, 0)
        t_scores = (
            jnp.einsum(
                "bkgd,itkd->bkgit", local_q, tail_key_rows, preferred_element_type=jnp.float32
            )
            * score_scale
        )
        t_valid = (local_anc[:, None] == slot_ids[None, :])[:, None, None, :, None] & tail_ok[
            None, None, None, :, :
        ]
        t_scores = jnp.where(t_valid, t_scores, NEG)
        f_keys = jnp.stack(fresh_keys, 0)
        f_values = jnp.stack(current_values, 0)
        local_made = jnp.stack(
            [
                lax.dynamic_slice_in_dim(item, my_prompt * BEAM_COUNT, BEAM_COUNT, 0)
                for item in makers
            ],
            1,
        )
        f_valid = (local_made[:, :, None] == slot_ids[None, None, :])[:, None, None, :, :]
        f_scores = (
            jnp.einsum("bkgd,jikd->bkgji", local_q, f_keys, preferred_element_type=jnp.float32)
            * score_scale
        )
        f_scores = jnp.where(f_valid, f_scores, NEG)
        local_max = jnp.maximum(t_scores.max(axis=(3, 4)), f_scores.max(axis=(3, 4)))
        pre_max = pre_scores.max(-1)
        group_maximum = jnp.where(mine, jnp.maximum(pre_max, local_max[None]), pre_max)
        mine_max = lax.dynamic_index_in_dim(group_maximum, my_prompt, 0, keepdims=False)
        pre_w = jnp.where(slab_ok, jnp.exp(pre_scores - group_maximum[..., None]), 0.0)
        totals = pre_w.sum(-1)
        numer = jnp.einsum(
            "pbkgs,pskd->pbkgd",
            pre_w.astype(jnp.bfloat16),
            slice_values,
            preferred_element_type=jnp.float32,
        )
        t_w = jnp.where(t_valid, jnp.exp(t_scores - mine_max[..., None, None]), 0.0)
        f_w = jnp.where(f_valid, jnp.exp(f_scores - mine_max[..., None, None]), 0.0)
        local_total = t_w.sum(axis=(3, 4)) + f_w.sum(axis=(3, 4))
        local_num = jnp.einsum(
            "bkgit,itkd->bkgd",
            t_w.astype(jnp.bfloat16),
            tail_value_rows,
            preferred_element_type=jnp.float32,
        )
        local_num = local_num + jnp.einsum(
            "bkgji,jikd->bkgd",
            f_w.astype(jnp.bfloat16),
            f_values,
            preferred_element_type=jnp.float32,
        )
        totals = jnp.where(mine, totals + local_total[None], totals)
        numer = jnp.where(mine[..., None], numer + local_num[None], numer)
        sending = numer.astype(jnp.bfloat16).reshape(devices, rows_per_chip, q_width)
        parts = lax.all_to_all(sending, "beam", split_axis=0, concat_axis=0, tiled=True)
        maxima, sums = (
            lax.all_to_all(
                group_maximum.reshape(devices, rows_per_chip, QUERY_HEADS),
                "beam",
                split_axis=0,
                concat_axis=0,
                tiled=True,
            ),
            lax.all_to_all(
                totals.reshape(devices, rows_per_chip, QUERY_HEADS),
                "beam",
                split_axis=0,
                concat_axis=0,
                tiled=True,
            ),
        )
        top = maxima.max(0)
        factors = jnp.exp(maxima - top[None])
        denom = (factors * sums).sum(0)
        combined = jnp.einsum(
            "srh,srhd->rhd",
            factors,
            parts.reshape(devices, rows_per_chip, QUERY_HEADS, HEAD_DIM),
            preferred_element_type=jnp.float32,
        )
        attention = (
            (combined / denom[..., None]).reshape(rows_per_chip, q_width).astype(jnp.bfloat16)
        )
        out_cols = jnp.dot(
            lax.all_gather(attention, "beam", axis=0, tiled=True),
            o_weight,
            preferred_element_type=jnp.float32,
        )
        results.append(out_cols.astype(jnp.bfloat16))
    return jnp.stack(results, 0)


MESH = pl.DeviceIdType.MESH
CONTRACT_LAST = (((1,), (1,)), ((), ()))
LOW = -1e29


def place():
    me = lax.axis_index("beam")
    return me, me // 4, me // 2 % 2, me % 2


def at(z, y, c):
    return (z * 2 + y) * 2 + c


def line(z):
    return [z + 1 - 2 * (z % 2), 3 - z, (z + 2) % 4]


def middle(z):
    return (z + 1) // 2 == 1


def outer(z):
    return (z + 1) // 2 != 1


def remote(src, dst, send, recv, target):
    return pltpu.make_async_remote_copy(
        src_ref=src, dst_ref=dst, send_sem=send, recv_sem=recv,
        device_id={"beam": target}, device_id_type=MESH,
    )


class Sends:
    def __init__(self, send):
        self.send, self.sent = send, []

    def push(self, src, dst, recv, target, only=None):
        copy = remote(src, dst, self.send.at[len(self.sent)], recv, target)
        if only is None:
            copy.start()
        else:
            pl.when(only)(copy.start)
        self.sent.append((copy, only))

    def finish(self):
        for copy, only in self.sent:
            if only is None:
                copy.wait_send()
            else:
                pl.when(only)(copy.wait_send)


class Gather:
    def __init__(self, parts, send, recv):
        self.parts, self.recv = parts, recv
        self.sends = Sends(send)
        self.me, self.z, self.y, self.c = place()

    def push(self, part, shard, target, only=None):
        ref = self.parts[part].at[shard]
        self.sends.push(ref, ref, self.recv.at[part, shard], target, only)

    def arrive(self, part, shard):
        ref = self.parts[part].at[shard]
        remote(ref, ref, self.sends.send.at[0], self.recv.at[part, shard], at(self.z, self.y, 1 - self.c)).wait_recv()

    def start(self, part):
        z, y, c = self.z, self.y, self.c
        self.push(part, self.me, at(line(z)[0], y, c))
        self.push(part, self.me, at(3 - z, y, c))
        self.push(part, self.me, at(z, 1 - y, c))
        self.push(part, self.me, at(z, y, 1 - c))

    def hop(self, part, k):
        z, y, c = self.z, self.y, self.c
        shard = at(line(z)[k], y, c)
        self.arrive(part, shard)
        if k < 2:
            self.push(part, shard, at(line(z)[1 - k], y, c), middle(z))
        self.push(part, shard, at(z, 1 - y, c))
        self.push(part, shard, at(z, y, 1 - c))

    def planes(self):
        return [self.z] + line(self.z)

    def cross(self, part, w):
        shard = at(w, 1 - self.y, self.c)
        self.arrive(part, shard)
        self.push(part, shard, at(self.z, self.y, 1 - self.c))

    def other(self, part, w, v):
        self.arrive(part, at(w, v, 1 - self.c))


def one_hot(mask):
    return jnp.where(mask, 1.0, 0.0).astype(jnp.bfloat16)


def iota(shape, axis):
    return lax.broadcasted_iota(jnp.int32, shape, axis)


def dot(a, b):
    return jnp.dot(a, b, preferred_element_type=jnp.float32)


def dot_t(a, b):
    return lax.dot_general(a, b, CONTRACT_LAST, preferred_element_type=jnp.float32)


def layer_kernel(
    scale,
    x_hbm, gain_hbm, wq_hbm, qb_hbm, wkv_hbm, kvb_hbm, wo_hbm, pk_hbm, pv_hbm, tk_hbm, tv_hbm,
    pidx_hbm, plen_hbm, tlens_hbm, tlen_hbm, par_hbm, freq_hbm,
    out_ref,
    pidx_ref, plen_ref, tlen_ref,
    x_ref, gain_ref, par_ref, tlen_row_ref, freq_ref, qb_ref, kvb_ref, ssem,
    full, nrm, lhs, wq, wkv, wo, qacc, kvacc, qs, kvx, pk, pv, tk, tv, vtp, vtt, atl, fm, bias, tables,
    own, own_st, yin, yin_st, mg, mg_st, zin, zin_st, fatt,
    asend, arecv, wsem, lsem, xsend, xrecv, qsend, qrecv, ysend, yrecv, zsend, zrecv, fsend, frecv,
):
    me, z, y, c = place()
    core, over = at(z, y, 1 - c), at(z, 1 - y, c)
    parts = full.shape[0]
    width = lhs.shape[1] // parts
    keep = width * 3 // 4
    tail_w = width // 4
    K2 = scale * math.log2(math.e)
    my = z // 2

    smalls = []
    for src, dst in (
        (x_hbm, x_ref), (gain_hbm, gain_ref), (par_hbm, par_ref), (tlen_hbm, tlen_row_ref), (freq_hbm, freq_ref),
        (qb_hbm, qb_ref), (kvb_hbm, kvb_ref), (pidx_hbm, pidx_ref), (plen_hbm, plen_ref), (tlens_hbm, tlen_ref),
    ):
        smalls.append(pltpu.make_async_copy(src, dst, ssem.at[len(smalls)]))
        smalls[-1].start()
    barrier = pltpu.get_barrier_semaphore()
    partners = [at((z + k) % 4, y, p) for k in range(1, 4) for p in range(2)]
    partners += [core, over, at(z, 1 - y, 1 - c)]
    for other in partners:
        pl.semaphore_signal(barrier, inc=1, device_id={"beam": other}, device_id_type=MESH)
    smalls[0].wait()
    smalls[1].wait()

    total = None
    for t in range(STEPS):
        xt = x_ref[t].astype(jnp.float32)
        ms = jnp.mean(xt * xt, axis=-1, keepdims=True)
        nrm[2 * t : 2 * t + 2, :] = xt * lax.rsqrt(ms + EPS) * gain_ref[...]
    for q in range(parts):
        base = q * width
        rest = nrm[0:6, base + keep : base + width]
        rows67 = [
            jnp.concatenate([rest[3 * h + j : 3 * h + j + 1] for j in range(3)], 1) for h in range(2)
        ]
        block = jnp.concatenate([nrm[0:6, base : base + keep]] + rows67, 0)
        full[q, me] = block.astype(jnp.bfloat16)

    pl.semaphore_wait(barrier, len(partners))

    ga = Gather([full.at[q] for q in range(parts)], asend, arecv)
    for q in range(parts):
        ga.start(q)

    half = wq_hbm.shape[0] // 2
    loads = []
    for src, dst in (
        (wq_hbm.at[0:half], wq.at[0:half]),
        (wkv_hbm, wkv),
        (wq_hbm.at[half : 2 * half], wq.at[half : 2 * half]),
    ):
        loads.append(pltpu.make_async_copy(src, dst, wsem.at[len(loads)]))
        loads[-1].start()
    cache_loads = []
    exchange = Sends(xsend)
    for n, (src, dst) in enumerate(((pk_hbm, pk), (pv_hbm, pv), (tk_hbm, tk), (tv_hbm, tv))):
        for wl in range(2):
            cols = slice(wl * 256, wl * 256 + 256)
            mine = pl.ds(pl.multiple_of(wl * 512 + c * 256, 256), 256)
            theirs = pl.ds(pl.multiple_of(wl * 512 + (1 - c) * 256, 256), 256)
            lead = (slice(None),) * (len(src.shape) - 1)
            cache_loads.append(
                pltpu.make_async_copy(src.at[lead + (mine,)], dst.at[(c,) + lead + (cols,)], lsem.at[n, wl])
            )
            cache_loads[-1].start()
            exchange.push(src.at[lead + (theirs,)], dst.at[(c,) + lead + (cols,)], xrecv.at[n, wl], core)
    out_load = pltpu.make_async_copy(wo_hbm, wo, wsem.at[3])
    out_load.start()

    for copy in smalls[2:]:
        copy.wait()
    eye32 = one_hot(iota((32, 32), 0) == iota((32, 32), 1))
    step = [one_hot(iota((32, 32), 0) == par_ref[t : t + 1, :]) for t in range(STEPS)]
    m20 = dot(step[1], step[2]).astype(jnp.bfloat16)
    made = {(0, 0): eye32, (1, 1): eye32, (2, 2): eye32, (1, 0): step[1], (2, 1): step[2], (2, 0): m20}
    anc = [step[0], dot(step[0], step[1]).astype(jnp.bfloat16), dot(step[0], m20).astype(jnp.bfloat16)]
    rho = iota((96, 32), 0)
    prompt = jnp.where(rho >= 48, 1, 0)
    when = lax.shift_right_logical(rho - 48 * prompt, 4)
    row = prompt * 16 + (rho & 15)
    lines = None
    for t in range(STEPS):
        sel = one_hot((when == t) & (row == iota((96, 32), 1)))
        term = dot_t(sel, anc[t])
        lines = term if lines is None else lines + term
    lens = jnp.sum(lines * tlen_row_ref[...].astype(jnp.float32), axis=1, keepdims=True)
    col = iota((96, 1), 0)
    second = col >= 48
    turn = lax.shift_right_logical(col - 48 * jnp.where(second, 1, 0), 4)
    pos = lens + jnp.where(second, plen_ref[1], plen_ref[0]).astype(jnp.float32) + turn.astype(jnp.float32)
    angle = pos * freq_ref[...]
    tables[0] = jnp.cos(angle)
    sine = jnp.sin(angle)
    tables[1] = jnp.where(iota((96, HEAD_DIM), 1) < HEAD_DIM // 2, -sine, sine)
    lane = iota((32, 384), 1)
    sixteen = lax.shift_right_logical(lane, 4)
    lane_step = sixteen - 3 * lax.shift_right_logical(sixteen * 11, 5)
    lane_beam = lane & 15
    pick = lambda p: [
        one_hot((lane_step == t) & (iota((32, 384), 0) == p * 16 + lane_beam)) for t in range(STEPS)
    ]
    here = pick(my)
    atl[...] = dot(anc[0], here[0]) + dot(anc[1], here[1]) + dot(anc[2], here[2])
    dest = pick(c)
    key_row = iota((48, 32), 0)
    fresh = None
    for j in range(STEPS):
        reach = None
        for t in range(j, STEPS):
            term = dot(made[t, j], dest[t])
            reach = term if reach is None else reach + term
        sel = one_hot(
            (lax.shift_right_logical(key_row, 4) == j) & (iota((48, 32), 1) == c * 16 + (key_row & 15))
        )
        term = dot(sel, reach.astype(jnp.bfloat16))
        fresh = term if fresh is None else fresh + term
    fm[...] = jnp.where(fresh > 0.5, 0.0, NEG)

    def tail_bias(i):
        a = (z * 2 + y) * 4 + i
        on = atl[pl.ds(a, 1), :] > 0.5
        ok = iota((256, 384), 0) < tlen_ref[a]
        bias[i] = jnp.where(on & ok, 0.0, NEG)

    for q in range(parts):
        ga.hop(q, 0)
        ga.hop(q, 1)
    tail_bias(0)
    tail_bias(1)
    for q in range(parts):
        ga.hop(q, 2)
    tail_bias(2)
    tail_bias(3)
    for w in ga.planes():
        for q in range(parts):
            ga.cross(q, w)

    pr = iota((96, 128), 0)
    pp = jnp.where(pr >= 48, 1, 0)
    local_row = 2 * lax.shift_right_logical(pr - 48 * pp, 4) + (pr & 1)
    shard_row = (pp * 8 + lax.shift_right_logical(pr & 15, 1)) * 8
    high = jnp.where(local_row >= 3, 1, 0)
    source = iota((96, 128), 1)
    first = one_hot(source == shard_row + local_row)
    thirds = [one_hot((source == shard_row + 6 + high) & (local_row - 3 * high == j)) for j in range(3)]
    qacc[...] = jnp.zeros_like(qacc)
    kvacc[...] = jnp.zeros_like(kvacc)
    block = min(2048, width)
    for q in range(parts):
        for w in ga.planes():
            for v in (y, 1 - y):
                ga.other(q, w, v)
        tails = None
        for j in range(3):
            got = full[q, :, :, j * tail_w : (j + 1) * tail_w].reshape(128, tail_w)
            both = dot(jnp.concatenate([first, thirds[j]], 0), got)
            lhs[:, q * width + j * tail_w : q * width + (j + 1) * tail_w] = both[:96].astype(jnp.bfloat16)
            tails = both[96:] if tails is None else tails + both[96:]
        lhs[:, q * width + keep : (q + 1) * width] = tails.astype(jnp.bfloat16)
        if q == 0:
            for copy in loads:
                copy.wait()

        def project(k, carry):
            ks = pl.ds(pl.multiple_of(q * width + k * block, block), block)
            a = lhs[:, ks]
            qacc[...] += dot(a, wq[ks, :])
            return carry

        lax.fori_loop(0, width // block, project, 0)

    cosine, signed = tables[0], tables[1]

    def rotate(v, co, si):
        return v * co + pltpu.roll(v, HEAD_DIM // 2, 1) * si

    pair = Sends(qsend)
    target = z % 2
    mine_slot = (z // 2) * 2 + y
    here_own = target == c
    near_w = z // 2
    near_z, facing_z, third_z = line(z)

    def piece(slot, half_, n):
        return qs.at[slot, half_, 2 * n : 2 * n + 2]

    for n in range(2):
        for h in (2 * n, 2 * n + 1):
            cols = slice(h * HEAD_DIM, (h + 1) * HEAD_DIM)
            v = (qacc[:, cols] + qb_ref[:, cols]).astype(jnp.bfloat16).astype(jnp.float32)
            qs[4, c, h] = rotate(v, cosine, signed).astype(jnp.bfloat16)

        def give(slot, to, only=None):
            pair.push(piece(4, c, n), piece(slot, c, n), qrecv.at[slot, c, n], to, only)

        give(mine_slot, at(near_z, y, target))
        give(4, core)
        give(mine_slot, at(z, 1 - y, target))
        give(mine_slot, at(third_z, y, target), outer(z))
        give(mine_slot, at(facing_z, y, target))

    def project_keys(k, carry):
        ks = pl.ds(pl.multiple_of(k * 2048, 2048), 2048)
        kvacc[...] += dot_t(lhs[:, ks], wkv[:, ks])
        return carry

    lax.fori_loop(0, lhs.shape[1] // 2048, project_keys, 0)
    kvx[c] = (kvacc[...] + jnp.concatenate([kvb_ref[0:1], kvb_ref[1:2]], 1)).astype(jnp.bfloat16)
    pair.push(kvx.at[c], kvx.at[c], qrecv.at[5, c, 0], core)

    for copy in cache_loads:
        copy.wait()
    for copy, _ in exchange.sent:
        copy.wait_recv()
    eye = one_hot(iota((128, 128), 0) == iota((128, 128), 1))

    def turn_values(kvh, carry):
        cols = pl.ds(pl.multiple_of(kvh * 128, 128), 128)
        for p in range(2):
            for s in range(2):
                vtp[kvh, p, :, s * 128 : s * 128 + 128] = dot_t(eye, pv[s, pidx_ref[p], :, cols]).astype(jnp.bfloat16)
        for i in range(4):
            vtt[kvh, i] = dot_t(eye, tv[i // 2, i % 2, :, cols]).astype(jnp.bfloat16)
        return carry

    lax.fori_loop(0, 4, turn_values, 0)

    def q_landed(slot, half_, n):
        ref = piece(slot, half_, n)
        remote(ref, ref, qsend.at[0], qrecv.at[slot, half_, n], core).wait_recv()

    def q_arrive(slot, half_):
        for n in range(2):
            q_landed(slot, half_, n)

    def relay(slot, only, targets):
        for n in range(2):
            for half_ in range(2):
                pl.when(only)(lambda: q_landed(slot, half_, n))
                for to, go in targets:
                    ref = piece(slot, half_, n)
                    pair.push(ref, ref, qrecv.at[slot, half_, n], to, go)

    near_slot = near_w * 2 + y
    far_slot = (1 - near_w) * 2 + y
    away = jnp.logical_not(here_own)
    inner_away = away & middle(z)
    relay(near_slot, away, [(over, away & outer(z))])
    relay(far_slot, inner_away, [(at(near_z, y, c), inner_away), (over, inner_away)])
    q_arrive(4, 1 - c)

    def stat_block(top, total):
        rid = iota((8, 128), 0)
        out = jnp.zeros((8, 128), jnp.float32)
        for n in range(3):
            out = jnp.where(rid == n, top[:, n * 128 : n * 128 + 128], out)
            out = jnp.where(rid == 4 + n, total[:, n * 128 : n * 128 + 128], out)
        return out

    def stats_of(st):
        return (
            jnp.concatenate([st[0:1], st[1:2], st[2:3]], 1),
            jnp.concatenate([st[4:5], st[5:6], st[6:7]], 1),
        )

    def softmax(scores, values):
        top = None
        for s in scores:
            m = jnp.max(s, axis=0, keepdims=True)
            top = m if top is None else jnp.maximum(top, m)
        safe = jnp.maximum(top, LOW)
        num = total = None
        for s, v in zip(scores, values):
            e = jnp.exp2((s - safe) * K2)
            part = jnp.sum(e, axis=0, keepdims=True)
            term = dot(v, e.astype(jnp.bfloat16))
            num = term if num is None else num + term
            total = part if total is None else total + part
        return num, top, total

    def queries(slot, p):
        start = pl.ds(pl.multiple_of(p * 48, 16), 48)
        return qs[slot, :, :, start, :].reshape(384, HEAD_DIM)

    ahead = Sends(ysend)
    back = Sends(zsend)

    cuts = [slice(n * 64, n * 64 + 64) for n in range(2)]

    def merge(n):
        w = c + 2 * (near_w if n == 0 else 1 - near_w)
        for p in range(2):
            stay = (w == z) & (c == p)
            go = jnp.logical_not(stay)
            to = jnp.where(stay, core, at(w, y, p))
            ref = yin_st.at[n, p]
            remote(ref, ref, ysend.at[0], yrecv.at[n, p, 2], over).wait_recv()
            ta, sa = stats_of(own_st[2 * n, p])
            tb, sb = stats_of(yin_st[n, p])
            top = jnp.maximum(ta, tb)
            ea, eb = jnp.exp2((ta - top) * K2), jnp.exp2((tb - top) * K2)
            mg_st[n, p] = stat_block(top, sa * ea + sb * eb)
            back.push(mg_st.at[n, p], zin_st.at[z], zrecv.at[z, 2], to, go)
            for h, cut in enumerate(cuts):
                ref = yin.at[n, p, cut]
                remote(ref, ref, ysend.at[0], yrecv.at[n, p, h], over).wait_recv()
                a, b = own[2 * n, p, cut].astype(jnp.float32), yin[n, p, cut].astype(jnp.float32)
                mg[n, p, cut] = (a * ea + b * eb).astype(jnp.bfloat16)
                back.push(mg.at[n, p, cut], zin.at[z, cut], zrecv.at[z, h], to, go)

            @pl.when(stay)
            def _():
                zin[z] = mg[n, p]
                zin_st[z] = mg_st[n, p]

    def attend(i, carry):
        odd = i % 2
        late = i // 2
        wl = near_w + late * (1 - 2 * near_w)
        v = y + odd * (1 - 2 * y)
        kvh = wl * 2 + v
        is_pair = here_own & (i == 0)
        slot = jnp.where(is_pair, 4, kvh)

        @pl.when((i == 3) | ((i == 1) & away))
        def _():
            q_arrive(kvh, 0)
            q_arrive(kvh, 1)

        cols = pl.ds(pl.multiple_of(kvh * 128, 128), 128)

        def prefix(p, q):
            out = []
            for s in range(2):
                keys = pk[s, pidx_ref[p], :, cols]
                ok = iota((128, 384), 0) + (at(z, y, s) * 128) < plen_ref[p]
                out.append(jnp.where(ok, dot_t(keys, q), NEG))
            return out, [vtp[kvh, p, :, s * 128 : s * 128 + 128] for s in range(2)]

        p = 1 - my
        num, top, tot = softmax(*prefix(p, queries(slot, p)))
        own[i, p] = num.astype(jnp.bfloat16)
        own_st[i, p] = stat_block(top, tot)
        q = queries(slot, my)
        scores, values = prefix(my, q)
        for n in range(4):
            scores.append(dot_t(tk[n // 2, n % 2, :, cols], q) + bias[n])
            values.append(vtt[kvh, n])
        num, top, tot = softmax(scores, values)
        own[i, my] = num.astype(jnp.bfloat16)
        own_st[i, my] = stat_block(top, tot)
        return carry

    def y_send(n):
        for p in range(2):
            ahead.push(own_st.at[2 * n + 1, p], yin_st.at[n, p], yrecv.at[n, p, 2], over)
            for h, cut in enumerate(cuts):
                ahead.push(own.at[2 * n + 1, p, cut], yin.at[n, p, cut], yrecv.at[n, p, h], over)

    lax.fori_loop(0, 1, attend, 0)
    relay(near_w * 2 + 1 - y, here_own, [(at(jnp.where(middle(z), third_z, near_z), y, c), here_own)])
    relay(far_slot, jnp.logical_not(inner_away), [(over, (away & outer(z)) | (here_own & middle(z)))])
    lax.fori_loop(1, 4, attend, 0)
    y_send(1)
    y_send(0)
    merge(1)
    merge(0)

    for sends in (ga.sends, exchange, pair):
        sends.finish()

    remote(kvx.at[1 - c], kvx.at[1 - c], qsend.at[0], qrecv.at[5, 1 - c, 0], core).wait_recv()
    rows = pl.ds(pl.multiple_of(c * 48, 16), 48)
    lo, hi = kvx[0, rows, :].astype(jnp.float32), kvx[1, rows, :].astype(jnp.float32)
    left = iota((48, HEAD_DIM), 1) < HEAD_DIM // 2
    key = jnp.where(left, lo, pltpu.roll(hi, HEAD_DIM // 2, 1))
    value = jnp.where(left, pltpu.roll(lo, HEAD_DIM // 2, 1), hi)
    key = rotate(key, tables[0, rows, :], tables[1, rows, :]).astype(jnp.bfloat16)
    value_t = dot_t(eye, value.astype(jnp.bfloat16)).astype(jnp.bfloat16)
    score = dot_t(key, queries(4, c)) + fm[...]
    f_num, f_top, f_tot = softmax([score], [value_t])

    for k in range(4):
        w = (z + k) % 4

        def landed():
            for h, cut in enumerate(cuts):
                ref = zin.at[w, cut]
                remote(ref, ref, zsend.at[0], zrecv.at[w, h], core).wait_recv()
            remote(zin_st.at[w], zin_st.at[w], zsend.at[0], zrecv.at[w, 2], core).wait_recv()

        if k:
            landed()
        else:
            pl.when(jnp.logical_not(here_own))(landed)
    stats = [stats_of(zin_st[k]) for k in range(4)]
    top = f_top
    for t_, _ in stats:
        top = jnp.maximum(top, t_)
    e = jnp.exp2((f_top - top) * K2)
    num, tot = f_num * e, f_tot * e
    for k in range(4):
        e = jnp.exp2((stats[k][0] - top) * K2)
        num = num + zin[k].astype(jnp.float32) * e
        tot = tot + stats[k][1] * e
    att_t = (num / tot).astype(jnp.bfloat16)
    eye384 = one_hot(iota((384, 384), 0) == iota((384, 384), 1))
    att = dot_t(eye384, att_t).astype(jnp.bfloat16)
    for h in range(8):
        fatt[h // 4, me, :, h % 4 * HEAD_DIM : (h % 4 + 1) * HEAD_DIM] = att[h * 48 : h * 48 + 48]

    out_load.wait()
    halves = range(fatt.shape[0])
    gf = Gather([fatt.at[n] for n in halves], fsend, frecv)
    for n in halves:
        gf.start(n)
    ahead.finish()
    back.finish()
    depth = fatt.shape[3]
    result = [None]

    def use(n, w, v):
        k = ((w * 2 + v) * 2 + n) * depth
        term = dot(
            jnp.concatenate([fatt[n, at(w, v, 0)], fatt[n, at(w, v, 1)]], 0),
            wo[pl.ds(pl.multiple_of(k, depth), depth), :],
        )
        result[0] = term if result[0] is None else result[0] + term

    planes = gf.planes()
    for n in halves:
        gf.hop(n, 0)
        gf.hop(n, 1)
    for n in halves:
        gf.cross(n, z)
        for w in planes[:2]:
            gf.other(n, w, y)
            use(n, w, y)
    for n in halves:
        gf.hop(n, 2)
    for w in planes[1:]:
        for n in halves:
            gf.cross(n, w)
    for w in planes[2:]:
        for n in halves:
            gf.other(n, w, y)
            use(n, w, y)
    for w in planes:
        for n in halves:
            gf.other(n, w, 1 - y)
            use(n, w, 1 - y)
    done = result[0].astype(jnp.bfloat16)
    for p in range(2):
        for t in range(STEPS):
            out_ref[t * 32 + p * 16 : t * 32 + p * 16 + 16, :] = done[p * 48 + t * 16 : p * 48 + t * 16 + 16]
    gf.sends.finish()


PARTS = 4


def layer(args, scale, devices):
    vmem = pl.BlockSpec(memory_space=pltpu.VMEM)
    hbm = pl.BlockSpec(memory_space=pltpu.HBM)
    bf = lambda *shape: pltpu.VMEM(shape, jnp.bfloat16)
    fl = lambda *shape: pltpu.VMEM(shape, jnp.float32)
    dma = lambda *shape: pltpu.SemaphoreType.DMA(shape)
    width = args[2].shape[0]
    cols = args[2].shape[1]
    return pl.pallas_call(
        lambda *refs: layer_kernel(scale, *refs),
        out_shape=jax.ShapeDtypeStruct((96, cols), jnp.bfloat16),
        in_specs=[hbm] * 17,
        out_specs=vmem,
        scratch_shapes=[
            pltpu.SMEM((2,), jnp.int32), pltpu.SMEM((2,), jnp.int32), pltpu.SMEM((32,), jnp.int32),
            bf(STEPS, 2, width), fl(1, width), pltpu.VMEM((STEPS, 32), jnp.int32), pltpu.VMEM((1, 32), jnp.int32),
            fl(1, HEAD_DIM), fl(1, cols), fl(2, 64), dma(10),
            bf(PARTS, devices, 8, width * 3 // 4 // PARTS), fl(8, width), bf(96, width),
            bf(width, cols), bf(128, width), bf(width, cols), fl(96, cols), fl(96, 128),
            bf(5, 2, 4, 96, 128), bf(2, 96, 128),
            bf(2, 4, 128, 512), bf(2, 4, 128, 512), bf(2, 2, 256, 512), bf(2, 2, 256, 512),
            bf(4, 2, 128, 256), bf(4, 4, 128, 256), fl(32, 384), fl(48, 384), fl(4, 256, 384), fl(2, 96, 128),
            bf(4, 2, 128, 384), fl(4, 2, 8, 128), bf(2, 2, 128, 384), fl(2, 2, 8, 128),
            bf(2, 2, 128, 384), fl(2, 2, 8, 128), bf(4, 128, 384), fl(4, 8, 128), bf(2, devices, 48, 512),
            dma(19 * PARTS), dma(PARTS, devices), dma(4), dma(4, 2), dma(8), dma(4, 2),
            dma(31), dma(6, 2, 2), dma(12), dma(2, 2, 3), dma(12), dma(4, 3), dma(38), dma(2, devices),
        ],
        compiler_params=pltpu.CompilerParams(
            collective_id=0, has_side_effects=True, vmem_limit_bytes=60 * 2**20
        ),
    )(*args)


def local(
    hidden,
    norm_gain,
    q_weight,
    q_bias,
    kv_weight,
    kv_bias,
    o_weight,
    prefix_key_cache,
    prefix_value_cache,
    prefix_index,
    prefix_lens,
    tail_key_cache,
    tail_value_cache,
    tail_lens,
    parents,
):
    devices = lax.axis_size("beam")
    rpc = hidden.shape[1]
    width = hidden.shape[2]
    fits = (
        devices == 16 and rpc == 2 and hidden.shape[0] == STEPS and width == 8192 and q_weight.shape[1] == 512
        and kv_weight.shape[2] == 64 and prefix_index.shape[0] == 2 and prefix_key_cache.shape == (4, 128, 1024)
        and tail_key_cache.shape[1] == 256
    )
    if not fits:
        return local_by_rows(
            hidden, norm_gain, q_weight, q_bias, kv_weight, kv_bias, o_weight, prefix_key_cache,
            prefix_value_cache, prefix_index, prefix_lens, tail_key_cache, tail_value_cache, tail_lens, parents,
        )
    half = np.power(ROPE_BASE, -np.arange(HEAD_DIM // 2) * 2.0 / HEAD_DIM)
    freqs = jnp.asarray(np.concatenate([half, half])[None, :], jnp.float32)
    out = layer(
        (
            hidden, norm_gain[None, :], q_weight, q_bias[None, :],
            jnp.transpose(kv_weight, (1, 2, 0)).reshape(128, width), kv_bias, o_weight,
            prefix_key_cache, prefix_value_cache, tail_key_cache, tail_value_cache,
            prefix_index, prefix_lens, tail_lens, tail_lens[None, :], parents, freqs,
        ),
        1.0 / math.sqrt(HEAD_DIM), devices,
    )
    return out.reshape(STEPS, 32, out.shape[1])


def solution(mesh):
    return jax.shard_map(
        local,
        mesh=mesh,
        in_specs=(
            P(None, ("grp", "beam"), None),
            P(),
            P(None, "beam"),
            P("beam"),
            P(None, None, "beam"),
            P(None, "beam"),
            P(None, "beam"),
            P("grp", "beam", None),
            P("grp", "beam", None),
            P("grp"),
            P("grp"),
            P(("grp", "beam"), None, None),
            P(("grp", "beam"), None, None),
            P("grp"),
            P(None, "grp"),
        ),
        out_specs=P(None, "grp", "beam"),
        check_vma=False,
    )
```
